32 devices in a mesh: seq: 8 (over z, y), dp: 4 (over x, core).
Axes of the slice: x: 2, y: 2, z: 4, core: 2. Of those that a mesh axis runs over, the one named last changes fastest.
Arguments:
- blocks: bfloat16 [4, 2048, 768], P('dp', 'seq'), may hold values from -6 to 6
- lengths: int32 [4, 4], P('dp'), may hold values from 1 to 1024, 1920 in all within a row
- bucket_table: int32 [2047], replicated, may hold values from 0 to 31, as said below
- first_gain: float32 [768], P(('seq', 'dp')), may hold values from 0.5 to 1.5
- query_weight: float32 [768, 768], P(('seq', 'dp')), may hold values from -0.109375 to 0.109375
- key_weight: float32 [768, 768], P(('seq', 'dp')), may hold values from -0.109375 to 0.109375
- value_weight: float32 [768, 768], P(('seq', 'dp')), may hold values from -0.21875 to 0.21875
- output_weight: float32 [768, 768], P(('seq', 'dp')), may hold values from -0.625 to 0.625
- table_weight: float32 [32, 12], replicated, may hold values from -4 to 4
- second_gain: float32 [768], P(('seq', 'dp')), may hold values from 0.5 to 1.5
- gate_weight: float32 [768, 2048], P(('seq', 'dp')), may hold values from -0.21875 to 0.21875
- up_weight: float32 [768, 2048], P(('seq', 'dp')), may hold values from -0.21875 to 0.21875
- down_weight: float32 [2048, 768], P(('seq', 'dp')), may hold values from -0.25 to 0.25
- cotangent: bfloat16 [4, 2048, 768], P('dp', 'seq'), may hold values from -6 to 6
Outputs:
- output: bfloat16 [4, 2048, 768], P('dp', 'seq')
- grad_blocks: float32 [4, 2048, 768], P('dp', 'seq')
- grad_first_gain: float32 [768], P(('seq', 'dp'))
- grad_query_weight: float32 [768, 768], P(('seq', 'dp'))
- grad_key_weight: float32 [768, 768], P(('seq', 'dp'))
- grad_value_weight: float32 [768, 768], P(('seq', 'dp'))
- grad_output_weight: float32 [768, 768], P(('seq', 'dp'))
- grad_table_weight: float32 [32, 12], replicated
- grad_second_gain: float32 [768], P(('seq', 'dp'))
- grad_gate_weight: float32 [768, 2048], P(('seq', 'dp'))
- grad_up_weight: float32 [768, 2048], P(('seq', 'dp'))
- grad_down_weight: float32 [2048, 768], P(('seq', 'dp'))
The draws below stay inside these ranges and needn't reach their ends.
Inputs may be any that keep to these rules, and one draw needn't show every extreme that they name: Each row of lengths sums to 1920, and its largest entry is 1024. bucket_table[1023 + r] is 0 for r = 0, between 1 and 15 for r < 0 and between 17 and 31 for r > 0, never falling as |r| grows on either side; it is 31 at r = 1023.
All inputs are finite; a program needn't handle non-finite values.
Results may differ from the reference program's by a relative error of at most 0.025.
Values may be sent and summed in bfloat16 or wider, within the bound.
No kernel may reach another device: no remote copies, remote signals or barrier semaphores. Data moves between devices by JAX's collectives and lax.ppermute only.
A program may use at most 128 MiB of HBM per device.

```python
import math
import jax
import jax.numpy as jnp
import numpy as np
from jax import lax

D = 768
HEADS = 12
HEAD_DIM = 64
FF = 2048
BUCKETS = 32
PACK = 2048
SEQS = 4
MAXLEN = 1024
PADDING = 128
N_DP = 4


def draw_bucket_table(key, part):
    fixed_limits = jnp.arange(1, 8, dtype=jnp.int32)
    drawn_limits = jnp.sort(jax.random.randint(key, (8,), 8, MAXLEN // 2, dtype=jnp.int32))
    limits = jnp.concatenate([fixed_limits, drawn_limits])
    distance = jnp.arange(2 * MAXLEN - 1, dtype=jnp.int32) - (MAXLEN - 1)
    magnitude = jnp.abs(distance)
    bucket = jnp.sum((magnitude[:, None] >= limits[None, :]).astype(jnp.int32), axis=1, dtype=jnp.int32)
    return bucket + BUCKETS // 2 * (distance > 0).astype(jnp.int32)


def steps_of(own_key, extent, pieces, low, high):
    gain, own = 1.0, jax.random.fold_in(own_key, 6)
    for position, shards_of in pieces:
        draws = jnp.exp(jax.random.uniform(jax.random.fold_in(own, position), (shards_of,), jnp.float32, low / len(pieces), high / len(pieces)))
        gain = gain * jnp.repeat(draws, extent[position] // shards_of).reshape([-1 if axis == position else 1 for axis in range(len(extent))])
    return gain


def length_profile(number_of, total, limit, skew):
    portions = [(1 << 20) // math.isqrt(rank ** skew) + 1 for rank in range(2, number_of + 1)]
    rest, counts = total - limit - (number_of - 1), [1] * (number_of - 1)
    while rest > 0:
        free = [i for i in range(number_of - 1) if counts[i] < limit]
        pool, remaining = sum([portions[i] for i in free]), rest
        for i in free:
            extra = min(limit - counts[i], max(1, remaining * portions[i] // pool), rest)
            counts[i] = counts[i] + extra
            rest = rest - extra
    return np.array([limit] + counts)


def uneven_parts(key, amount, total, most, slope):
    if amount == 2:
        one = jax.random.randint(key, (), max(1, total - most), min(most, total - 1) + 1)
        return jnp.stack([one, total - one])
    tallies = jnp.asarray(length_profile(amount, total, most, slope), jnp.int32)
    twos = (amount - 1) // 2
    donor, sink = tallies[1:1 + 2 * twos:2], tallies[2:2 + 2 * twos:2]
    slack = jnp.minimum(donor - 1, most - sink)
    passed = jax.random.randint(jax.random.fold_in(key, 1), (twos,), 0, 1 << 20) % (slack + 1)
    tallies = tallies.at[1:1 + 2 * twos:2].set(donor - passed).at[2:2 + 2 * twos:2].set(sink + passed)
    return tallies[jax.random.permutation(jax.random.fold_in(key, 2), amount)]


def normal_values(rng, dims, scale, most, cuts=(), held_as=jnp.bfloat16):
    drawn = jax.random.normal(rng, dims, jnp.float32) * scale
    if len(cuts) > 0:
        drawn = steps_of(rng, dims, cuts, -0.22, 0.18) * drawn
    return jnp.clip(drawn, min=-most, max=most).astype(held_as)


def setup_inputs(seed: int = 0) -> dict:
    keys = jax.random.split(jax.random.key(seed), 15)
    return {
        "blocks": normal_values(keys[0], (N_DP, PACK, D), 1.0, 6.0, ((0, 4), (1, 8))),
        "lengths": jax.vmap(lambda own: uneven_parts(own, SEQS, PACK - PADDING, MAXLEN, 2))(jax.random.split(keys[1], N_DP)).reshape((N_DP, SEQS)).astype(jnp.int32),
        "bucket_table": draw_bucket_table(jax.random.fold_in(keys[14], 71), 0),
        "first_gain": jnp.clip(1.0 + 0.1 * jax.random.normal(keys[3], (D,), jnp.float32), 0.5, 1.5),
        "query_weight": normal_values(keys[4], (D, D), (4 * D) ** -0.5, 0.109375, ((0, 32),), jnp.float32),
        "key_weight": normal_values(keys[5], (D, D), (4 * D) ** -0.5, 0.109375, ((0, 32),), jnp.float32),
        "value_weight": normal_values(keys[6], (D, D), D ** -0.5, 0.21875, ((0, 32),), jnp.float32),
        "output_weight": normal_values(keys[7], (D, D), (D // 8) ** -0.5, 0.625, ((0, 32),), jnp.float32),
        "table_weight": normal_values(keys[8], (BUCKETS, HEADS), 1.0, 4.0, (), jnp.float32),
        "second_gain": jnp.clip(1.0 + 0.1 * jax.random.normal(keys[9], (D,), jnp.float32), 0.5, 1.5),
        "gate_weight": normal_values(keys[10], (D, FF), D ** -0.5, 0.21875, ((0, 32),), jnp.float32),
        "up_weight": normal_values(keys[11], (D, FF), D ** -0.5, 0.21875, ((0, 32),), jnp.float32),
        "down_weight": normal_values(keys[12], (FF, D), (FF // 4) ** -0.5, 0.25, ((0, 32),), jnp.float32),
        "cotangent": normal_values(keys[13], (N_DP, PACK, D), 1.0, 6.0, ((0, 4), (1, 8))),
    }


@jax.custom_vjp
def low(v):
    return lax.optimization_barrier(v.astype(jnp.bfloat16)).astype(jnp.float32)

@jax.custom_vjp
def low_back(v):
    return v

def low_keep(v):
    return (low(v), None)

def low_pass(kept, grad):
    return (grad,)

def back_keep(v):
    return (v, None)

def back_low(kept, grad):
    return (low(grad),)
low.defvjp(low_keep, low_pass)
low_back.defvjp(back_keep, back_low)
EPSILON = 1e-06
MASKED = -1e+30
HIGHEST = lax.Precision.HIGHEST

def matmul(left_side, right_side):
    return jnp.dot(left_side, right_side, precision=HIGHEST)

def rms_scale(values, scaling):
    return values * lax.rsqrt(lax.optimization_barrier(jnp.mean(values * values, axis=-1, keepdims=True)) + EPSILON) * scaling

def segment_ids(length_row):
    seq_ends = jnp.cumsum(length_row, dtype=jnp.int32)
    places = jnp.arange(PACK, dtype=jnp.int32)
    return lax.optimization_barrier(jnp.sum((places[:, None] >= seq_ends[None, :]).astype(jnp.int32), axis=1, dtype=jnp.int32))

def forward(blocks, first_gain, query_weight, key_weight, value_weight, output_weight, table_weight, second_gain, gate_weight, up_weight, down_weight, segments, bucket_table):
    gain_one = low(first_gain)
    weight_query = low(query_weight)
    weight_key = low(key_weight)
    weight_value = low(value_weight)
    weight_output = low(output_weight)
    gain_two = low(second_gain)
    weight_gate = low(gate_weight)
    weight_up = low(up_weight)
    weight_down = low(down_weight)
    query_rows = 512 if PACK % 512 == 0 else PACK

    def one_pack(pack_pair):
        pack_rows, pack_seg = pack_pair
        normed = low(rms_scale(pack_rows, gain_one))
        queries = low(low_back(matmul(normed, weight_query))).reshape(PACK, HEADS, HEAD_DIM)
        key_rows = low(low_back(matmul(normed, weight_key))).reshape(PACK, HEADS, HEAD_DIM)
        values = low(low_back(matmul(normed, weight_value))).reshape(PACK, HEADS, HEAD_DIM)

        def query_block(counter):
            first_row = counter * query_rows
            block_queries = lax.dynamic_slice_in_dim(queries, first_row, query_rows, 0)
            scores = jnp.einsum('qhd,khd->hqk', block_queries, key_rows, precision=HIGHEST)
            query_places = first_row + jnp.arange(query_rows, dtype=jnp.int32)
            key_places = jnp.arange(PACK, dtype=jnp.int32)
            distance = jnp.clip(key_places[None, :] - query_places[:, None], 1 - MAXLEN, MAXLEN - 1) + (MAXLEN - 1)
            buckets = bucket_table[distance]
            bias_values = jnp.transpose(table_weight[buckets], (2, 0, 1))
            query_seg = lax.dynamic_slice_in_dim(pack_seg, first_row, query_rows, 0)
            same_seq = query_seg[:, None] == pack_seg[None, :]
            scores = low_back(jnp.where(same_seq[None], scores + bias_values, MASKED))
            probabilities = low(jax.nn.softmax(scores, axis=-1))
            return jnp.einsum('hqk,khd->qhd', probabilities, values, precision=HIGHEST)
        attended = lax.map(jax.checkpoint(query_block), jnp.arange(PACK // query_rows, dtype=jnp.int32))
        valid_rows = (pack_seg < SEQS).astype(jnp.float32)
        attended = attended.reshape(PACK, D) * valid_rows[:, None]
        mixed_low = low(low_back(attended))
        middle = pack_rows + low_back(matmul(mixed_low, weight_output))
        normed_two = low(rms_scale(middle, gain_two))
        gate_values = low_back(matmul(normed_two, weight_gate))
        upward = low_back(matmul(normed_two, weight_up))
        hidden = low(jax.nn.gelu(gate_values, approximate=True) * upward)
        return middle + low_back(matmul(hidden, weight_down))
    return lax.map(one_pack, (blocks, segments))

def reference(blocks, lengths, bucket_table, first_gain, query_weight, key_weight, value_weight, output_weight, table_weight, second_gain, gate_weight, up_weight, down_weight, cotangent):
    segments = jax.vmap(segment_ids)(lengths)
    primals = (blocks.astype(jnp.float32), first_gain, query_weight, key_weight, value_weight, output_weight, table_weight, second_gain, gate_weight, up_weight, down_weight)

    def layer_call(*weights):
        return forward(*weights, segments, bucket_table)
    output, pullback = jax.vjp(layer_call, *primals)
    gradients = pullback(cotangent.astype(jnp.float32))
    return (output.astype(jnp.bfloat16), gradients[0], gradients[1], gradients[2], gradients[3], gradients[4], gradients[5], gradients[6], gradients[7], gradients[8], gradients[9], gradients[10])
```

```python
import functools

import jax
import jax.numpy as jnp
from jax import lax
from jax.experimental import pallas as pl
from jax.experimental.pallas import tpu as pltpu
from jax.sharding import PartitionSpec as P

EPSILON = 1e-06
BIG = -1e30
HIGHEST = lax.Precision.HIGHEST
BOTH = ("seq", "dp")
TILE = 128
STEP = 4
SPAN = STEP * TILE
F32 = jnp.float32
BF16 = jnp.bfloat16
LOWEST = -3.0e38


def bias_of(tiles_ref, pair, tile):
    halves_of = [tiles_ref[2 * pair + side, pl.ds(tile, STEP)].reshape(SPAN, TILE) for side in range(2)]
    return jnp.concatenate(halves_of, axis=1)


def dot(a, b):
    return jnp.dot(a, b, preferred_element_type=F32)


def tiles_kernel(line_ref, tiles_ref):
    tile_count = tiles_ref.shape[1]
    for index in range(tile_count):
        window = line_ref[0, :, pl.ds((tile_count - 1 - index) * TILE, 2 * TILE)]
        spread = jnp.broadcast_to(window, (TILE, 2 * TILE))
        rolled = pltpu.roll(spread, 0, 1, stride=1, stride_axis=0)
        tiles_ref[0, index] = rolled[:, TILE:]


def bias_tiles(lines, tile_count):
    heads, width = lines.shape
    return pl.pallas_call(
        tiles_kernel,
        out_shape=jax.ShapeDtypeStruct((heads, tile_count, TILE, TILE), F32),
        grid=(heads,),
        in_specs=[pl.BlockSpec((1, 1, width), lambda h: (h, 0, 0))],
        out_specs=pl.BlockSpec((1, tile_count, TILE, TILE), lambda h: (h, 0, 0, 0)),
    )(lines.reshape(heads, 1, width))


def halves(pair, head_dim):
    top = lax.broadcasted_iota(jnp.int32, pair.shape, 0) < head_dim
    zero = jnp.zeros_like(pair)
    return jnp.concatenate([jnp.where(top, pair, zero), jnp.where(top, zero, pair)], axis=1)


def halves_rows(pair, head_dim):
    left = lax.broadcasted_iota(jnp.int32, pair.shape, 1) < head_dim
    zero = jnp.zeros_like(pair)
    return jnp.concatenate([jnp.where(left, pair, zero), jnp.where(left, zero, pair)], axis=0)


def merge_halves(both, head_dim):
    top = lax.broadcasted_iota(jnp.int32, (both.shape[0], TILE), 0) < head_dim
    return jnp.where(top, both[:, :TILE], both[:, TILE:])


def fold(values, op):
    return op(values.reshape(values.shape[0] // 8, 8, values.shape[1]), axis=0)


def cols(pair):
    return slice(pair * TILE, (pair + 1) * TILE)


def wide(pair):
    return slice(pair * 2 * TILE, (pair + 1) * 2 * TILE)


def query_side(query_ref, query_feat_ref, block, pair, head_dim):
    rows = slice(block * TILE, (block + 1) * TILE)
    turned = query_ref[cols(pair), rows]
    feat = query_feat_ref[:, rows]
    return jnp.concatenate([halves(turned, head_dim), jnp.concatenate([feat, feat], axis=1)], axis=0)


def forward_kernel(
    first_ref, last_ref, query_ref, key_ref, value_turned_ref, key_feat_ref, query_feat_ref, tiles_ref,
    out_ref, log_ref, score_ref, total_ref, *, pairs, blocks, head_dim,
):
    for block in range(blocks):
        rows = slice(block * TILE, (block + 1) * TILE)
        first, last = first_ref[block], last_ref[block]
        query_sides = [query_side(query_ref, query_feat_ref, block, pair, head_dim) for pair in range(pairs)]

        def score_step(index, highest):
            start = pl.multiple_of((first + index * STEP) * TILE, TILE)
            feat = key_feat_ref[pl.ds(start, SPAN), :]
            tile = first + index * STEP - block + (blocks - 1)
            result = []
            for pair in range(pairs):
                left = jnp.concatenate([key_ref[pl.ds(start, SPAN), cols(pair)], feat], axis=1)
                bias = bias_of(tiles_ref, pair, tile)
                scores = dot(left, query_sides[pair]) + bias
                score_ref[pl.ds(start, SPAN), wide(pair)] = scores
                result.append(jnp.maximum(highest[pair], fold(scores, jnp.max)))
            return tuple(result)

        start_max = tuple(jnp.full((8, 2 * TILE), LOWEST, F32) for _ in range(pairs))
        highest = lax.fori_loop(0, last, score_step, start_max)
        peak = [jnp.max(value, axis=0, keepdims=True) for value in highest]
        total_ref[...] = jnp.zeros_like(total_ref)

        def value_step(index, sums):
            start = pl.multiple_of((first + index * STEP) * TILE, TILE)
            result = []
            for pair in range(pairs):
                weights = jnp.exp(score_ref[pl.ds(start, SPAN), wide(pair)] - peak[pair])
                result.append(sums[pair] + fold(weights, jnp.sum))
                total_ref[:, wide(pair)] += dot(
                    value_turned_ref[cols(pair), pl.ds(start, SPAN)], weights.astype(BF16)
                )
            return tuple(result)

        start_sum = tuple(jnp.zeros((8, 2 * TILE), F32) for _ in range(pairs))
        sums = lax.fori_loop(0, last, value_step, start_sum)
        for pair in range(pairs):
            denominator = jnp.sum(sums[pair], axis=0, keepdims=True)
            out_ref[cols(pair), rows] = merge_halves(total_ref[:, wide(pair)] / denominator, head_dim)
            log_ref[0, block * pairs + pair : block * pairs + pair + 1, :] = peak[pair] + jnp.log(denominator)


def attend(first, last, queries, keys, values_turned, key_feat, query_feat, tiles, head_dim, pairs):
    width, row_count = queries.shape
    window = keys.shape[0]
    blocks = row_count // TILE
    groups = width // (pairs * TILE)
    tile_count = tiles.shape[1]
    kernel = functools.partial(
        forward_kernel, pairs=pairs, blocks=blocks, head_dim=head_dim
    )
    work = row_count * 1280 * width
    return pl.pallas_call(
        kernel,
        out_shape=(
            jax.ShapeDtypeStruct((width, row_count), F32),
            jax.ShapeDtypeStruct((groups, blocks * pairs, 2 * TILE), F32),
        ),
        grid_spec=pltpu.PrefetchScalarGridSpec(
            num_scalar_prefetch=2,
            grid=(groups,),
            in_specs=[
                pl.BlockSpec((pairs * TILE, row_count), lambda g, a, b: (g, 0)),
                pl.BlockSpec((window, pairs * TILE), lambda g, a, b: (0, g)),
                pl.BlockSpec((pairs * TILE, window), lambda g, a, b: (g, 0)),
                pl.BlockSpec((window, TILE), lambda g, a, b: (0, 0)),
                pl.BlockSpec((TILE, row_count), lambda g, a, b: (0, 0)),
                pl.BlockSpec((2 * pairs, tile_count, TILE, TILE), lambda g, a, b: (g, 0, 0, 0)),
            ],
            out_specs=[
                pl.BlockSpec((pairs * TILE, row_count), lambda g, a, b: (g, 0)),
                pl.BlockSpec((1, blocks * pairs, 2 * TILE), lambda g, a, b: (g, 0, 0)),
            ],
            scratch_shapes=[
                pltpu.VMEM((window, pairs * 2 * TILE), F32),
                pltpu.VMEM((TILE, pairs * 2 * TILE), F32),
            ],
        ),
        compiler_params=pltpu.CompilerParams(vmem_limit_bytes=50 << 20),
        cost_estimate=pl.CostEstimate(flops=16 * work, bytes_accessed=24 << 20, transcendentals=row_count * 1280 * 12),
    )(first, last, queries, keys, values_turned, key_feat, query_feat, tiles)


def backward_kernel(
    first_ref, last_ref, query_ref, query_turned_ref, key_ref, key_turned_ref, value_ref, grad_ref, grad_turned_ref, out_ref, log_ref,
    key_feat_ref, query_feat_ref, tiles_ref,
    grad_query_ref, grad_key_ref, grad_value_ref, tile_total,
    key_total, value_total, query_total, *, pairs, blocks, head_dim,
):
    key_total[...] = jnp.zeros_like(key_total)
    value_total[...] = jnp.zeros_like(value_total)
    tile_total[...] = jnp.zeros_like(tile_total)
    for block in range(blocks):
        rows = slice(block * TILE, (block + 1) * TILE)
        first, last = first_ref[block], last_ref[block]
        query_sides, grad_sides, query_stacks, grad_stacks, logs, deltas = [], [], [], [], [], []
        for pair in range(pairs):
            query_sides.append(query_side(query_turned_ref, query_feat_ref, block, pair, head_dim))
            grad_pair = grad_ref[rows, cols(pair)]
            grad_turned = grad_turned_ref[cols(pair), rows]
            grad_sides.append(halves(grad_turned, head_dim))
            query_stacks.append(halves_rows(query_ref[rows, cols(pair)], head_dim))
            grad_stacks.append(halves_rows(grad_pair, head_dim))
            logs.append(log_ref[0, block * pairs + pair : block * pairs + pair + 1, :])
            both = halves(grad_turned.astype(F32) * out_ref[cols(pair), rows], head_dim)
            deltas.append(jnp.sum(both, axis=0, keepdims=True))
        query_total[...] = jnp.zeros_like(query_total)

        def step(index, carry):
            start = pl.multiple_of((first + index * STEP) * TILE, TILE)
            span = pl.ds(start, SPAN)
            feat = key_feat_ref[span, :]
            tile = first + index * STEP - block + (blocks - 1)
            for pair in range(pairs):
                left = jnp.concatenate([key_ref[span, cols(pair)], feat], axis=1)
                bias = bias_of(tiles_ref, pair, tile)
                weights = jnp.exp(dot(left, query_sides[pair]) + bias - logs[pair])
                grad_weights = dot(value_ref[span, cols(pair)], grad_sides[pair])
                grad_scores = weights * (grad_weights - deltas[pair])
                tile_total[2 * pair, pl.ds(tile, STEP)] += grad_scores[:, :TILE].reshape(STEP, TILE, TILE)
                tile_total[2 * pair + 1, pl.ds(tile, STEP)] += grad_scores[:, TILE:].reshape(STEP, TILE, TILE)
                scores_low = grad_scores.astype(BF16)
                value_total[span, cols(pair)] += dot(weights.astype(BF16), grad_stacks[pair])
                key_total[span, cols(pair)] += dot(scores_low, query_stacks[pair])
                query_total[:, wide(pair)] += dot(key_turned_ref[cols(pair), span], scores_low)
            return carry

        lax.fori_loop(0, last, step, 0)
        for pair in range(pairs):
            grad_query_ref[cols(pair), rows] = merge_halves(query_total[:, wide(pair)], head_dim).astype(BF16)
    grad_key_ref[...] = key_total[...].astype(BF16)
    grad_value_ref[...] = value_total[...].astype(BF16)


def attend_back(first, last, queries, queries_turned, keys, keys_turned, values, grads, grads_turned, outs, logs, key_feat, query_feat, tiles, head_dim, pairs):
    row_count, width = queries.shape
    window = keys.shape[0]
    blocks = row_count // TILE
    groups = width // (pairs * TILE)
    heads, tile_count = tiles.shape[:2]
    kernel = functools.partial(backward_kernel, pairs=pairs, blocks=blocks, head_dim=head_dim)
    rows_spec = pl.BlockSpec((row_count, pairs * TILE), lambda g, a, b: (0, g))
    turned_spec = pl.BlockSpec((pairs * TILE, row_count), lambda g, a, b: (g, 0))
    window_spec = pl.BlockSpec((window, pairs * TILE), lambda g, a, b: (0, g))
    work = row_count * 1280 * width
    return pl.pallas_call(
        kernel,
        out_shape=(
            jax.ShapeDtypeStruct((width, row_count), BF16),
            jax.ShapeDtypeStruct((window, width), BF16),
            jax.ShapeDtypeStruct((window, width), BF16),
            jax.ShapeDtypeStruct((heads, tile_count, TILE, TILE), F32),
        ),
        grid_spec=pltpu.PrefetchScalarGridSpec(
            num_scalar_prefetch=2,
            grid=(groups,),
            in_specs=[
                rows_spec,
                turned_spec,
                window_spec,
                pl.BlockSpec((pairs * TILE, window), lambda g, a, b: (g, 0)),
                window_spec,
                rows_spec,
                turned_spec,
                turned_spec,
                pl.BlockSpec((1, blocks * pairs, 2 * TILE), lambda g, a, b: (g, 0, 0)),
                pl.BlockSpec((window, TILE), lambda g, a, b: (0, 0)),
                pl.BlockSpec((TILE, row_count), lambda g, a, b: (0, 0)),
                pl.BlockSpec((2 * pairs, tile_count, TILE, TILE), lambda g, a, b: (g, 0, 0, 0)),
            ],
            out_specs=[
                turned_spec,
                window_spec,
                window_spec,
                pl.BlockSpec((2 * pairs, tile_count, TILE, TILE), lambda g, a, b: (g, 0, 0, 0)),
            ],
            scratch_shapes=[
                pltpu.VMEM((window, pairs * TILE), F32),
                pltpu.VMEM((window, pairs * TILE), F32),
                pltpu.VMEM((TILE, pairs * 2 * TILE), F32),
            ],
        ),
        input_output_aliases={13: 3},
        compiler_params=pltpu.CompilerParams(vmem_limit_bytes=56 << 20),
        cost_estimate=pl.CostEstimate(flops=40 * work, bytes_accessed=32 << 20, transcendentals=row_count * 1280 * 12),
    )(first, last, queries, queries_turned, keys, keys_turned, values, grads, grads_turned, outs, logs, key_feat, query_feat, tiles)


def diagonal_kernel(tiles_ref, line_ref):
    for index in range(tiles_ref.shape[1]):
        tile = tiles_ref[0, index]
        padded = jnp.concatenate([tile, jnp.zeros_like(tile)], axis=1)
        size = TILE // 2
        while size >= 8:
            padded = padded[:size] + pltpu.roll(padded[size:], 2 * TILE - size, 1)
            size //= 2
        line_ref[0, index] = padded


def diagonal_sums(tiles):
    heads, tile_count = tiles.shape[:2]
    return pl.pallas_call(
        diagonal_kernel,
        out_shape=jax.ShapeDtypeStruct((heads, tile_count, 8, 2 * TILE), F32),
        grid=(heads,),
        in_specs=[pl.BlockSpec((1, tile_count, TILE, TILE), lambda h: (h, 0, 0, 0))],
        out_specs=pl.BlockSpec((1, tile_count, 8, 2 * TILE), lambda h: (h, 0, 0, 0)),
    )(tiles)


def shifted(value, axis, steps):
    count = lax.axis_size(axis)
    pairs = [(source, source + steps) for source in range(count) if 0 <= source + steps < count]
    return lax.ppermute(value, axis, pairs)


def swapped(value, axis, bit):
    count = lax.axis_size(axis)
    return lax.ppermute(value, axis, [(source, source ^ bit) for source in range(count)])


def sum_everywhere(value):
    for axis in BOTH:
        count = lax.axis_size(axis)
        if count & (count - 1):
            value = lax.psum(value, axis)
            continue
        bit = 1
        while bit < count:
            value = value + swapped(value, axis, bit)
            bit *= 2
    return value


def rows_of(value, rows):
    height, width = value.shape
    columns = height * width // rows
    if height % 8 or rows % 8 or width % TILE or columns % TILE:
        return value.reshape(rows, columns)
    tiles = value.reshape(height // 8, 8, width // TILE, TILE).transpose(0, 2, 1, 3)
    tiles = tiles.reshape(rows // 8, columns // TILE, 8, TILE).transpose(0, 2, 1, 3)
    return tiles.reshape(rows, columns)


def parts_of(value, parts, to_rows):
    rows = value.shape[0] // parts
    columns = rows * value.shape[1] // to_rows
    if rows % 8 or to_rows % 8 or value.shape[1] % TILE or columns % TILE:
        return value.reshape(parts * to_rows, columns)
    tiles = value.reshape(parts, rows // 8, 8, value.shape[1] // TILE, TILE).transpose(0, 1, 3, 2, 4)
    tiles = tiles.reshape(parts, to_rows // 8, columns // TILE, 8, TILE).transpose(0, 1, 3, 2, 4)
    return tiles.reshape(parts * to_rows, columns)


def contract(left_side, right_side, left_dim, right_dim):
    return lax.dot_general(
        left_side, right_side, (((left_dim,), (right_dim,)), ((), ())), preferred_element_type=F32
    )


def gelu_pair(v):
    scale = 0.7978845608028654
    bent = jnp.tanh(scale * (v + 0.044715 * v * v * v))
    value = 0.5 * v * (1.0 + bent)
    slope = 0.5 * (1.0 + bent) + 0.5 * v * (1.0 - bent * bent) * scale * (1.0 + 3.0 * 0.044715 * v * v)
    return value, slope


def body(
    blocks,
    lengths,
    bucket_table,
    first_gain,
    query_weight,
    key_weight,
    value_weight,
    output_weight,
    table_weight,
    second_gain,
    gate_weight,
    up_weight,
    down_weight,
    cotangent,
):
    seq_count = lax.axis_size("seq")
    device_count = seq_count * lax.axis_size("dp")
    seq_rank = lax.axis_index("seq")
    row_count, width = blocks.shape[1:]
    pack_rows = row_count * seq_count
    bucket_count, heads = table_weight.shape
    head_dim = width // heads
    seq_total = lengths.shape[1]
    max_length = (bucket_table.shape[0] + 1) // 2
    shard_rows = query_weight.shape[0]
    hidden_width = gate_weight.shape[1]
    reach = min((max_length - 1 + row_count - 1) // row_count, seq_count - 1)
    query_blocks = row_count // TILE
    window = (2 * reach + 1) * row_count
    window_blocks = window // TILE
    tile_count = window_blocks + query_blocks - 1
    center = reach * query_blocks + query_blocks - 1
    pairs = 2 if window <= 2304 else 1

    own = blocks[0]
    near = [shifted(own, "seq", -step) for step in range(1, reach + 1)]
    far = [shifted(own, "seq", step) for step in range(1, reach + 1)]
    window_blocks_low = jnp.concatenate(far[::-1] + [own] + near, axis=0)

    gains = jnp.stack([first_gain.astype(BF16), second_gain.astype(BF16)], axis=1)
    gains = jnp.pad(gains, ((0, 0), (0, TILE - 2)))
    shard = jnp.concatenate(
        [
            query_weight.astype(BF16),
            key_weight.astype(BF16),
            value_weight.astype(BF16),
            gains,
            output_weight.astype(BF16),
            gate_weight.astype(BF16),
            up_weight.astype(BF16),
            rows_of(down_weight.astype(BF16), shard_rows),
        ],
        axis=1,
    )
    gathered = lax.all_gather(shard, BOTH, axis=0, tiled=True)
    down_columns = down_weight.shape[0] * width // shard_rows
    places = [width, width, width, TILE, width, 2 * hidden_width, down_columns]
    cuts = []
    start = 0
    for place in places:
        cuts.append(gathered[:, start : start + place])
        start += place
    weight_query, weight_key, weight_value, gain_columns, weight_output, weight_pair, weight_down = cuts
    weight_down = parts_of(weight_down, device_count, down_weight.shape[0])
    gain_one = gain_columns[:, 0].astype(F32)[None, :]
    gain_two = gain_columns[:, 1].astype(F32)[None, :]

    seq_ends = jnp.cumsum(lengths[0], dtype=jnp.int32)
    query_first = seq_rank * row_count
    window_first = query_first - reach * row_count

    def segments(at):
        return jnp.sum((at[:, None] >= seq_ends[None, :]).astype(jnp.int32), axis=1, dtype=jnp.int32)

    query_places = query_first + jnp.arange(row_count, dtype=jnp.int32)
    key_places = window_first + jnp.arange(window, dtype=jnp.int32)
    query_seg = segments(query_places)
    key_seg = jnp.where((key_places >= 0) & (key_places < pack_rows), segments(key_places), -1)
    lanes = jnp.arange(TILE, dtype=jnp.int32)
    key_feat = jnp.where(
        (key_seg[:, None] != lanes[None, :]) & (lanes[None, :] <= seq_total), BIG, 0.0
    ).astype(BF16)
    query_feat = (lanes[:, None] == query_seg[None, :]).astype(BF16)
    valid_rows = (query_seg < seq_total).astype(F32)
    seq_starts = jnp.concatenate([jnp.zeros((1,), jnp.int32), seq_ends])
    seq_stops = jnp.concatenate([seq_ends, jnp.full((1,), pack_rows, jnp.int32)])
    seq_ids = jnp.arange(seq_total + 1, dtype=jnp.int32)
    low_seg = query_seg[::TILE]
    high_seg = query_seg[TILE - 1 :: TILE]
    low = jnp.sum(jnp.where(low_seg[:, None] == seq_ids[None, :], seq_starts[None, :], 0), axis=1)
    high = jnp.sum(jnp.where(high_seg[:, None] == seq_ids[None, :], seq_stops[None, :], 0), axis=1)
    first = (low - window_first) // TILE
    last = (high - window_first + TILE - 1) // TILE
    steps = (last - first + STEP - 1) // STEP
    first = jnp.minimum(first, window_blocks - steps * STEP).astype(jnp.int32)
    steps = steps.astype(jnp.int32)

    line_width = (tile_count + 1) * TILE
    ahead = (tile_count - center) * TILE - (max_length - 1)
    behind = line_width - ahead - bucket_table.shape[0]
    bucket_line = jnp.pad(bucket_table[::-1], (max(ahead, 0), max(behind, 0)), mode="edge")
    bucket_line = bucket_line[max(-ahead, 0) : max(-ahead, 0) + line_width]
    bucket_ids = jnp.arange(bucket_count, dtype=jnp.int32)
    line_hot = (bucket_line[None, :] == bucket_ids[:, None]).astype(F32)
    lines = lax.dot_general(table_weight, line_hot, (((0,), (0,)), ((), ())), precision=HIGHEST)
    tiles = bias_tiles(lines, tile_count)

    window_rows = window_blocks_low.astype(F32)
    window_scale = lax.rsqrt(jnp.mean(window_rows * window_rows, axis=1, keepdims=True) + EPSILON)
    window_normed = (window_rows * window_scale * gain_one).astype(BF16)
    own_slice = slice(reach * row_count, (reach + 1) * row_count)
    tokens = own.astype(F32)
    scale_one = lax.rsqrt(jnp.mean(tokens * tokens, axis=1, keepdims=True) + EPSILON)
    normed_own = window_normed[own_slice]
    keys = contract(window_normed, weight_key, 1, 0).astype(BF16)
    values_turned = contract(weight_value, window_normed, 0, 1).astype(BF16)
    queries_turned = contract(weight_query, normed_own, 0, 1).astype(BF16)
    outs, logs = attend(
        first, steps, queries_turned, keys, values_turned, key_feat, query_feat, tiles, head_dim, pairs
    )
    attended = (outs * valid_rows[None, :]).astype(BF16)
    middle = tokens + contract(attended, weight_output, 0, 0)

    scale_two = lax.rsqrt(jnp.mean(middle * middle, axis=1, keepdims=True) + EPSILON)
    second = middle * scale_two
    second_low = (second * gain_two).astype(BF16)
    both_ways = contract(second_low, weight_pair, 1, 0)
    gate_values, upward = both_ways[:, :hidden_width], both_ways[:, hidden_width:]
    active, slope = gelu_pair(gate_values)
    hidden = (active * upward).astype(BF16)
    output = middle + contract(hidden, weight_down, 1, 0)
    grad_out = cotangent[0]
    grad_hidden = contract(grad_out, weight_down, 1, 1)
    grad_pair = jnp.concatenate(
        [(grad_hidden * upward * slope).astype(BF16), (grad_hidden * active).astype(BF16)], axis=1
    )
    grad_second = contract(grad_pair, weight_pair, 1, 1)
    grad_gain_two = jnp.sum(grad_second * second, axis=0)
    scaled = grad_second * gain_two
    grad_middle = grad_out.astype(F32) + scale_two * (
        scaled - second * jnp.mean(scaled * second, axis=1, keepdims=True)
    )
    grad_branch = grad_middle.astype(BF16)
    grad_mixed = (contract(grad_branch, weight_output, 1, 1).astype(BF16).astype(F32) * valid_rows[:, None]).astype(BF16)
    grad_mixed_turned = (
        contract(weight_output, grad_branch, 1, 1).astype(BF16).astype(F32) * valid_rows[None, :]
    ).astype(BF16)
    grad_down = contract(hidden, grad_out, 0, 0).astype(BF16)
    grad_pair_weight = contract(second_low, grad_pair, 0, 0).astype(BF16)
    grad_output_weight = contract(attended, grad_branch, 1, 0).astype(BF16)

    queries = contract(normed_own, weight_query, 1, 0).astype(BF16)
    keys_turned = contract(weight_key, window_normed, 0, 1).astype(BF16)
    values = contract(window_normed, weight_value, 1, 0).astype(BF16)
    grad_queries, grad_keys, grad_values, tile_sums = attend_back(
        first, steps, queries, queries_turned, keys, keys_turned, values, grad_mixed, grad_mixed_turned,
        outs, logs, key_feat, query_feat, tiles, head_dim, pairs,
    )
    partial = contract(grad_keys, weight_key, 1, 1) + contract(grad_values, weight_value, 1, 1)
    partial_low = partial.astype(BF16)
    grad_normed = partial[own_slice] + contract(grad_queries, weight_query, 0, 1)
    for step in range(1, reach + 1):
        ahead_part = partial_low[(reach + step) * row_count : (reach + step + 1) * row_count]
        behind_part = partial_low[(reach - step) * row_count : (reach - step + 1) * row_count]
        grad_normed = grad_normed + shifted(ahead_part, "seq", step).astype(F32)
        grad_normed = grad_normed + shifted(behind_part, "seq", -step).astype(F32)
    grad_query_weight = contract(normed_own, grad_queries, 0, 1).astype(BF16)
    grad_key_weight = contract(window_normed, grad_keys, 0, 0).astype(BF16)
    grad_value_weight = contract(window_normed, grad_values, 0, 0).astype(BF16)
    normed_rows = tokens * scale_one
    grad_gain_one = jnp.sum(grad_normed * normed_rows, axis=0)
    scaled_one = grad_normed * gain_one
    grad_blocks = grad_middle + scale_one * (
        scaled_one - normed_rows * jnp.mean(scaled_one * normed_rows, axis=1, keepdims=True)
    )

    sums = diagonal_sums(tile_sums)
    diagonals = sum(jnp.roll(sums[:, :, row], -row, axis=2) for row in range(8))
    flipped = bucket_line.reshape(tile_count + 1, TILE)[::-1]
    bucket_at = jnp.concatenate([flipped[:-1], flipped[1:]], axis=1).reshape(-1)
    bucket_hot = (bucket_at[:, None] == bucket_ids[None, :]).astype(F32)
    grad_table = lax.dot_general(
        bucket_hot, diagonals.reshape(heads, -1), (((0,), (1,)), ((), ())), precision=HIGHEST
    )
    grad_table = sum_everywhere(grad_table)

    grad_gains = jnp.stack([grad_gain_one, grad_gain_two], axis=1).astype(BF16)
    grad_gains = jnp.pad(grad_gains, ((0, 0), (0, TILE - 2)))
    grads = jnp.concatenate(
        [
            grad_query_weight,
            grad_key_weight,
            grad_value_weight,
            grad_gains,
            grad_output_weight,
            grad_pair_weight,
            parts_of(grad_down, device_count, shard_rows),
        ],
        axis=1,
    )
    summed = lax.psum_scatter(grads, BOTH, scatter_dimension=0, tiled=True).astype(F32)
    pieces = []
    start = 0
    for place in [width, width, width, TILE, width, hidden_width, hidden_width, down_columns]:
        pieces.append(summed[:, start : start + place])
        start += place
    return (
        output.astype(BF16)[None],
        grad_blocks[None],
        pieces[3][:, 0],
        pieces[0],
        pieces[1],
        pieces[2],
        pieces[4],
        grad_table,
        pieces[3][:, 1],
        pieces[5],
        pieces[6],
        rows_of(pieces[7], down_weight.shape[0]),
    )


def solution(mesh):
    return jax.shard_map(
        body,
        mesh=mesh,
        in_specs=(
            P("dp", "seq", None),
            P("dp", None),
            P(),
            P(("seq", "dp")),
            P(("seq", "dp"), None),
            P(("seq", "dp"), None),
            P(("seq", "dp"), None),
            P(("seq", "dp"), None),
            P(),
            P(("seq", "dp")),
            P(("seq", "dp"), None),
            P(("seq", "dp"), None),
            P(("seq", "dp"), None),
            P("dp", "seq", None),
        ),
        out_specs=(
            P("dp", "seq", None),
            P("dp", "seq", None),
            P(("seq", "dp")),
            P(("seq", "dp"), None),
            P(("seq", "dp"), None),
            P(("seq", "dp"), None),
            P(("seq", "dp"), None),
            P(),
            P(("seq", "dp")),
            P(("seq", "dp"), None),
            P(("seq", "dp"), None),
            P(("seq", "dp"), None),
        ),
        check_vma=False,
    )
```

```python
import functools

import jax
import jax.numpy as jnp
from jax import lax
from jax.experimental import pallas as pl
from jax.experimental.pallas import tpu as pltpu
from jax.sharding import PartitionSpec as P

EPSILON = 1e-06
BIG = -1e30
HIGHEST = lax.Precision.HIGHEST
BOTH = ("seq", "dp")
SMALL = pl.CostEstimate(flops=1, bytes_accessed=1, transcendentals=0)
TILE = 128
STEP = 4
SPAN = STEP * TILE
F32 = jnp.float32
BF16 = jnp.bfloat16
LOWEST = -3.0e38


def bias_of(tiles_ref, pair, tile):
    halves_of = [tiles_ref[2 * pair + side, pl.ds(tile, STEP)].reshape(SPAN, TILE) for side in range(2)]
    return jnp.concatenate(halves_of, axis=1)


def dot(a, b):
    return jnp.dot(a, b, preferred_element_type=F32)


def tiles_kernel(line_ref, tiles_ref):
    tile_count = tiles_ref.shape[1]
    for index in range(tile_count):
        window = line_ref[0, :, pl.ds((tile_count - 1 - index) * TILE, 2 * TILE)]
        spread = jnp.broadcast_to(window, (TILE, 2 * TILE))
        rolled = pltpu.roll(spread, 0, 1, stride=1, stride_axis=0)
        tiles_ref[0, index] = rolled[:, TILE:]


def bias_tiles(lines, tile_count):
    heads, width = lines.shape
    return pl.pallas_call(
        tiles_kernel,
        out_shape=jax.ShapeDtypeStruct((heads, tile_count, TILE, TILE), F32),
        grid=(heads,),
        in_specs=[pl.BlockSpec((1, 1, width), lambda h: (h, 0, 0))],
        out_specs=pl.BlockSpec((1, tile_count, TILE, TILE), lambda h: (h, 0, 0, 0)),
        cost_estimate=SMALL,
    )(lines.reshape(heads, 1, width))


def halves(pair, head_dim):
    top = lax.broadcasted_iota(jnp.int32, pair.shape, 0) < head_dim
    zero = jnp.zeros_like(pair)
    return jnp.concatenate([jnp.where(top, pair, zero), jnp.where(top, zero, pair)], axis=1)


def halves_rows(pair, head_dim):
    left = lax.broadcasted_iota(jnp.int32, pair.shape, 1) < head_dim
    zero = jnp.zeros_like(pair)
    return jnp.concatenate([jnp.where(left, pair, zero), jnp.where(left, zero, pair)], axis=0)


def merge_halves(both, head_dim):
    top = lax.broadcasted_iota(jnp.int32, (both.shape[0], TILE), 0) < head_dim
    return jnp.where(top, both[:, :TILE], both[:, TILE:])


def fold(values, op):
    return op(values.reshape(values.shape[0] // 8, 8, values.shape[1]), axis=0)


def cols(pair):
    return slice(pair * TILE, (pair + 1) * TILE)


def wide(pair):
    return slice(pair * 2 * TILE, (pair + 1) * 2 * TILE)


def query_side(query_ref, query_feat_ref, block, pair, head_dim):
    rows = slice(block * TILE, (block + 1) * TILE)
    turned = query_ref[cols(pair), rows]
    feat = query_feat_ref[:, rows]
    return jnp.concatenate([halves(turned, head_dim), jnp.concatenate([feat, feat], axis=1)], axis=0)


def forward_kernel(
    first_ref, last_ref, query_ref, key_ref, value_turned_ref, key_feat_ref, query_feat_ref, tiles_ref,
    out_ref, log_ref, score_ref, total_ref, *, pairs, blocks, head_dim,
):
    for block in range(blocks):
        rows = slice(block * TILE, (block + 1) * TILE)
        first, last = first_ref[block], last_ref[block]
        query_sides = [query_side(query_ref, query_feat_ref, block, pair, head_dim) for pair in range(pairs)]

        def score_step(index, highest):
            start = pl.multiple_of((first + index * STEP) * TILE, TILE)
            feat = key_feat_ref[pl.ds(start, SPAN), :]
            tile = first + index * STEP - block + (blocks - 1)
            result = []
            for pair in range(pairs):
                left = jnp.concatenate([key_ref[pl.ds(start, SPAN), cols(pair)], feat], axis=1)
                bias = bias_of(tiles_ref, pair, tile)
                scores = dot(left, query_sides[pair]) + bias
                score_ref[pl.ds(start, SPAN), wide(pair)] = scores
                result.append(jnp.maximum(highest[pair], fold(scores, jnp.max)))
            return tuple(result)

        start_max = tuple(jnp.full((8, 2 * TILE), LOWEST, F32) for _ in range(pairs))
        highest = lax.fori_loop(0, last, score_step, start_max)
        peak = [jnp.max(value, axis=0, keepdims=True) for value in highest]
        total_ref[...] = jnp.zeros_like(total_ref)

        def value_step(index, sums):
            start = pl.multiple_of((first + index * STEP) * TILE, TILE)
            result = []
            for pair in range(pairs):
                weights = jnp.exp(score_ref[pl.ds(start, SPAN), wide(pair)] - peak[pair])
                result.append(sums[pair] + fold(weights, jnp.sum))
                total_ref[:, wide(pair)] += dot(
                    value_turned_ref[cols(pair), pl.ds(start, SPAN)], weights.astype(BF16)
                )
            return tuple(result)

        start_sum = tuple(jnp.zeros((8, 2 * TILE), F32) for _ in range(pairs))
        sums = lax.fori_loop(0, last, value_step, start_sum)
        for pair in range(pairs):
            denominator = jnp.sum(sums[pair], axis=0, keepdims=True)
            out_ref[cols(pair), rows] = merge_halves(total_ref[:, wide(pair)] / denominator, head_dim)
            log_ref[0, block * pairs + pair : block * pairs + pair + 1, :] = peak[pair] + jnp.log(denominator)


def attend(first, last, queries, keys, values_turned, key_feat, query_feat, tiles, head_dim, pairs):
    width, row_count = queries.shape
    window = keys.shape[0]
    blocks = row_count // TILE
    groups = width // (pairs * TILE)
    tile_count = tiles.shape[1]
    kernel = functools.partial(
        forward_kernel, pairs=pairs, blocks=blocks, head_dim=head_dim
    )
    work = row_count * 1280 * width
    return pl.pallas_call(
        kernel,
        out_shape=(
            jax.ShapeDtypeStruct((width, row_count), F32),
            jax.ShapeDtypeStruct((groups, blocks * pairs, 2 * TILE), F32),
        ),
        grid_spec=pltpu.PrefetchScalarGridSpec(
            num_scalar_prefetch=2,
            grid=(groups,),
            in_specs=[
                pl.BlockSpec((pairs * TILE, row_count), lambda g, a, b: (g, 0)),
                pl.BlockSpec((window, pairs * TILE), lambda g, a, b: (0, g)),
                pl.BlockSpec((pairs * TILE, window), lambda g, a, b: (g, 0)),
                pl.BlockSpec((window, TILE), lambda g, a, b: (0, 0)),
                pl.BlockSpec((TILE, row_count), lambda g, a, b: (0, 0)),
                pl.BlockSpec((2 * pairs, tile_count, TILE, TILE), lambda g, a, b: (g, 0, 0, 0)),
            ],
            out_specs=[
                pl.BlockSpec((pairs * TILE, row_count), lambda g, a, b: (g, 0)),
                pl.BlockSpec((1, blocks * pairs, 2 * TILE), lambda g, a, b: (g, 0, 0)),
            ],
            scratch_shapes=[
                pltpu.VMEM((window, pairs * 2 * TILE), F32),
                pltpu.VMEM((TILE, pairs * 2 * TILE), F32),
            ],
        ),
        compiler_params=pltpu.CompilerParams(vmem_limit_bytes=50 << 20),
        cost_estimate=pl.CostEstimate(flops=16 * work, bytes_accessed=24 << 20, transcendentals=row_count * 1280 * 12),
    )(first, last, queries, keys, values_turned, key_feat, query_feat, tiles)


def backward_kernel(
    first_ref, last_ref, query_ref, query_turned_ref, key_ref, key_turned_ref, value_ref, grad_ref, grad_turned_ref, out_ref, log_ref,
    key_feat_ref, query_feat_ref, tiles_ref,
    grad_query_ref, grad_key_ref, grad_value_ref, tile_total,
    key_total, value_total, query_total, *, pairs, blocks, head_dim,
):
    key_total[...] = jnp.zeros_like(key_total)
    value_total[...] = jnp.zeros_like(value_total)
    tile_total[...] = jnp.zeros_like(tile_total)
    for block in range(blocks):
        rows = slice(block * TILE, (block + 1) * TILE)
        first, last = first_ref[block], last_ref[block]
        query_sides, grad_sides, query_stacks, grad_stacks, logs, deltas = [], [], [], [], [], []
        for pair in range(pairs):
            query_sides.append(query_side(query_turned_ref, query_feat_ref, block, pair, head_dim))
            grad_pair = grad_ref[rows, cols(pair)]
            grad_turned = grad_turned_ref[cols(pair), rows]
            grad_sides.append(halves(grad_turned, head_dim))
            query_stacks.append(halves_rows(query_ref[rows, cols(pair)], head_dim))
            grad_stacks.append(halves_rows(grad_pair, head_dim))
            logs.append(log_ref[0, block * pairs + pair : block * pairs + pair + 1, :])
            both = halves(grad_turned.astype(F32) * out_ref[cols(pair), rows], head_dim)
            deltas.append(jnp.sum(both, axis=0, keepdims=True))
        query_total[...] = jnp.zeros_like(query_total)

        def step(index, carry):
            start = pl.multiple_of((first + index * STEP) * TILE, TILE)
            span = pl.ds(start, SPAN)
            feat = key_feat_ref[span, :]
            tile = first + index * STEP - block + (blocks - 1)
            for pair in range(pairs):
                left = jnp.concatenate([key_ref[span, cols(pair)], feat], axis=1)
                bias = bias_of(tiles_ref, pair, tile)
                weights = jnp.exp(dot(left, query_sides[pair]) + bias - logs[pair])
                grad_weights = dot(value_ref[span, cols(pair)], grad_sides[pair])
                grad_scores = weights * (grad_weights - deltas[pair])
                tile_total[2 * pair, pl.ds(tile, STEP)] += grad_scores[:, :TILE].reshape(STEP, TILE, TILE)
                tile_total[2 * pair + 1, pl.ds(tile, STEP)] += grad_scores[:, TILE:].reshape(STEP, TILE, TILE)
                scores_low = grad_scores.astype(BF16)
                value_total[span, cols(pair)] += dot(weights.astype(BF16), grad_stacks[pair])
                key_total[span, cols(pair)] += dot(scores_low, query_stacks[pair])
                query_total[:, wide(pair)] += dot(key_turned_ref[cols(pair), span], scores_low)
            return carry

        lax.fori_loop(0, last, step, 0)
        for pair in range(pairs):
            grad_query_ref[cols(pair), rows] = merge_halves(query_total[:, wide(pair)], head_dim).astype(BF16)
    grad_key_ref[...] = key_total[...].astype(BF16)
    grad_value_ref[...] = value_total[...].astype(BF16)


def attend_back(first, last, queries, queries_turned, keys, keys_turned, values, grads, grads_turned, outs, logs, key_feat, query_feat, tiles, head_dim, pairs):
    row_count, width = queries.shape
    window = keys.shape[0]
    blocks = row_count // TILE
    groups = width // (pairs * TILE)
    heads, tile_count = tiles.shape[:2]
    kernel = functools.partial(backward_kernel, pairs=pairs, blocks=blocks, head_dim=head_dim)
    rows_spec = pl.BlockSpec((row_count, pairs * TILE), lambda g, a, b: (0, g))
    turned_spec = pl.BlockSpec((pairs * TILE, row_count), lambda g, a, b: (g, 0))
    window_spec = pl.BlockSpec((window, pairs * TILE), lambda g, a, b: (0, g))
    work = row_count * 1280 * width
    return pl.pallas_call(
        kernel,
        out_shape=(
            jax.ShapeDtypeStruct((width, row_count), BF16),
            jax.ShapeDtypeStruct((window, width), BF16),
            jax.ShapeDtypeStruct((window, width), BF16),
            jax.ShapeDtypeStruct((heads, tile_count, TILE, TILE), F32),
        ),
        grid_spec=pltpu.PrefetchScalarGridSpec(
            num_scalar_prefetch=2,
            grid=(groups,),
            in_specs=[
                rows_spec,
                turned_spec,
                window_spec,
                pl.BlockSpec((pairs * TILE, window), lambda g, a, b: (g, 0)),
                window_spec,
                rows_spec,
                turned_spec,
                turned_spec,
                pl.BlockSpec((1, blocks * pairs, 2 * TILE), lambda g, a, b: (g, 0, 0)),
                pl.BlockSpec((window, TILE), lambda g, a, b: (0, 0)),
                pl.BlockSpec((TILE, row_count), lambda g, a, b: (0, 0)),
                pl.BlockSpec((2 * pairs, tile_count, TILE, TILE), lambda g, a, b: (g, 0, 0, 0)),
            ],
            out_specs=[
                turned_spec,
                window_spec,
                window_spec,
                pl.BlockSpec((2 * pairs, tile_count, TILE, TILE), lambda g, a, b: (g, 0, 0, 0)),
            ],
            scratch_shapes=[
                pltpu.VMEM((window, pairs * TILE), F32),
                pltpu.VMEM((window, pairs * TILE), F32),
                pltpu.VMEM((TILE, pairs * 2 * TILE), F32),
            ],
        ),
        input_output_aliases={13: 3},
        compiler_params=pltpu.CompilerParams(vmem_limit_bytes=56 << 20),
        cost_estimate=pl.CostEstimate(flops=40 * work, bytes_accessed=32 << 20, transcendentals=row_count * 1280 * 12),
    )(first, last, queries, queries_turned, keys, keys_turned, values, grads, grads_turned, outs, logs, key_feat, query_feat, tiles)


def diagonal_kernel(range_ref, tiles_ref, line_ref):
    heads, tile_count = tiles_ref.shape[:2]
    for index in range(tile_count):
        used = (index >= range_ref[0]) & (index < range_ref[1])

        @pl.when(used)
        def _():
            for head in range(heads):
                tile = tiles_ref[head, index]
                padded = jnp.concatenate([tile, jnp.zeros_like(tile)], axis=1)
                size = TILE // 2
                while size >= 8:
                    padded = padded[:size] + pltpu.roll(padded[size:], 2 * TILE - size, 1)
                    size //= 2
                line_ref[head, index] = padded

        @pl.when(jnp.logical_not(used))
        def _():
            for head in range(heads):
                line_ref[head, index] = jnp.zeros((8, 2 * TILE), F32)


def diagonal_sums(tiles, used, chunk):
    heads, tile_count = tiles.shape[:2]
    results = []
    for start in range(0, heads, chunk):
        results.append(
            pl.pallas_call(
                diagonal_kernel,
                out_shape=jax.ShapeDtypeStruct((chunk, tile_count, 8, 2 * TILE), F32),
                grid_spec=pltpu.PrefetchScalarGridSpec(
                    num_scalar_prefetch=1,
                    grid=(1,),
                    in_specs=[
                        pl.BlockSpec(
                            (chunk, tile_count, TILE, TILE),
                            functools.partial(lambda first, h, r: (first, 0, 0, 0), start // chunk),
                        )
                    ],
                    out_specs=pl.BlockSpec((chunk, tile_count, 8, 2 * TILE), lambda h, r: (0, 0, 0, 0)),
                ),
                cost_estimate=SMALL,
                compiler_params=pltpu.CompilerParams(vmem_limit_bytes=40 << 20),
            )(used, tiles)
        )
    return jnp.concatenate(results, axis=0)


def shifted(value, axis, steps):
    count = lax.axis_size(axis)
    pairs = [(source, source + steps) for source in range(count) if 0 <= source + steps < count]
    return lax.ppermute(value, axis, pairs)


def flat_swap(value, mask):
    count = lax.axis_size("seq") * lax.axis_size("dp")
    return lax.ppermute(value, BOTH, [(source, source ^ mask) for source in range(count)])


def groups_of(low, bits):
    groups = []
    if bits % 2:
        groups.append((low, 1))
        low, bits = low + 1, bits - 1
    while bits:
        groups.append((low, 2))
        low, bits = low + 2, bits - 2
    return groups


def bits_of(count):
    bits = count.bit_length() - 1
    assert count == 1 << bits
    return bits


def all_groups(count):
    return [(0, 1)] + groups_of(1, bits_of(count) - 1)


def tie(*values):
    return lax.optimization_barrier(values)


def swaps(piece, group):
    low, bits = group
    return [flat_swap(piece, step << low) for step in range(1, 1 << bits)]


def swap_masks(masks, group):
    low, bits = group
    return [mask ^ (step << low) for step in range(1, 1 << bits) for mask in masks]


def stack_kernel(*refs):
    target = refs[-1]
    start = 0
    for source in refs[:-1]:
        target[start : start + source.shape[0]] = source[...]
        start += source.shape[0]


def stacked(pieces):
    if len(pieces) == 1:
        return pieces[0]
    count = sum(piece.shape[0] for piece in pieces)
    return pl.pallas_call(
        stack_kernel,
        out_shape=jax.ShapeDtypeStruct((count,) + pieces[0].shape[1:], pieces[0].dtype),
        in_specs=[pl.BlockSpec(memory_space=pltpu.VMEM)] * len(pieces),
        out_specs=pl.BlockSpec(memory_space=pltpu.VMEM),
        cost_estimate=SMALL,
        compiler_params=pltpu.CompilerParams(vmem_limit_bytes=40 << 20),
    )(*pieces)


def units_kernel(rank_ref, gate_ref, up_ref, units_ref, *, dp_count):
    left = lax.broadcasted_iota(jnp.int32, (gate_ref.shape[0], TILE), 1) < TILE // 2
    for side, source in enumerate((gate_ref, up_ref)):
        span = source.shape[1] // dp_count
        for owner in range(dp_count):
            for pair in range(span // TILE):
                halves_of = []
                for odd in range(2):
                    unit = (2 * pair + odd) * dp_count + owner
                    tile = source[:, unit // 2 * TILE : (unit // 2 + 1) * TILE]
                    halves_of.append(tile if unit % 2 == odd else pltpu.roll(tile, TILE // 2, 1))
                start = side * span + pair * TILE
                merged = jnp.where(left, halves_of[0], halves_of[1])
                units_ref[rank_ref[0] ^ owner, :, start : start + TILE] = merged.astype(BF16)


def units_of(gate_weight, up_weight, dp_rank, dp_count, seq_count, unit):
    rows, hidden_width = gate_weight.shape
    share = seq_count * unit
    if unit != TILE // 2 or rows % 8:
        both = jnp.stack([gate_weight.astype(BF16), up_weight.astype(BF16)], axis=1)
        both = both.reshape(rows, 2, seq_count, dp_count, unit)
        taken = [
            lax.dynamic_index_in_dim(both, dp_rank ^ mask, 3, keepdims=False).reshape(rows, 2 * share)
            for mask in range(dp_count)
        ]
        return jnp.stack(taken)
    return pl.pallas_call(
        functools.partial(units_kernel, dp_count=dp_count),
        out_shape=jax.ShapeDtypeStruct((dp_count, rows, 2 * share), BF16),
        in_specs=[pl.BlockSpec(memory_space=pltpu.SMEM)] + [pl.BlockSpec(memory_space=pltpu.VMEM)] * 2,
        out_specs=pl.BlockSpec(memory_space=pltpu.VMEM),
    )(dp_rank[None].astype(jnp.int32), gate_weight, up_weight)


def columns_kernel(rank_ref, *refs, dp_count):
    sources, (gate_ref, up_ref), scratch = refs[:dp_count], refs[dp_count : dp_count + 2], refs[-1]
    for mask in range(dp_count):
        scratch[rank_ref[0] ^ mask] = sources[mask][...].astype(F32)
    left = lax.broadcasted_iota(jnp.int32, (gate_ref.shape[0], TILE), 1) < TILE // 2
    for side, target in enumerate((gate_ref, up_ref)):
        span = target.shape[1] // dp_count
        for tile in range(target.shape[1] // TILE):
            halves_of = []
            for odd in range(2):
                group, owner = divmod(2 * tile + odd, dp_count)
                start = side * span + group // 2 * TILE
                part = scratch[owner, :, start : start + TILE]
                halves_of.append(part if group % 2 == odd else pltpu.roll(part, TILE // 2, 1))
            target[:, tile * TILE : (tile + 1) * TILE] = jnp.where(left, halves_of[0], halves_of[1])


def columns_of(parts, dp_rank, dp_count, seq_count, unit):
    rows = parts[0].shape[0]
    hidden_width = seq_count * dp_count * unit
    if unit != TILE // 2 or rows % 8:
        both = jnp.stack(parts)
        both = jnp.stack(
            [lax.dynamic_index_in_dim(both, dp_rank ^ index, 0, keepdims=False) for index in range(dp_count)], axis=1
        )
        both = both.reshape(rows, dp_count, 2, seq_count, unit).transpose(0, 2, 3, 1, 4)
        both = both.reshape(rows, 2, hidden_width).astype(F32)
        return both[:, 0], both[:, 1]
    return pl.pallas_call(
        functools.partial(columns_kernel, dp_count=dp_count),
        out_shape=(jax.ShapeDtypeStruct((rows, hidden_width), F32),) * 2,
        in_specs=[pl.BlockSpec(memory_space=pltpu.SMEM)] + [pl.BlockSpec(memory_space=pltpu.VMEM)] * dp_count,
        out_specs=(pl.BlockSpec(memory_space=pltpu.VMEM),) * 2,
        scratch_shapes=[pltpu.VMEM((dp_count,) + parts[0].shape, F32)],
        cost_estimate=SMALL,
    )(dp_rank[None].astype(jnp.int32), *parts)


def shard_kernel(*refs):
    target = refs[-1]
    start = 0
    for source in refs[:-1]:
        columns = source.shape[1]
        target[:, start : start + columns] = source[...].astype(BF16)
        start += columns


def side_by_side(arrays):
    columns = sum(array.shape[1] for array in arrays)
    return pl.pallas_call(
        shard_kernel,
        out_shape=jax.ShapeDtypeStruct((arrays[0].shape[0], columns), BF16),
        in_specs=[pl.BlockSpec(memory_space=pltpu.VMEM)] * len(arrays),
        out_specs=pl.BlockSpec(memory_space=pltpu.VMEM),
        cost_estimate=SMALL,
        compiler_params=pltpu.CompilerParams(vmem_limit_bytes=40 << 20),
    )(*arrays)


def norm_kernel(gain_ref, *refs):
    target = refs[-1]
    gain = gain_ref[...].astype(F32).T[:1]
    start = 0
    for source in refs[:-1]:
        rows = source[...].astype(F32)
        scale = lax.rsqrt(jnp.mean(rows * rows, axis=1, keepdims=True) + EPSILON)
        target[start : start + source.shape[0]] = (rows * scale * gain).astype(BF16)
        start += source.shape[0]


def normed_rows_of(pieces, weights, block):
    rows, width = pieces[0].shape
    return pl.pallas_call(
        norm_kernel,
        out_shape=jax.ShapeDtypeStruct((len(pieces) * rows, width), BF16),
        grid=(1,),
        in_specs=[pl.BlockSpec((width, TILE), lambda k: (0, block))]
        + [pl.BlockSpec((rows, width), lambda k: (0, 0))] * len(pieces),
        out_specs=pl.BlockSpec((len(pieces) * rows, width), lambda k: (0, 0)),
        compiler_params=pltpu.CompilerParams(vmem_limit_bytes=40 << 20),
    )(weights, *pieces)


def place_kernel(rank_ref, *refs, masks):
    target = refs[-1]
    rank = rank_ref[0]
    for source, part in zip(refs, masks):
        for index, mask in enumerate(part):
            target[rank ^ mask] = source[index]


def placed(held, masks, rank):
    count = sum(len(part) for part in masks)
    shape = held[0].shape[1:]
    return pl.pallas_call(
        functools.partial(place_kernel, masks=masks),
        out_shape=jax.ShapeDtypeStruct((count,) + shape, held[0].dtype),
        in_specs=[pl.BlockSpec(memory_space=pltpu.SMEM)] + [pl.BlockSpec(memory_space=pltpu.VMEM)] * len(held),
        out_specs=pl.BlockSpec(memory_space=pltpu.VMEM),
        cost_estimate=SMALL,
        compiler_params=pltpu.CompilerParams(vmem_limit_bytes=40 << 20),
    )(rank[None].astype(jnp.int32), *held)


def place_far_kernel(rank_ref, source_ref, pair_ref, down_ref, *, dp_count):
    for owner in range(source_ref.shape[0]):
        for entry in range(dp_count):
            pair_ref[owner * dp_count + (rank_ref[0] ^ entry)] = source_ref[owner, entry]
        for entry in range(dp_count // 2):
            down_ref[owner, entry] = source_ref[owner, dp_count + entry]


def place_far(held, dp_rank, dp_count):
    count = held.shape[0]
    shape = held.shape[2:]
    return pl.pallas_call(
        functools.partial(place_far_kernel, dp_count=dp_count),
        out_shape=(
            jax.ShapeDtypeStruct((count * dp_count,) + shape, held.dtype),
            jax.ShapeDtypeStruct((count, dp_count // 2) + shape, held.dtype),
        ),
        in_specs=[pl.BlockSpec(memory_space=pltpu.SMEM), pl.BlockSpec(memory_space=pltpu.VMEM)],
        out_specs=(pl.BlockSpec(memory_space=pltpu.VMEM), pl.BlockSpec(memory_space=pltpu.VMEM)),
        cost_estimate=SMALL,
        compiler_params=pltpu.CompilerParams(vmem_limit_bytes=40 << 20),
    )(dp_rank[None].astype(jnp.int32), held)


def split_and_swap(held, mine, group):
    low, bits = group
    held = held.reshape((-1, 1 << bits) + held.shape[1:])
    kept = lax.dynamic_index_in_dim(held, mine, 1, keepdims=False)
    got = [
        flat_swap(lax.dynamic_index_in_dim(held, mine ^ step, 1, keepdims=False), step << low)
        for step in range(1, 1 << bits)
    ]
    return kept, got


def joined(kept, got):
    return kept.astype(F32) + sum(piece.astype(F32) for piece in got)


def spread_dp(parts, bits):
    held = {(mask, 0): part for mask, part in parts.items()}
    for bit in range(bits):
        step = 1 << bit
        keys = sorted(key for key in held if key[0] & step)
        sent = flat_swap(jnp.stack([held[key] for key in keys]), step)
        held = {key: part for key, part in held.items() if not key[0] & step}
        held.update({(goal ^ step, source ^ step): sent[k] for k, (goal, source) in enumerate(keys)})
    return [held[(0, mask)] for mask in range(1 << bits)]


def gather_dp(value, bits):
    held = {0: value}
    for bit in range(bits - 1, -1, -1):
        held.update({mask ^ (1 << bit): flat_swap(piece, 1 << bit) for mask, piece in list(held.items())})
    return [held[mask] for mask in range(1 << bits)]


def scatter_dp(parts, bits):
    held = dict(enumerate(parts))
    for bit in range(bits):
        step = 1 << bit
        held = {
            mask: piece.astype(F32) + flat_swap(held[mask ^ step].astype(BF16), step).astype(F32)
            for mask, piece in held.items()
            if not mask & step
        }
    return held[0]


def sum_everywhere(value, groups):
    for group in groups:
        value = sum_in_pairs([value] + swaps(value, group))
    return value


def sum_in_pairs(values):
    while len(values) > 1:
        values = [values[k] + values[k + 1] for k in range(0, len(values), 2)]
    return values[0]


def parts_of(value, parts, to_rows):
    rows = value.shape[0] // parts
    columns = rows * value.shape[1] // to_rows
    if rows % 8 or to_rows % 8 or value.shape[1] % TILE or columns % TILE:
        return value.reshape(parts * to_rows, columns)
    tiles = value.reshape(parts, rows // 8, 8, value.shape[1] // TILE, TILE).transpose(0, 1, 3, 2, 4)
    tiles = tiles.reshape(parts, to_rows // 8, columns // TILE, 8, TILE).transpose(0, 1, 3, 2, 4)
    return tiles.reshape(parts * to_rows, columns)


def contract(left_side, right_side, left_dim, right_dim):
    return lax.dot_general(
        left_side, right_side, (((left_dim,), (right_dim,)), ((), ())), preferred_element_type=F32
    )


def gelu_pair(v):
    scale = 0.7978845608028654
    bent = jnp.tanh(scale * (v + 0.044715 * v * v * v))
    value = 0.5 * v * (1.0 + bent)
    slope = 0.5 * (1.0 + bent) + 0.5 * v * (1.0 - bent * bent) * scale * (1.0 + 3.0 * 0.044715 * v * v)
    return value, slope


def body(
    blocks,
    lengths,
    bucket_table,
    first_gain,
    query_weight,
    key_weight,
    value_weight,
    output_weight,
    table_weight,
    second_gain,
    gate_weight,
    up_weight,
    down_weight,
    cotangent,
):
    seq_count = lax.axis_size("seq")
    device_count = seq_count * lax.axis_size("dp")
    seq_rank = lax.axis_index("seq")
    row_count, width = blocks.shape[1:]
    pack_rows = row_count * seq_count
    bucket_count, heads = table_weight.shape
    head_dim = width // heads
    seq_total = lengths.shape[1]
    max_length = (bucket_table.shape[0] + 1) // 2
    shard_rows = query_weight.shape[0]
    hidden_width = gate_weight.shape[1]
    reach = min((max_length - 1 + row_count - 1) // row_count, seq_count - 1)
    query_blocks = row_count // TILE
    window = (2 * reach + 1) * row_count
    window_blocks = window // TILE
    tile_count = window_blocks + query_blocks - 1
    center = reach * query_blocks + query_blocks - 1
    pairs = 2 if window <= 2304 else 1

    dp_count = lax.axis_size("dp")
    dp_rank = lax.axis_index("dp")
    dp_bits = bits_of(dp_count)
    rank = seq_rank * dp_count + dp_rank
    groups = all_groups(device_count)
    own = blocks[0]

    gains = jnp.pad(jnp.stack([first_gain, second_gain], axis=1), ((0, 0), (0, TILE - 2)))
    near_shard = side_by_side([query_weight, key_weight, value_weight, output_weight, gains])

    unit = down_weight.shape[0]
    share = seq_count * unit
    pair_units = units_of(gate_weight, up_weight, dp_rank, dp_count, seq_count, unit)

    line_width = (tile_count + 1) * TILE
    ahead = (tile_count - center) * TILE - (max_length - 1)
    behind = line_width - ahead - bucket_table.shape[0]
    bucket_line = jnp.pad(bucket_table[::-1], (max(ahead, 0), max(behind, 0)), mode="edge")
    bucket_line = bucket_line[max(-ahead, 0) : max(-ahead, 0) + line_width]
    bucket_ids = jnp.arange(bucket_count, dtype=jnp.int32)
    line_hot = (bucket_line[None, :] == bucket_ids[:, None]).astype(F32)
    lines = lax.dot_general(table_weight, line_hot, (((0,), (0,)), ((), ())), precision=HIGHEST)

    order = groups[::-1]
    near_shard = near_shard[None]
    masks = [0]
    around = {0: own}
    near_held = near_shard
    stages = len(order)
    for stage, group in enumerate(order):
        got = swaps(near_held, group)
        last = stage == stages - 1
        moves = [step for step in range(1, reach + 1) if step == stage + 1 or (last and step > stage)]
        arrived = {}
        for step in moves:
            arrived[step] = shifted(own, "seq", step)
            arrived[-step] = shifted(own, "seq", -step)
        got_masks = swap_masks(masks, group)
        if last:
            held, masks = [near_held] + got, [masks] + [
                got_masks[k * len(masks) : (k + 1) * len(masks)] for k in range(len(got))
            ]
        else:
            if stage == 0:
                lines = tie(lines, got[0])[0]
            if stage == 1:
                tiles = bias_tiles(lines, tile_count)
                near_held, got, arrived, tiles = tie(near_held, got, arrived, tiles)
            else:
                near_held, got, arrived = tie(near_held, got, arrived)
            near_held = stacked([near_held] + got)
            masks = masks + got_masks
        around.update(arrived)
    near_full = placed(held, masks, rank)
    near_full = near_full.reshape(device_count * shard_rows, 4 * width + TILE)
    weight_query = near_full[:, :width]
    weight_key = near_full[:, width : 2 * width]
    weight_value = near_full[:, 2 * width : 3 * width]
    weight_output = near_full[:, 3 * width : 4 * width]
    gain_columns = near_full[:, 4 * width :]

    pair_parts = spread_dp({mask: pair_units[mask] for mask in range(dp_count)}, dp_bits)
    down_parts = parts_of(down_weight.astype(BF16), 1, shard_rows * dp_count // 2)
    down_parts = down_parts.reshape(dp_count // 2, shard_rows, 2 * share)
    far_shard = stacked([part[None] for part in pair_parts] + [down_parts])
    far_held = lax.all_gather(tie(far_shard, around)[0], "seq", axis=0, tiled=False)
    gain_one = gain_columns[:, 0].astype(F32)[None, :]
    gain_two = gain_columns[:, 1].astype(F32)[None, :]

    seq_ends = jnp.cumsum(lengths[0], dtype=jnp.int32)
    query_first = seq_rank * row_count
    window_first = query_first - reach * row_count

    def segments(at):
        return jnp.sum((at[:, None] >= seq_ends[None, :]).astype(jnp.int32), axis=1, dtype=jnp.int32)

    query_places = query_first + jnp.arange(row_count, dtype=jnp.int32)
    key_places = window_first + jnp.arange(window, dtype=jnp.int32)
    query_seg = segments(query_places)
    key_seg = jnp.where((key_places >= 0) & (key_places < pack_rows), segments(key_places), -1)
    lanes = jnp.arange(TILE, dtype=jnp.int32)
    key_feat = jnp.where(
        (key_seg[:, None] != lanes[None, :]) & (lanes[None, :] <= seq_total), BIG, 0.0
    ).astype(BF16)
    query_feat = (lanes[:, None] == query_seg[None, :]).astype(BF16)
    valid_rows = (query_seg < seq_total).astype(F32)
    seq_starts = jnp.concatenate([jnp.zeros((1,), jnp.int32), seq_ends])
    seq_stops = jnp.concatenate([seq_ends, jnp.full((1,), pack_rows, jnp.int32)])
    seq_ids = jnp.arange(seq_total + 1, dtype=jnp.int32)
    low_seg = query_seg[::TILE]
    high_seg = query_seg[TILE - 1 :: TILE]
    low = jnp.sum(jnp.where(low_seg[:, None] == seq_ids[None, :], seq_starts[None, :], 0), axis=1)
    high = jnp.sum(jnp.where(high_seg[:, None] == seq_ids[None, :], seq_stops[None, :], 0), axis=1)
    first = (low - window_first) // TILE
    last = (high - window_first + TILE - 1) // TILE
    steps = (last - first + STEP - 1) // STEP
    first = jnp.minimum(first, window_blocks - steps * STEP).astype(jnp.int32)
    steps = steps.astype(jnp.int32)


    window_normed = normed_rows_of(
        [around[-step] for step in range(-reach, reach + 1)], near_full, 4 * width // TILE
    )
    own_slice = slice(reach * row_count, (reach + 1) * row_count)
    tokens = own.astype(F32)
    scale_one = lax.rsqrt(jnp.mean(tokens * tokens, axis=1, keepdims=True) + EPSILON)
    normed_own = window_normed[own_slice]
    keys = contract(window_normed, weight_key, 1, 0).astype(BF16)
    values_turned = contract(weight_value, window_normed, 0, 1).astype(BF16)
    queries_turned = contract(weight_query, normed_own, 0, 1).astype(BF16)
    outs, logs = attend(
        first, steps, queries_turned, keys, values_turned, key_feat, query_feat, tiles, head_dim, pairs
    )
    far_full = place_far(tie(far_held, outs)[0], dp_rank, dp_count)
    weight_pair = far_full[0].reshape(device_count * shard_rows, 2 * share)
    weight_down = parts_of(far_full[1].reshape(-1, 2 * share), seq_count, unit)
    attended = (outs * valid_rows[None, :]).astype(BF16)
    middle = tokens + contract(attended, weight_output, 0, 0)

    scale_two = lax.rsqrt(jnp.mean(middle * middle, axis=1, keepdims=True) + EPSILON)
    second = middle * scale_two
    second_low = (second * gain_two).astype(BF16)
    every_second = jnp.concatenate(gather_dp(second_low, dp_bits), axis=0)
    every_grad = jnp.concatenate(gather_dp(cotangent[0], dp_bits), axis=0)
    both_ways = contract(every_second, weight_pair, 1, 0)
    gate_values, upward = both_ways[:, :share], both_ways[:, share:]
    active, slope = gelu_pair(gate_values)
    hidden = (active * upward).astype(BF16)
    grad_hidden = contract(every_grad, weight_down, 1, 1)
    grad_pair = jnp.concatenate(
        [(grad_hidden * upward * slope).astype(BF16), (grad_hidden * active).astype(BF16)], axis=1
    )
    every_back = contract(grad_pair, weight_pair, 1, 1).astype(BF16)
    grad_second = scatter_dp(jnp.split(every_back, dp_count, axis=0), dp_bits)
    every_out = contract(hidden, weight_down, 1, 0).astype(BF16)
    output = middle + scatter_dp(jnp.split(every_out, dp_count, axis=0), dp_bits)
    grad_out = cotangent[0]
    scaled = grad_second * gain_two
    grad_middle = grad_out.astype(F32) + scale_two * (
        scaled - second * jnp.mean(scaled * second, axis=1, keepdims=True)
    )
    grad_branch = grad_middle.astype(BF16)
    grad_mixed = (contract(grad_branch, weight_output, 1, 1).astype(BF16).astype(F32) * valid_rows[:, None]).astype(BF16)
    grad_mixed_turned = (
        contract(weight_output, grad_branch, 1, 1).astype(BF16).astype(F32) * valid_rows[None, :]
    ).astype(BF16)
    grad_output_weight = contract(attended, grad_branch, 1, 0).astype(BF16)
    grad_down = contract(hidden, every_grad, 0, 0).astype(BF16)
    grad_down = parts_of(grad_down, seq_count, shard_rows * dp_count // 2)
    grad_pair_weight = contract(every_second, grad_pair, 0, 0).astype(BF16)
    far_grads = jnp.concatenate(
        [
            grad_pair_weight.reshape(seq_count, dp_count, shard_rows, 2 * share),
            grad_down.reshape(seq_count, dp_count // 2, shard_rows, 2 * share),
        ],
        axis=1,
    )
    far_grads, grad_mixed, grad_mixed_turned, grad_output_weight = tie(
        far_grads, grad_mixed, grad_mixed_turned, grad_output_weight
    )
    far_sum = lax.psum_scatter(far_grads, "seq", scatter_dimension=0, tiled=True)[0]

    queries = contract(normed_own, weight_query, 1, 0).astype(BF16)
    keys_turned = contract(weight_key, window_normed, 0, 1).astype(BF16)
    values = contract(window_normed, weight_value, 1, 0).astype(BF16)
    grad_queries, grad_keys, grad_values, tile_sums = attend_back(
        first, steps, queries, queries_turned, keys, keys_turned, values, grad_mixed, grad_mixed_turned,
        outs, logs, key_feat, query_feat, tiles, head_dim, pairs,
    )
    partial = contract(grad_keys, weight_key, 1, 1) + contract(grad_values, weight_value, 1, 1)
    partial_low = partial.astype(BF16)

    def returned_from(low_rows, step):
        parts = []
        for turn in (step, -step):
            part = low_rows[(reach + turn) * row_count : (reach + turn + 1) * row_count]
            parts.append(shifted(part, "seq", turn))
        return parts

    steps_left = list(range(1, reach + 1))
    returned = []
    partial_low, grad_queries, grad_keys, grad_values, tile_sums = tie(
        partial_low, grad_queries, grad_keys, grad_values, tile_sums
    )
    tile_first = first - jnp.arange(query_blocks, dtype=jnp.int32) + (query_blocks - 1)
    used = jnp.stack([jnp.min(tile_first), jnp.max(tile_first + steps * STEP)])
    sums = diagonal_sums(tile_sums, used, 4)
    for step in (steps_left.pop(0), steps_left.pop(-1)) if reach > 1 else steps_left:
        returned += returned_from(partial_low, step)
    grad_query_weight = contract(normed_own, grad_queries, 0, 1).astype(BF16)
    grad_key_weight = contract(window_normed, grad_keys, 0, 0).astype(BF16)
    grad_value_weight = contract(window_normed, grad_values, 0, 0).astype(BF16)
    near_grads = jnp.concatenate([grad_query_weight, grad_key_weight, grad_value_weight, grad_output_weight], axis=1)
    near_held = near_grads.reshape(device_count, shard_rows, 4 * width)
    for stage, (low, bits) in enumerate(groups):
        kept, got = split_and_swap(near_held, (rank >> low) & ((1 << bits) - 1), (low, bits))
        arrived = []
        if stage and steps_left:
            last_stage = stage == len(groups) - 1
            for step in list(steps_left) if last_stage else steps_left[:1]:
                steps_left.remove(step)
                arrived += returned_from(partial_low, step)
        if stage == 0:
            kept, got, returned, partial_low, sums = tie(kept, got, returned, partial_low, sums)
        elif stage == 1:
            kept, got, arrived, partial_low, far_sum = tie(kept, got, arrived, partial_low, far_sum)
        else:
            kept, got, arrived, partial_low = tie(kept, got, arrived, partial_low)
        returned = returned + arrived
        total = joined(kept, got)
        near_held = total.astype(BF16)
    near_sum = total.reshape(shard_rows, 4 * width)
    grad_normed = partial[own_slice] + contract(grad_queries, weight_query, 0, 1)
    grad_normed = grad_normed + sum(piece.astype(F32) for piece in returned)
    pair_back = spread_dp(
        {mask: lax.dynamic_index_in_dim(far_sum, dp_rank ^ mask, 0, keepdims=False) for mask in range(dp_count)}, dp_bits
    )
    grad_gate_own, grad_up_own = columns_of(pair_back, dp_rank, dp_count, seq_count, unit)
    grad_down_own = parts_of(far_sum[dp_count:].astype(F32).reshape(-1, 2 * share), 1, unit)
    normed_rows = tokens * scale_one
    scaled_one = grad_normed * gain_one
    grad_blocks = grad_middle + scale_one * (
        scaled_one - normed_rows * jnp.mean(scaled_one * normed_rows, axis=1, keepdims=True)
    )

    diagonals = sum(jnp.roll(sums[:, :, row], -row, axis=2) for row in range(8))
    flipped = bucket_line.reshape(tile_count + 1, TILE)[::-1]
    bucket_at = jnp.concatenate([flipped[:-1], flipped[1:]], axis=1).reshape(-1)
    bucket_hot = (bucket_at[:, None] == bucket_ids[None, :]).astype(F32)
    grad_table = lax.dot_general(
        bucket_hot, diagonals.reshape(heads, -1), (((0,), (1,)), ((), ())), precision=HIGHEST
    )
    grad_table = sum_everywhere(grad_table, [(bit, 1) for bit in range(bits_of(device_count))])

    def gain_grad(gain, weights, grads):
        total = sum(jnp.sum(weight.astype(BF16).astype(F32) * grad, axis=1) for weight, grad in zip(weights, grads))
        return total / gain.astype(BF16).astype(F32)

    near_parts = [near_sum[:, k * width : (k + 1) * width] for k in range(4)]
    grad_gain_one = gain_grad(first_gain, (query_weight, key_weight, value_weight), near_parts[:3])
    grad_gain_two = gain_grad(second_gain, (gate_weight, up_weight), (grad_gate_own, grad_up_own))
    return (
        output.astype(BF16)[None],
        grad_blocks[None],
        grad_gain_one,
        near_parts[0],
        near_parts[1],
        near_parts[2],
        near_parts[3],
        grad_table,
        grad_gain_two,
        grad_gate_own,
        grad_up_own,
        grad_down_own,
    )


def solution(mesh):
    return jax.shard_map(
        body,
        mesh=mesh,
        in_specs=(
            P("dp", "seq", None),
            P("dp", None),
            P(),
            P(("seq", "dp")),
            P(("seq", "dp"), None),
            P(("seq", "dp"), None),
            P(("seq", "dp"), None),
            P(("seq", "dp"), None),
            P(),
            P(("seq", "dp")),
            P(("seq", "dp"), None),
            P(("seq", "dp"), None),
            P(("seq", "dp"), None),
            P("dp", "seq", None),
        ),
        out_specs=(
            P("dp", "seq", None),
            P("dp", "seq", None),
            P(("seq", "dp")),
            P(("seq", "dp"), None),
            P(("seq", "dp"), None),
            P(("seq", "dp"), None),
            P(("seq", "dp"), None),
            P(),
            P(("seq", "dp")),
            P(("seq", "dp"), None),
            P(("seq", "dp"), None),
            P(("seq", "dp"), None),
        ),
        check_vma=False,
    )
```

```python
import functools

import jax
import jax.numpy as jnp
from jax import lax
from jax.experimental import pallas as pl
from jax.experimental.pallas import tpu as pltpu
from jax.sharding import PartitionSpec as P

EPSILON = 1e-06
BIG = -1e30
HIGHEST = lax.Precision.HIGHEST
BOTH = ("seq", "dp")
SMALL = pl.CostEstimate(flops=1, bytes_accessed=1, transcendentals=0)
TILE = 128
STEP = 4
SPAN = STEP * TILE
F32 = jnp.float32
BF16 = jnp.bfloat16
LOWEST = -3.0e38


def bias_of(tiles_ref, pair, tile):
    halves_of = [tiles_ref[2 * pair + side, pl.ds(tile, STEP)].reshape(SPAN, TILE) for side in range(2)]
    return jnp.concatenate(halves_of, axis=1)


def dot(a, b):
    return jnp.dot(a, b, preferred_element_type=F32)


def tiles_kernel(line_ref, tiles_ref):
    tile_count = tiles_ref.shape[1]
    for index in range(tile_count):
        window = line_ref[0, :, pl.ds((tile_count - 1 - index) * TILE, 2 * TILE)]
        spread = jnp.broadcast_to(window, (TILE, 2 * TILE))
        rolled = pltpu.roll(spread, 0, 1, stride=1, stride_axis=0)
        tiles_ref[0, index] = rolled[:, TILE:]


def bias_tiles(lines, tile_count):
    heads, width = lines.shape
    return pl.pallas_call(
        tiles_kernel,
        out_shape=jax.ShapeDtypeStruct((heads, tile_count, TILE, TILE), F32),
        grid=(heads,),
        in_specs=[pl.BlockSpec((1, 1, width), lambda h: (h, 0, 0))],
        out_specs=pl.BlockSpec((1, tile_count, TILE, TILE), lambda h: (h, 0, 0, 0)),
        cost_estimate=SMALL,
    )(lines.reshape(heads, 1, width))


def halves(pair, head_dim):
    top = lax.broadcasted_iota(jnp.int32, pair.shape, 0) < head_dim
    zero = jnp.zeros_like(pair)
    return jnp.concatenate([jnp.where(top, pair, zero), jnp.where(top, zero, pair)], axis=1)


def halves_rows(pair, head_dim):
    left = lax.broadcasted_iota(jnp.int32, pair.shape, 1) < head_dim
    zero = jnp.zeros_like(pair)
    return jnp.concatenate([jnp.where(left, pair, zero), jnp.where(left, zero, pair)], axis=0)


def merge_halves(both, head_dim):
    top = lax.broadcasted_iota(jnp.int32, (both.shape[0], TILE), 0) < head_dim
    return jnp.where(top, both[:, :TILE], both[:, TILE:])


def fold(values, op):
    return op(values.reshape(values.shape[0] // 8, 8, values.shape[1]), axis=0)


def cols(pair):
    return slice(pair * TILE, (pair + 1) * TILE)


def wide(pair):
    return slice(pair * 2 * TILE, (pair + 1) * 2 * TILE)


def query_side(query_ref, query_feat_ref, block, pair, head_dim):
    rows = slice(block * TILE, (block + 1) * TILE)
    turned = query_ref[cols(pair), rows]
    feat = query_feat_ref[:, rows]
    return jnp.concatenate([halves(turned, head_dim), jnp.concatenate([feat, feat], axis=1)], axis=0)


def forward_kernel(
    first_ref, last_ref, query_ref, key_ref, value_turned_ref, key_feat_ref, query_feat_ref, tiles_ref,
    out_ref, log_ref, score_ref, total_ref, *, pairs, blocks, head_dim,
):
    for block in range(blocks):
        rows = slice(block * TILE, (block + 1) * TILE)
        first, last = first_ref[block], last_ref[block]
        query_sides = [query_side(query_ref, query_feat_ref, block, pair, head_dim) for pair in range(pairs)]

        def score_step(index, highest):
            start = pl.multiple_of((first + index * STEP) * TILE, TILE)
            feat = key_feat_ref[pl.ds(start, SPAN), :]
            tile = first + index * STEP - block + (blocks - 1)
            result = []
            for pair in range(pairs):
                left = jnp.concatenate([key_ref[pl.ds(start, SPAN), cols(pair)], feat], axis=1)
                bias = bias_of(tiles_ref, pair, tile)
                scores = dot(left, query_sides[pair]) + bias
                score_ref[pl.ds(start, SPAN), wide(pair)] = scores
                result.append(jnp.maximum(highest[pair], fold(scores, jnp.max)))
            return tuple(result)

        start_max = tuple(jnp.full((8, 2 * TILE), LOWEST, F32) for _ in range(pairs))
        highest = lax.fori_loop(0, last, score_step, start_max)
        peak = [jnp.max(value, axis=0, keepdims=True) for value in highest]
        total_ref[...] = jnp.zeros_like(total_ref)

        def value_step(index, sums):
            start = pl.multiple_of((first + index * STEP) * TILE, TILE)
            result = []
            for pair in range(pairs):
                weights = jnp.exp(score_ref[pl.ds(start, SPAN), wide(pair)] - peak[pair])
                result.append(sums[pair] + fold(weights, jnp.sum))
                total_ref[:, wide(pair)] += dot(
                    value_turned_ref[cols(pair), pl.ds(start, SPAN)], weights.astype(BF16)
                )
            return tuple(result)

        start_sum = tuple(jnp.zeros((8, 2 * TILE), F32) for _ in range(pairs))
        sums = lax.fori_loop(0, last, value_step, start_sum)
        for pair in range(pairs):
            denominator = jnp.sum(sums[pair], axis=0, keepdims=True)
            out_ref[cols(pair), rows] = merge_halves(total_ref[:, wide(pair)] / denominator, head_dim)
            log_ref[0, block * pairs + pair : block * pairs + pair + 1, :] = peak[pair] + jnp.log(denominator)


def attend(first, last, queries, keys, values_turned, key_feat, query_feat, tiles, head_dim, pairs):
    width, row_count = queries.shape
    window = keys.shape[0]
    blocks = row_count // TILE
    groups = width // (pairs * TILE)
    tile_count = tiles.shape[1]
    kernel = functools.partial(
        forward_kernel, pairs=pairs, blocks=blocks, head_dim=head_dim
    )
    work = row_count * 1280 * width
    return pl.pallas_call(
        kernel,
        out_shape=(
            jax.ShapeDtypeStruct((width, row_count), F32),
            jax.ShapeDtypeStruct((groups, blocks * pairs, 2 * TILE), F32),
        ),
        grid_spec=pltpu.PrefetchScalarGridSpec(
            num_scalar_prefetch=2,
            grid=(groups,),
            in_specs=[
                pl.BlockSpec((pairs * TILE, row_count), lambda g, a, b: (g, 0)),
                pl.BlockSpec((window, pairs * TILE), lambda g, a, b: (0, g)),
                pl.BlockSpec((pairs * TILE, window), lambda g, a, b: (g, 0)),
                pl.BlockSpec((window, TILE), lambda g, a, b: (0, 0)),
                pl.BlockSpec((TILE, row_count), lambda g, a, b: (0, 0)),
                pl.BlockSpec((2 * pairs, tile_count, TILE, TILE), lambda g, a, b: (g, 0, 0, 0)),
            ],
            out_specs=[
                pl.BlockSpec((pairs * TILE, row_count), lambda g, a, b: (g, 0)),
                pl.BlockSpec((1, blocks * pairs, 2 * TILE), lambda g, a, b: (g, 0, 0)),
            ],
            scratch_shapes=[
                pltpu.VMEM((window, pairs * 2 * TILE), F32),
                pltpu.VMEM((TILE, pairs * 2 * TILE), F32),
            ],
        ),
        compiler_params=pltpu.CompilerParams(vmem_limit_bytes=50 << 20),
        cost_estimate=pl.CostEstimate(flops=16 * work, bytes_accessed=24 << 20, transcendentals=row_count * 1280 * 12),
    )(first, last, queries, keys, values_turned, key_feat, query_feat, tiles)


def backward_kernel(
    first_ref, last_ref, query_ref, query_turned_ref, key_ref, key_turned_ref, value_ref, grad_ref, grad_turned_ref, out_ref, log_ref,
    key_feat_ref, query_feat_ref, tiles_ref,
    grad_query_ref, grad_key_ref, grad_value_ref, tile_total,
    key_total, value_total, query_total, *, pairs, blocks, head_dim,
):
    key_total[...] = jnp.zeros_like(key_total)
    value_total[...] = jnp.zeros_like(value_total)
    tile_total[...] = jnp.zeros_like(tile_total)
    for block in range(blocks):
        rows = slice(block * TILE, (block + 1) * TILE)
        first, last = first_ref[block], last_ref[block]
        query_sides, grad_sides, query_stacks, grad_stacks, logs, deltas = [], [], [], [], [], []
        for pair in range(pairs):
            query_sides.append(query_side(query_turned_ref, query_feat_ref, block, pair, head_dim))
            grad_pair = grad_ref[rows, cols(pair)]
            grad_turned = grad_turned_ref[cols(pair), rows]
            grad_sides.append(halves(grad_turned, head_dim))
            query_stacks.append(halves_rows(query_ref[rows, cols(pair)], head_dim))
            grad_stacks.append(halves_rows(grad_pair, head_dim))
            logs.append(log_ref[0, block * pairs + pair : block * pairs + pair + 1, :])
            both = halves(grad_turned.astype(F32) * out_ref[cols(pair), rows], head_dim)
            deltas.append(jnp.sum(both, axis=0, keepdims=True))
        query_total[...] = jnp.zeros_like(query_total)

        def step(index, carry):
            start = pl.multiple_of((first + index * STEP) * TILE, TILE)
            span = pl.ds(start, SPAN)
            feat = key_feat_ref[span, :]
            tile = first + index * STEP - block + (blocks - 1)
            for pair in range(pairs):
                left = jnp.concatenate([key_ref[span, cols(pair)], feat], axis=1)
                bias = bias_of(tiles_ref, pair, tile)
                weights = jnp.exp(dot(left, query_sides[pair]) + bias - logs[pair])
                grad_weights = dot(value_ref[span, cols(pair)], grad_sides[pair])
                grad_scores = weights * (grad_weights - deltas[pair])
                tile_total[2 * pair, pl.ds(tile, STEP)] += grad_scores[:, :TILE].reshape(STEP, TILE, TILE)
                tile_total[2 * pair + 1, pl.ds(tile, STEP)] += grad_scores[:, TILE:].reshape(STEP, TILE, TILE)
                scores_low = grad_scores.astype(BF16)
                value_total[span, cols(pair)] += dot(weights.astype(BF16), grad_stacks[pair])
                key_total[span, cols(pair)] += dot(scores_low, query_stacks[pair])
                query_total[:, wide(pair)] += dot(key_turned_ref[cols(pair), span], scores_low)
            return carry

        lax.fori_loop(0, last, step, 0)
        for pair in range(pairs):
            grad_query_ref[cols(pair), rows] = merge_halves(query_total[:, wide(pair)], head_dim).astype(BF16)
    grad_key_ref[...] = key_total[...].astype(BF16)
    grad_value_ref[...] = value_total[...].astype(BF16)


def attend_back(first, last, queries, queries_turned, keys, keys_turned, values, grads, grads_turned, outs, logs, key_feat, query_feat, tiles, head_dim, pairs):
    row_count, width = queries.shape
    window = keys.shape[0]
    blocks = row_count // TILE
    groups = width // (pairs * TILE)
    heads, tile_count = tiles.shape[:2]
    kernel = functools.partial(backward_kernel, pairs=pairs, blocks=blocks, head_dim=head_dim)
    rows_spec = pl.BlockSpec((row_count, pairs * TILE), lambda g, a, b: (0, g))
    turned_spec = pl.BlockSpec((pairs * TILE, row_count), lambda g, a, b: (g, 0))
    window_spec = pl.BlockSpec((window, pairs * TILE), lambda g, a, b: (0, g))
    work = row_count * 1280 * width
    return pl.pallas_call(
        kernel,
        out_shape=(
            jax.ShapeDtypeStruct((width, row_count), BF16),
            jax.ShapeDtypeStruct((window, width), BF16),
            jax.ShapeDtypeStruct((window, width), BF16),
            jax.ShapeDtypeStruct((heads, tile_count, TILE, TILE), F32),
        ),
        grid_spec=pltpu.PrefetchScalarGridSpec(
            num_scalar_prefetch=2,
            grid=(groups,),
            in_specs=[
                rows_spec,
                turned_spec,
                window_spec,
                pl.BlockSpec((pairs * TILE, window), lambda g, a, b: (g, 0)),
                window_spec,
                rows_spec,
                turned_spec,
                turned_spec,
                pl.BlockSpec((1, blocks * pairs, 2 * TILE), lambda g, a, b: (g, 0, 0)),
                pl.BlockSpec((window, TILE), lambda g, a, b: (0, 0)),
                pl.BlockSpec((TILE, row_count), lambda g, a, b: (0, 0)),
                pl.BlockSpec((2 * pairs, tile_count, TILE, TILE), lambda g, a, b: (g, 0, 0, 0)),
            ],
            out_specs=[
                turned_spec,
                window_spec,
                window_spec,
                pl.BlockSpec((2 * pairs, tile_count, TILE, TILE), lambda g, a, b: (g, 0, 0, 0)),
            ],
            scratch_shapes=[
                pltpu.VMEM((window, pairs * TILE), F32),
                pltpu.VMEM((window, pairs * TILE), F32),
                pltpu.VMEM((TILE, pairs * 2 * TILE), F32),
            ],
        ),
        input_output_aliases={13: 3},
        compiler_params=pltpu.CompilerParams(vmem_limit_bytes=56 << 20),
        cost_estimate=pl.CostEstimate(flops=40 * work, bytes_accessed=32 << 20, transcendentals=row_count * 1280 * 12),
    )(first, last, queries, queries_turned, keys, keys_turned, values, grads, grads_turned, outs, logs, key_feat, query_feat, tiles)


def table_kernel(range_ref, tiles_ref, bucket_ref, table_ref):
    index = pl.program_id(0)
    heads = tiles_ref.shape[0]

    @pl.when(index == 0)
    def _():
        table_ref[...] = jnp.zeros_like(table_ref)

    @pl.when((index >= range_ref[0]) & (index < range_ref[1]))
    def _():
        rows = []
        for head in range(heads):
            tile = tiles_ref[head, 0]
            padded = jnp.concatenate([tile, jnp.zeros_like(tile)], axis=1)
            size = TILE // 2
            while size >= 1:
                padded = padded[:size] + pltpu.roll(padded[size:], 2 * TILE - size, 1)
                size //= 2
            rows.append(padded)
        sums = jnp.concatenate(rows, axis=0)
        buckets = lax.broadcasted_iota(jnp.int32, (table_ref.shape[1], 2 * TILE), 0)
        hot = (buckets == bucket_ref[0]).astype(F32)
        table_ref[...] += lax.dot_general(
            sums, hot, (((1,), (1,)), ((), ())), preferred_element_type=F32, precision=HIGHEST
        )


def table_sums(tiles, used, bucket_at, bucket_count):
    heads, tile_count = tiles.shape[:2]

    def held(index, used_ref):
        return jnp.minimum(jnp.maximum(index, used_ref[0]), used_ref[1] - 1)

    return pl.pallas_call(
        table_kernel,
        out_shape=jax.ShapeDtypeStruct((heads, bucket_count), F32),
        grid_spec=pltpu.PrefetchScalarGridSpec(
            num_scalar_prefetch=1,
            grid=(tile_count,),
            in_specs=[
                pl.BlockSpec((heads, 1, TILE, TILE), lambda t, r: (0, held(t, r), 0, 0)),
                pl.BlockSpec((1, 1, 2 * TILE), lambda t, r: (t, 0, 0)),
            ],
            out_specs=pl.BlockSpec((heads, bucket_count), lambda t, r: (0, 0)),
        ),
        cost_estimate=SMALL,
        compiler_params=pltpu.CompilerParams(vmem_limit_bytes=40 << 20),
    )(used, tiles, bucket_at)


def window_kernel(range_ref, key_ref, value_ref, key_weight_ref, value_weight_ref, out_ref):
    index = pl.program_id(0)
    tiles = out_ref.shape[0] // TILE
    needed = ((index + 1) * tiles > range_ref[0]) & (index * tiles < range_ref[1])

    @pl.when(needed)
    def _():
        out_ref[...] = (
            contract(key_ref[...], key_weight_ref[...], 1, 1) + contract(value_ref[...], value_weight_ref[...], 1, 1)
        ).astype(BF16)

    @pl.when(jnp.logical_not(needed))
    def _():
        out_ref[...] = jnp.zeros_like(out_ref)


def window_gradient(grad_keys, grad_values, weights, spots, covered, row_count):
    window, width = grad_keys.shape
    tiles = row_count // TILE

    def rows(index, covered_ref):
        low = lax.div(covered_ref[0], tiles)
        high = lax.div(covered_ref[1] - 1, tiles)
        return jnp.minimum(jnp.maximum(index, low), high), 0

    return pl.pallas_call(
        window_kernel,
        out_shape=jax.ShapeDtypeStruct((window, width), BF16),
        grid_spec=pltpu.PrefetchScalarGridSpec(
            num_scalar_prefetch=1,
            grid=(window // row_count,),
            in_specs=[
                pl.BlockSpec((row_count, width), rows),
                pl.BlockSpec((row_count, width), rows),
                pl.BlockSpec((width, width), lambda k, r: (0, spots[0])),
                pl.BlockSpec((width, width), lambda k, r: (0, spots[1])),
            ],
            out_specs=pl.BlockSpec((row_count, width), lambda k, r: (k, 0)),
        ),
        cost_estimate=SMALL,
        compiler_params=pltpu.CompilerParams(vmem_limit_bytes=40 << 20),
    )(covered, grad_keys, grad_values, weights, weights)


def shifted(value, axis, steps):
    count = lax.axis_size(axis)
    pairs = [(source, source + steps) for source in range(count) if 0 <= source + steps < count]
    return lax.ppermute(value, axis, pairs)


def flat_swap(value, mask):
    count = lax.axis_size("seq") * lax.axis_size("dp")
    return lax.ppermute(value, BOTH, [(source, source ^ mask) for source in range(count)])


def groups_of(low, bits):
    groups = []
    if bits % 2:
        groups.append((low, 1))
        low, bits = low + 1, bits - 1
    while bits:
        groups.append((low, 2))
        low, bits = low + 2, bits - 2
    return groups


def bits_of(count):
    bits = count.bit_length() - 1
    assert count == 1 << bits
    return bits


def all_groups(count):
    return [(0, 1)] + groups_of(1, bits_of(count) - 1)


def tie(*values):
    return lax.optimization_barrier(values)


def swaps(piece, group):
    low, bits = group
    return [flat_swap(piece, step << low) for step in range(1, 1 << bits)]


def swap_masks(masks, group):
    low, bits = group
    return [mask ^ (step << low) for step in range(1, 1 << bits) for mask in masks]


def stack_kernel(*refs):
    target = refs[-1]
    start = 0
    for source in refs[:-1]:
        target[start : start + source.shape[0]] = source[...]
        start += source.shape[0]


def stacked(pieces):
    if len(pieces) == 1:
        return pieces[0]
    count = sum(piece.shape[0] for piece in pieces)
    return pl.pallas_call(
        stack_kernel,
        out_shape=jax.ShapeDtypeStruct((count,) + pieces[0].shape[1:], pieces[0].dtype),
        in_specs=[pl.BlockSpec(memory_space=pltpu.VMEM)] * len(pieces),
        out_specs=pl.BlockSpec(memory_space=pltpu.VMEM),
        cost_estimate=SMALL,
        compiler_params=pltpu.CompilerParams(vmem_limit_bytes=40 << 20),
    )(*pieces)


def units_kernel(rank_ref, gate_ref, up_ref, units_ref, *, dp_count):
    left = lax.broadcasted_iota(jnp.int32, (gate_ref.shape[0], TILE), 1) < TILE // 2
    for side, source in enumerate((gate_ref, up_ref)):
        span = source.shape[1] // dp_count
        for owner in range(dp_count):
            for pair in range(span // TILE):
                halves_of = []
                for odd in range(2):
                    unit = (2 * pair + odd) * dp_count + owner
                    tile = source[:, unit // 2 * TILE : (unit // 2 + 1) * TILE]
                    halves_of.append(tile if unit % 2 == odd else pltpu.roll(tile, TILE // 2, 1))
                start = side * span + pair * TILE
                merged = jnp.where(left, halves_of[0], halves_of[1])
                units_ref[rank_ref[0] ^ owner, :, start : start + TILE] = merged.astype(BF16)


def units_of(gate_weight, up_weight, dp_rank, dp_count, seq_count, unit):
    rows, hidden_width = gate_weight.shape
    share = seq_count * unit
    if unit != TILE // 2 or rows % 8:
        both = jnp.stack([gate_weight.astype(BF16), up_weight.astype(BF16)], axis=1)
        both = both.reshape(rows, 2, seq_count, dp_count, unit)
        taken = [
            lax.dynamic_index_in_dim(both, dp_rank ^ mask, 3, keepdims=False).reshape(rows, 2 * share)
            for mask in range(dp_count)
        ]
        return jnp.stack(taken)
    return pl.pallas_call(
        functools.partial(units_kernel, dp_count=dp_count),
        out_shape=jax.ShapeDtypeStruct((dp_count, rows, 2 * share), BF16),
        in_specs=[pl.BlockSpec(memory_space=pltpu.SMEM)] + [pl.BlockSpec(memory_space=pltpu.VMEM)] * 2,
        out_specs=pl.BlockSpec(memory_space=pltpu.VMEM),
    )(dp_rank[None].astype(jnp.int32), gate_weight, up_weight)


def columns_kernel(rank_ref, *refs, dp_count):
    sources, (gate_ref, up_ref), scratch = refs[:dp_count], refs[dp_count : dp_count + 2], refs[-1]
    for mask in range(dp_count):
        scratch[rank_ref[0] ^ mask] = sources[mask][...].astype(F32)
    left = lax.broadcasted_iota(jnp.int32, (gate_ref.shape[0], TILE), 1) < TILE // 2
    for side, target in enumerate((gate_ref, up_ref)):
        span = target.shape[1] // dp_count
        for tile in range(target.shape[1] // TILE):
            halves_of = []
            for odd in range(2):
                group, owner = divmod(2 * tile + odd, dp_count)
                start = side * span + group // 2 * TILE
                part = scratch[owner, :, start : start + TILE]
                halves_of.append(part if group % 2 == odd else pltpu.roll(part, TILE // 2, 1))
            target[:, tile * TILE : (tile + 1) * TILE] = jnp.where(left, halves_of[0], halves_of[1])


def columns_of(parts, dp_rank, dp_count, seq_count, unit):
    rows = parts[0].shape[0]
    hidden_width = seq_count * dp_count * unit
    if unit != TILE // 2 or rows % 8:
        both = jnp.stack(parts)
        both = jnp.stack(
            [lax.dynamic_index_in_dim(both, dp_rank ^ index, 0, keepdims=False) for index in range(dp_count)], axis=1
        )
        both = both.reshape(rows, dp_count, 2, seq_count, unit).transpose(0, 2, 3, 1, 4)
        both = both.reshape(rows, 2, hidden_width).astype(F32)
        return both[:, 0], both[:, 1]
    return pl.pallas_call(
        functools.partial(columns_kernel, dp_count=dp_count),
        out_shape=(jax.ShapeDtypeStruct((rows, hidden_width), F32),) * 2,
        in_specs=[pl.BlockSpec(memory_space=pltpu.SMEM)] + [pl.BlockSpec(memory_space=pltpu.VMEM)] * dp_count,
        out_specs=(pl.BlockSpec(memory_space=pltpu.VMEM),) * 2,
        scratch_shapes=[pltpu.VMEM((dp_count,) + parts[0].shape, F32)],
        cost_estimate=SMALL,
    )(dp_rank[None].astype(jnp.int32), *parts)


def shard_kernel(*refs):
    target = refs[-1]
    start = 0
    for source in refs[:-1]:
        columns = source.shape[1]
        target[:, start : start + columns] = source[...].astype(BF16)
        start += columns


def side_by_side(arrays):
    columns = sum(array.shape[1] for array in arrays)
    return pl.pallas_call(
        shard_kernel,
        out_shape=jax.ShapeDtypeStruct((arrays[0].shape[0], columns), BF16),
        in_specs=[pl.BlockSpec(memory_space=pltpu.VMEM)] * len(arrays),
        out_specs=pl.BlockSpec(memory_space=pltpu.VMEM),
        cost_estimate=SMALL,
        compiler_params=pltpu.CompilerParams(vmem_limit_bytes=40 << 20),
    )(*arrays)


def norm_kernel(gain_ref, *refs):
    target = refs[-1]
    gain = gain_ref[...].astype(F32).T[:1]
    start = 0
    for source in refs[:-1]:
        rows = source[...].astype(F32)
        scale = lax.rsqrt(jnp.mean(rows * rows, axis=1, keepdims=True) + EPSILON)
        target[start : start + source.shape[0]] = (rows * scale * gain).astype(BF16)
        start += source.shape[0]


def normed_rows_of(pieces, weights, block):
    rows, width = pieces[0].shape
    return pl.pallas_call(
        norm_kernel,
        out_shape=jax.ShapeDtypeStruct((len(pieces) * rows, width), BF16),
        grid=(1,),
        in_specs=[pl.BlockSpec((width, TILE), lambda k: (0, block))]
        + [pl.BlockSpec((rows, width), lambda k: (0, 0))] * len(pieces),
        out_specs=pl.BlockSpec((len(pieces) * rows, width), lambda k: (0, 0)),
        compiler_params=pltpu.CompilerParams(vmem_limit_bytes=40 << 20),
    )(weights, *pieces)


def place_kernel(rank_ref, *refs, masks):
    target = refs[-1]
    rank = rank_ref[0]
    for source, part in zip(refs, masks):
        for index, mask in enumerate(part):
            target[rank ^ mask] = source[index]


def placed(held, masks, rank):
    count = sum(len(part) for part in masks)
    shape = held[0].shape[1:]
    return pl.pallas_call(
        functools.partial(place_kernel, masks=masks),
        out_shape=jax.ShapeDtypeStruct((count,) + shape, held[0].dtype),
        in_specs=[pl.BlockSpec(memory_space=pltpu.SMEM)] + [pl.BlockSpec(memory_space=pltpu.VMEM)] * len(held),
        out_specs=pl.BlockSpec(memory_space=pltpu.VMEM),
        cost_estimate=SMALL,
        compiler_params=pltpu.CompilerParams(vmem_limit_bytes=40 << 20),
    )(rank[None].astype(jnp.int32), *held)


def place_far_kernel(rank_ref, *refs, masks, dp_count):
    pair_ref, down_ref = refs[-2:]
    rank = rank_ref[0]
    for source, part in zip(refs, masks):
        for index, mask in enumerate(part):
            owner = rank ^ mask
            for entry in range(dp_count):
                pair_ref[owner ^ entry] = source[index, entry]
            for entry in range(dp_count // 2):
                down_ref[owner // dp_count, entry] = source[index, dp_count + entry]


def place_far(held, masks, rank, dp_count):
    count = sum(len(part) for part in masks)
    shape = held[0].shape[2:]
    dtype = held[0].dtype
    return pl.pallas_call(
        functools.partial(place_far_kernel, masks=masks, dp_count=dp_count),
        out_shape=(
            jax.ShapeDtypeStruct((count * dp_count,) + shape, dtype),
            jax.ShapeDtypeStruct((count, dp_count // 2) + shape, dtype),
        ),
        in_specs=[pl.BlockSpec(memory_space=pltpu.SMEM)] + [pl.BlockSpec(memory_space=pltpu.VMEM)] * len(held),
        out_specs=(pl.BlockSpec(memory_space=pltpu.VMEM), pl.BlockSpec(memory_space=pltpu.VMEM)),
        cost_estimate=SMALL,
        compiler_params=pltpu.CompilerParams(vmem_limit_bytes=40 << 20),
    )(rank[None].astype(jnp.int32), *held)


def split_and_swap(held, mine, group):
    low, bits = group
    held = held.reshape((-1, 1 << bits) + held.shape[1:])
    kept = lax.dynamic_index_in_dim(held, mine, 1, keepdims=False)
    got = [
        flat_swap(lax.dynamic_index_in_dim(held, mine ^ step, 1, keepdims=False), step << low)
        for step in range(1, 1 << bits)
    ]
    return kept, got


def joined(kept, got):
    values = [piece.astype(F32) for piece in [kept] + got]
    while len(values) > 1:
        values = [values[k] + values[k + 1] for k in range(0, len(values), 2)]
    return values[0]


def spread_dp(parts, bits):
    held = {(mask, 0): part for mask, part in parts.items()}
    for bit in range(bits):
        step = 1 << bit
        keys = sorted(key for key in held if key[0] & step)
        sent = flat_swap(jnp.stack([held[key] for key in keys]), step)
        held = {key: part for key, part in held.items() if not key[0] & step}
        held.update({(goal ^ step, source ^ step): sent[k] for k, (goal, source) in enumerate(keys)})
    return [held[(0, mask)] for mask in range(1 << bits)]


def gather_dp(value, bits):
    held = {0: value}
    for bit in range(bits - 1, -1, -1):
        held.update({mask ^ (1 << bit): flat_swap(piece, 1 << bit) for mask, piece in list(held.items())})
    return [held[mask] for mask in range(1 << bits)]


def scatter_dp(parts, bits):
    held = dict(enumerate(parts))
    for bit in range(bits):
        step = 1 << bit
        held = {
            mask: piece.astype(F32) + flat_swap(held[mask ^ step].astype(BF16), step).astype(F32)
            for mask, piece in held.items()
            if not mask & step
        }
    return held[0]


def parts_of(value, parts, to_rows):
    rows = value.shape[0] // parts
    columns = rows * value.shape[1] // to_rows
    if rows % 8 or to_rows % 8 or value.shape[1] % TILE or columns % TILE:
        return value.reshape(parts * to_rows, columns)
    tiles = value.reshape(parts, rows // 8, 8, value.shape[1] // TILE, TILE).transpose(0, 1, 3, 2, 4)
    tiles = tiles.reshape(parts, to_rows // 8, columns // TILE, 8, TILE).transpose(0, 1, 3, 2, 4)
    return tiles.reshape(parts * to_rows, columns)


def contract(left_side, right_side, left_dim, right_dim):
    return lax.dot_general(
        left_side, right_side, (((left_dim,), (right_dim,)), ((), ())), preferred_element_type=F32
    )


def gelu_pair(v):
    scale = 0.7978845608028654
    bent = jnp.tanh(scale * (v + 0.044715 * v * v * v))
    value = 0.5 * v * (1.0 + bent)
    slope = 0.5 * (1.0 + bent) + 0.5 * v * (1.0 - bent * bent) * scale * (1.0 + 3.0 * 0.044715 * v * v)
    return value, slope


def body(
    blocks,
    lengths,
    bucket_table,
    first_gain,
    query_weight,
    key_weight,
    value_weight,
    output_weight,
    table_weight,
    second_gain,
    gate_weight,
    up_weight,
    down_weight,
    cotangent,
):
    seq_count = lax.axis_size("seq")
    device_count = seq_count * lax.axis_size("dp")
    seq_rank = lax.axis_index("seq")
    row_count, width = blocks.shape[1:]
    pack_rows = row_count * seq_count
    bucket_count, heads = table_weight.shape
    head_dim = width // heads
    seq_total = lengths.shape[1]
    max_length = (bucket_table.shape[0] + 1) // 2
    shard_rows = query_weight.shape[0]
    hidden_width = gate_weight.shape[1]
    reach = min((max_length - 1 + row_count - 1) // row_count, seq_count - 1)
    query_blocks = row_count // TILE
    window = (2 * reach + 1) * row_count
    window_blocks = window // TILE
    tile_count = window_blocks + query_blocks - 1
    center = reach * query_blocks + query_blocks - 1
    pairs = 2 if window <= 2304 else 1

    dp_count = lax.axis_size("dp")
    dp_rank = lax.axis_index("dp")
    dp_bits = bits_of(dp_count)
    rank = seq_rank * dp_count + dp_rank
    groups = all_groups(device_count)
    seq_groups = groups_of(dp_bits, bits_of(seq_count))
    own = blocks[0]

    gains = jnp.pad(jnp.stack([first_gain, second_gain], axis=1), ((0, 0), (0, TILE - 2)))
    near_shard = side_by_side([query_weight, key_weight, value_weight, output_weight, gains])

    unit = down_weight.shape[0]
    share = seq_count * unit
    pair_units = units_of(gate_weight, up_weight, dp_rank, dp_count, seq_count, unit)

    line_width = (tile_count + 1) * TILE
    ahead = (tile_count - center) * TILE - (max_length - 1)
    behind = line_width - ahead - bucket_table.shape[0]
    bucket_line = jnp.pad(bucket_table[::-1], (max(ahead, 0), max(behind, 0)), mode="edge")
    bucket_line = bucket_line[max(-ahead, 0) : max(-ahead, 0) + line_width]
    bucket_ids = jnp.arange(bucket_count, dtype=jnp.int32)
    line_hot = (bucket_line[None, :] == bucket_ids[:, None]).astype(F32)
    lines = lax.dot_general(table_weight, line_hot, (((0,), (0,)), ((), ())), precision=HIGHEST)

    order = groups[::-1]
    near_shard = near_shard[None]
    masks = [0]
    around = {0: own}
    near_held = near_shard
    stages = len(order)
    for stage, group in enumerate(order):
        got = swaps(near_held, group)
        last = stage == stages - 1
        moves = [step for step in range(1, reach + 1) if step == stage + 1 or (last and step > stage)]
        arrived = {}
        for step in moves:
            arrived[step] = shifted(own, "seq", step)
            arrived[-step] = shifted(own, "seq", -step)
        got_masks = swap_masks(masks, group)
        if last:
            held, masks = [near_held] + got, [masks] + [
                got_masks[k * len(masks) : (k + 1) * len(masks)] for k in range(len(got))
            ]
        else:
            if stage == 0:
                lines = tie(lines, got[0])[0]
            if stage == 1:
                tiles = bias_tiles(lines, tile_count)
                near_held, got, arrived, tiles = tie(near_held, got, arrived, tiles)
            else:
                near_held, got, arrived = tie(near_held, got, arrived)
            near_held = stacked([near_held] + got)
            masks = masks + got_masks
        around.update(arrived)
    near_full = placed(held, masks, rank)
    near_full = near_full.reshape(device_count * shard_rows, 4 * width + TILE)
    weight_query = near_full[:, :width]
    weight_key = near_full[:, width : 2 * width]
    weight_value = near_full[:, 2 * width : 3 * width]
    weight_output = near_full[:, 3 * width : 4 * width]
    gain_columns = near_full[:, 4 * width :]

    pair_parts = spread_dp({mask: pair_units[mask] for mask in range(dp_count)}, dp_bits)
    down_parts = parts_of(down_weight.astype(BF16), 1, shard_rows * dp_count // 2)
    down_parts = down_parts.reshape(dp_count // 2, shard_rows, 2 * share)
    far_shard = stacked([part[None] for part in pair_parts] + [down_parts])
    far_shard = tie(far_shard, around)[0][None]
    far_order = seq_groups[::-1]
    far_first = swaps(far_shard, far_order[0])
    far_own = [piece for group in far_order[1:2] for piece in swaps(far_shard, group)]
    gain_one = gain_columns[:, 0].astype(F32)[None, :]
    gain_two = gain_columns[:, 1].astype(F32)[None, :]

    seq_ends = jnp.cumsum(lengths[0], dtype=jnp.int32)
    query_first = seq_rank * row_count
    window_first = query_first - reach * row_count

    def segments(at):
        return jnp.sum((at[:, None] >= seq_ends[None, :]).astype(jnp.int32), axis=1, dtype=jnp.int32)

    query_places = query_first + jnp.arange(row_count, dtype=jnp.int32)
    key_places = window_first + jnp.arange(window, dtype=jnp.int32)
    query_seg = segments(query_places)
    key_seg = jnp.where((key_places >= 0) & (key_places < pack_rows), segments(key_places), -1)
    lanes = jnp.arange(TILE, dtype=jnp.int32)
    key_feat = jnp.where(
        (key_seg[:, None] != lanes[None, :]) & (lanes[None, :] <= seq_total), BIG, 0.0
    ).astype(BF16)
    query_feat = (lanes[:, None] == query_seg[None, :]).astype(BF16)
    valid_rows = (query_seg < seq_total).astype(F32)
    seq_starts = jnp.concatenate([jnp.zeros((1,), jnp.int32), seq_ends])
    seq_stops = jnp.concatenate([seq_ends, jnp.full((1,), pack_rows, jnp.int32)])
    seq_ids = jnp.arange(seq_total + 1, dtype=jnp.int32)
    low_seg = query_seg[::TILE]
    high_seg = query_seg[TILE - 1 :: TILE]
    low = jnp.sum(jnp.where(low_seg[:, None] == seq_ids[None, :], seq_starts[None, :], 0), axis=1)
    high = jnp.sum(jnp.where(high_seg[:, None] == seq_ids[None, :], seq_stops[None, :], 0), axis=1)
    first = (low - window_first) // TILE
    last = (high - window_first + TILE - 1) // TILE
    steps = (last - first + STEP - 1) // STEP
    first = jnp.minimum(first, window_blocks - steps * STEP).astype(jnp.int32)
    steps = steps.astype(jnp.int32)


    window_normed = normed_rows_of(
        [around[-step] for step in range(-reach, reach + 1)], near_full, 4 * width // TILE
    )
    own_slice = slice(reach * row_count, (reach + 1) * row_count)
    tokens = own.astype(F32)
    scale_one = lax.rsqrt(jnp.mean(tokens * tokens, axis=1, keepdims=True) + EPSILON)
    normed_own = window_normed[own_slice]
    keys = contract(window_normed, weight_key, 1, 0).astype(BF16)
    values_turned = contract(weight_value, window_normed, 0, 1).astype(BF16)
    queries_turned = contract(weight_query, normed_own, 0, 1).astype(BF16)
    outs, logs = attend(
        first, steps, queries_turned, keys, values_turned, key_feat, query_feat, tiles, head_dim, pairs
    )
    far_first = stacked(tie(far_first, outs)[0])
    first_masks = swap_masks([0], far_order[0])
    far_held, far_masks = [far_shard, far_first], [[0], first_masks]
    for number, group in enumerate(far_order[1:]):
        got, got_masks = [], []
        for piece, part in zip(far_held, far_masks):
            more = far_own if piece is far_shard and number == 0 else swaps(piece, group)
            extra = swap_masks(part, group)
            got += more
            got_masks += [extra[k * len(part) : (k + 1) * len(part)] for k in range(len(more))]
        far_held, far_masks = far_held + got, far_masks + got_masks
    far_full = place_far(far_held, far_masks, rank, dp_count)
    weight_pair = far_full[0].reshape(device_count * shard_rows, 2 * share)
    weight_down = parts_of(far_full[1].reshape(-1, 2 * share), seq_count, unit)
    attended = (outs * valid_rows[None, :]).astype(BF16)
    middle = tokens + contract(attended, weight_output, 0, 0)

    scale_two = lax.rsqrt(jnp.mean(middle * middle, axis=1, keepdims=True) + EPSILON)
    second = middle * scale_two
    second_low = (second * gain_two).astype(BF16)
    every_second = jnp.concatenate(gather_dp(second_low, dp_bits), axis=0)
    every_grad = jnp.concatenate(gather_dp(cotangent[0], dp_bits), axis=0)
    both_ways = contract(every_second, weight_pair, 1, 0)
    gate_values, upward = both_ways[:, :share], both_ways[:, share:]
    active, slope = gelu_pair(gate_values)
    hidden = (active * upward).astype(BF16)
    grad_hidden = contract(every_grad, weight_down, 1, 1)
    grad_pair = jnp.concatenate(
        [(grad_hidden * upward * slope).astype(BF16), (grad_hidden * active).astype(BF16)], axis=1
    )
    every_back = contract(grad_pair, weight_pair, 1, 1).astype(BF16)
    grad_second = scatter_dp(jnp.split(every_back, dp_count, axis=0), dp_bits)
    every_out = contract(hidden, weight_down, 1, 0).astype(BF16)
    output = middle + scatter_dp(jnp.split(every_out, dp_count, axis=0), dp_bits)
    grad_out = cotangent[0]
    scaled = grad_second * gain_two
    grad_middle = grad_out.astype(F32) + scale_two * (
        scaled - second * jnp.mean(scaled * second, axis=1, keepdims=True)
    )
    grad_branch = grad_middle.astype(BF16)
    grad_mixed = (contract(grad_branch, weight_output, 1, 1).astype(BF16).astype(F32) * valid_rows[:, None]).astype(BF16)
    grad_mixed_turned = (
        contract(weight_output, grad_branch, 1, 1).astype(BF16).astype(F32) * valid_rows[None, :]
    ).astype(BF16)
    grad_output_weight = contract(attended, grad_branch, 1, 0).astype(BF16)
    grad_down = contract(hidden, every_grad, 0, 0).astype(BF16)
    grad_down = parts_of(grad_down, seq_count, shard_rows * dp_count // 2)
    grad_pair_weight = contract(every_second, grad_pair, 0, 0).astype(BF16)
    far_grads = jnp.concatenate(
        [
            grad_pair_weight.reshape(seq_count, dp_count, shard_rows, 2 * share),
            grad_down.reshape(seq_count, dp_count // 2, shard_rows, 2 * share),
        ],
        axis=1,
    )
    far_grads, grad_mixed, grad_mixed_turned, grad_output_weight = tie(
        far_grads, grad_mixed, grad_mixed_turned, grad_output_weight
    )
    bits = seq_groups[0][1]
    far_kept, far_got = split_and_swap(far_grads, seq_rank & ((1 << bits) - 1), seq_groups[0])

    queries = contract(normed_own, weight_query, 1, 0).astype(BF16)
    keys_turned = contract(weight_key, window_normed, 0, 1).astype(BF16)
    values = contract(window_normed, weight_value, 1, 0).astype(BF16)
    grad_queries, grad_keys, grad_values, tile_sums = attend_back(
        first, steps, queries, queries_turned, keys, keys_turned, values, grad_mixed, grad_mixed_turned,
        outs, logs, key_feat, query_feat, tiles, head_dim, pairs,
    )
    grad_queries, grad_keys, grad_values, tile_sums, far_kept, far_got = tie(
        grad_queries, grad_keys, grad_values, tile_sums, far_kept, far_got
    )
    for low, bits in seq_groups[1:]:
        far_held = joined(far_kept, far_got).astype(BF16)
        far_kept, far_got = split_and_swap(far_held, (rank >> low) & ((1 << bits) - 1), (low, bits))
    covered = jnp.stack([jnp.min(first), jnp.max(first + steps * STEP)])
    partial_low = window_gradient(grad_keys, grad_values, near_full, (1, 2), covered, row_count)

    def returned_from(low_rows, step):
        parts = []
        for turn in (step, -step):
            part = low_rows[(reach + turn) * row_count : (reach + turn + 1) * row_count]
            parts.append(shifted(part, "seq", turn))
        return parts

    returned = returned_from(partial_low, 1)
    grad_query_weight = contract(normed_own, grad_queries, 0, 1).astype(BF16)
    grad_key_weight = contract(window_normed, grad_keys, 0, 0).astype(BF16)
    grad_value_weight = contract(window_normed, grad_values, 0, 0).astype(BF16)

    tile_first = first - jnp.arange(query_blocks, dtype=jnp.int32) + (query_blocks - 1)
    used = jnp.stack([jnp.min(tile_first), jnp.max(tile_first + steps * STEP)])
    flipped = bucket_line.reshape(tile_count + 1, TILE)[::-1]
    bucket_at = jnp.concatenate([flipped[:-1], flipped[1:]], axis=1)[:, None, :]
    grad_table = table_sums(tile_sums, used, bucket_at, bucket_count).T
    table_rows = -(-grad_table.size // TILE)
    table_block = jnp.pad(grad_table.reshape(-1), (0, table_rows * TILE - grad_table.size)).reshape(table_rows, TILE)
    table_block = jnp.pad(table_block, ((0, shard_rows - table_rows), (0, 0))).astype(BF16)
    near_grads = jnp.concatenate(
        [
            grad_query_weight,
            grad_key_weight,
            grad_value_weight,
            grad_output_weight,
            jnp.tile(table_block, (device_count, 1)),
        ],
        axis=1,
    )
    near_grads, partial_low, returned, far_kept, far_got = tie(
        near_grads, partial_low, returned, far_kept, far_got
    )
    far_sum = joined(far_kept, far_got).reshape(far_grads.shape[1:]).astype(BF16)

    left = list(range(reach, 2, -1))
    waiting = returned_from(partial_low, 2) if reach > 1 else []
    near_held = near_grads.reshape(device_count, shard_rows, 4 * width + TILE)
    for stage, (low, bits) in enumerate(groups):
        kept, got = split_and_swap(near_held, (rank >> low) & ((1 << bits) - 1), (low, bits))
        if stage == 0:
            kept, got, partial_low = tie(kept, got, partial_low)
        else:
            arrived = returned_from(partial_low, left.pop(0)) if left else []
            kept, got, arrived, waiting, partial_low, far_sum = tie(
                kept, got, arrived, waiting, partial_low, far_sum
            )
            returned, waiting = returned + arrived + waiting, []
        total = joined(kept, got)
        near_held = total.astype(BF16)
    for step in left:
        returned = returned + returned_from(partial_low, step)
    near_sum = total.reshape(shard_rows, 4 * width + TILE)
    grad_normed = partial_low[own_slice].astype(F32) + contract(grad_queries, weight_query, 0, 1)
    grad_normed = grad_normed + sum(piece.astype(F32) for piece in returned)
    pair_back = spread_dp(
        {mask: lax.dynamic_index_in_dim(far_sum, dp_rank ^ mask, 0, keepdims=False) for mask in range(dp_count)}, dp_bits
    )
    grad_gate_own, grad_up_own = columns_of(pair_back, dp_rank, dp_count, seq_count, unit)
    grad_down_own = parts_of(far_sum[dp_count:].astype(F32).reshape(-1, 2 * share), 1, unit)
    normed_rows = tokens * scale_one
    scaled_one = grad_normed * gain_one
    grad_blocks = grad_middle + scale_one * (
        scaled_one - normed_rows * jnp.mean(scaled_one * normed_rows, axis=1, keepdims=True)
    )

    grad_table = near_sum[:table_rows, 4 * width :].reshape(-1)[: table_weight.size].reshape(table_weight.shape)

    def gain_grad(gain, weights, grads):
        total = sum(jnp.sum(weight.astype(BF16).astype(F32) * grad, axis=1) for weight, grad in zip(weights, grads))
        return total / gain.astype(BF16).astype(F32)

    near_parts = [near_sum[:, k * width : (k + 1) * width] for k in range(4)]
    grad_gain_one = gain_grad(first_gain, (query_weight, key_weight, value_weight), near_parts[:3])
    grad_gain_two = gain_grad(second_gain, (gate_weight, up_weight), (grad_gate_own, grad_up_own))
    return (
        output.astype(BF16)[None],
        grad_blocks[None],
        grad_gain_one,
        near_parts[0],
        near_parts[1],
        near_parts[2],
        near_parts[3],
        grad_table,
        grad_gain_two,
        grad_gate_own,
        grad_up_own,
        grad_down_own,
    )


def solution(mesh):
    return jax.shard_map(
        body,
        mesh=mesh,
        in_specs=(
            P("dp", "seq", None),
            P("dp", None),
            P(),
            P(("seq", "dp")),
            P(("seq", "dp"), None),
            P(("seq", "dp"), None),
            P(("seq", "dp"), None),
            P(("seq", "dp"), None),
            P(),
            P(("seq", "dp")),
            P(("seq", "dp"), None),
            P(("seq", "dp"), None),
            P(("seq", "dp"), None),
            P("dp", "seq", None),
        ),
        out_specs=(
            P("dp", "seq", None),
            P("dp", "seq", None),
            P(("seq", "dp")),
            P(("seq", "dp"), None),
            P(("seq", "dp"), None),
            P(("seq", "dp"), None),
            P(("seq", "dp"), None),
            P(),
            P(("seq", "dp")),
            P(("seq", "dp"), None),
            P(("seq", "dp"), None),
            P(("seq", "dp"), None),
        ),
        check_vma=False,
    )
```

```python
import functools

import jax
import jax.numpy as jnp
from jax import lax
from jax.experimental import pallas as pl
from jax.experimental.pallas import tpu as pltpu
from jax.sharding import PartitionSpec as P

EPSILON = 1e-06
BIG = -1e30
HIGHEST = lax.Precision.HIGHEST
BOTH = ("seq", "dp")
SMALL = pl.CostEstimate(flops=1, bytes_accessed=1, transcendentals=0)
TILE = 128
STEP = 4
SPAN = STEP * TILE
F32 = jnp.float32
BF16 = jnp.bfloat16
LOWEST = -3.0e38


def bias_of(tiles_ref, pair, tile):
    halves_of = [tiles_ref[2 * pair + side, pl.ds(tile, STEP)].reshape(SPAN, TILE) for side in range(2)]
    return jnp.concatenate(halves_of, axis=1)


def dot(a, b):
    return jnp.dot(a, b, preferred_element_type=F32)


def tiles_kernel(line_ref, tiles_ref):
    tile_count = tiles_ref.shape[1]
    for index in range(tile_count):
        window = line_ref[0, :, pl.ds((tile_count - 1 - index) * TILE, 2 * TILE)]
        spread = jnp.broadcast_to(window, (TILE, 2 * TILE))
        rolled = pltpu.roll(spread, 0, 1, stride=1, stride_axis=0)
        tiles_ref[0, index] = rolled[:, TILE:]


def bias_tiles(lines, tile_count):
    heads, width = lines.shape
    return pl.pallas_call(
        tiles_kernel,
        out_shape=jax.ShapeDtypeStruct((heads, tile_count, TILE, TILE), F32),
        grid=(heads,),
        in_specs=[pl.BlockSpec((1, 1, width), lambda h: (h, 0, 0))],
        out_specs=pl.BlockSpec((1, tile_count, TILE, TILE), lambda h: (h, 0, 0, 0)),
        cost_estimate=SMALL,
    )(lines.reshape(heads, 1, width))


def halves(pair, head_dim):
    top = lax.broadcasted_iota(jnp.int32, pair.shape, 0) < head_dim
    zero = jnp.zeros_like(pair)
    return jnp.concatenate([jnp.where(top, pair, zero), jnp.where(top, zero, pair)], axis=1)


def halves_rows(pair, head_dim):
    left = lax.broadcasted_iota(jnp.int32, pair.shape, 1) < head_dim
    zero = jnp.zeros_like(pair)
    return jnp.concatenate([jnp.where(left, pair, zero), jnp.where(left, zero, pair)], axis=0)


def merge_halves(both, head_dim):
    top = lax.broadcasted_iota(jnp.int32, (both.shape[0], TILE), 0) < head_dim
    return jnp.where(top, both[:, :TILE], both[:, TILE:])


def fold(values, op):
    return op(values.reshape(values.shape[0] // 8, 8, values.shape[1]), axis=0)


def cols(pair):
    return slice(pair * TILE, (pair + 1) * TILE)


def wide(pair):
    return slice(pair * 2 * TILE, (pair + 1) * 2 * TILE)


def query_side(query_ref, query_feat_ref, block, pair, head_dim):
    rows = slice(block * TILE, (block + 1) * TILE)
    turned = query_ref[cols(pair), rows]
    feat = query_feat_ref[:, rows]
    return jnp.concatenate([halves(turned, head_dim), jnp.concatenate([feat, feat], axis=1)], axis=0)


def forward_kernel(
    first_ref, last_ref, query_ref, key_ref, value_turned_ref, key_feat_ref, query_feat_ref, tiles_ref,
    out_ref, log_ref, score_ref, total_ref, *, pairs, blocks, head_dim,
):
    for block in range(blocks):
        rows = slice(block * TILE, (block + 1) * TILE)
        first, last = first_ref[block], last_ref[block]
        query_sides = [query_side(query_ref, query_feat_ref, block, pair, head_dim) for pair in range(pairs)]

        def score_step(index, highest):
            start = pl.multiple_of((first + index * STEP) * TILE, TILE)
            feat = key_feat_ref[pl.ds(start, SPAN), :]
            tile = first + index * STEP - block + (blocks - 1)
            result = []
            for pair in range(pairs):
                left = jnp.concatenate([key_ref[pl.ds(start, SPAN), cols(pair)], feat], axis=1)
                bias = bias_of(tiles_ref, pair, tile)
                scores = dot(left, query_sides[pair]) + bias
                score_ref[pl.ds(start, SPAN), wide(pair)] = scores
                result.append(jnp.maximum(highest[pair], fold(scores, jnp.max)))
            return tuple(result)

        start_max = tuple(jnp.full((8, 2 * TILE), LOWEST, F32) for _ in range(pairs))
        highest = lax.fori_loop(0, last, score_step, start_max)
        peak = [jnp.max(value, axis=0, keepdims=True) for value in highest]
        total_ref[...] = jnp.zeros_like(total_ref)

        def value_step(index, sums):
            start = pl.multiple_of((first + index * STEP) * TILE, TILE)
            result = []
            for pair in range(pairs):
                weights = jnp.exp(score_ref[pl.ds(start, SPAN), wide(pair)] - peak[pair])
                result.append(sums[pair] + fold(weights, jnp.sum))
                total_ref[:, wide(pair)] += dot(
                    value_turned_ref[cols(pair), pl.ds(start, SPAN)], weights.astype(BF16)
                )
            return tuple(result)

        start_sum = tuple(jnp.zeros((8, 2 * TILE), F32) for _ in range(pairs))
        sums = lax.fori_loop(0, last, value_step, start_sum)
        for pair in range(pairs):
            denominator = jnp.sum(sums[pair], axis=0, keepdims=True)
            out_ref[cols(pair), rows] = merge_halves(total_ref[:, wide(pair)] / denominator, head_dim)
            log_ref[0, block * pairs + pair : block * pairs + pair + 1, :] = peak[pair] + jnp.log(denominator)


def attend(first, last, queries, keys, values_turned, key_feat, query_feat, tiles, head_dim, pairs):
    width, row_count = queries.shape
    window = keys.shape[0]
    blocks = row_count // TILE
    groups = width // (pairs * TILE)
    tile_count = tiles.shape[1]
    kernel = functools.partial(
        forward_kernel, pairs=pairs, blocks=blocks, head_dim=head_dim
    )
    work = row_count * 1280 * width
    return pl.pallas_call(
        kernel,
        out_shape=(
            jax.ShapeDtypeStruct((width, row_count), F32),
            jax.ShapeDtypeStruct((groups, blocks * pairs, 2 * TILE), F32),
        ),
        grid_spec=pltpu.PrefetchScalarGridSpec(
            num_scalar_prefetch=2,
            grid=(groups,),
            in_specs=[
                pl.BlockSpec((pairs * TILE, row_count), lambda g, a, b: (g, 0)),
                pl.BlockSpec((window, pairs * TILE), lambda g, a, b: (0, g)),
                pl.BlockSpec((pairs * TILE, window), lambda g, a, b: (g, 0)),
                pl.BlockSpec((window, TILE), lambda g, a, b: (0, 0)),
                pl.BlockSpec((TILE, row_count), lambda g, a, b: (0, 0)),
                pl.BlockSpec((2 * pairs, tile_count, TILE, TILE), lambda g, a, b: (g, 0, 0, 0)),
            ],
            out_specs=[
                pl.BlockSpec((pairs * TILE, row_count), lambda g, a, b: (g, 0)),
                pl.BlockSpec((1, blocks * pairs, 2 * TILE), lambda g, a, b: (g, 0, 0)),
            ],
            scratch_shapes=[
                pltpu.VMEM((window, pairs * 2 * TILE), F32),
                pltpu.VMEM((TILE, pairs * 2 * TILE), F32),
            ],
        ),
        compiler_params=pltpu.CompilerParams(vmem_limit_bytes=50 << 20),
        cost_estimate=pl.CostEstimate(flops=16 * work, bytes_accessed=24 << 20, transcendentals=row_count * 1280 * 12),
    )(first, last, queries, keys, values_turned, key_feat, query_feat, tiles)


def backward_kernel(
    first_ref, last_ref, query_ref, query_turned_ref, key_ref, key_turned_ref, value_ref, grad_ref, grad_turned_ref, out_ref, log_ref,
    key_feat_ref, query_feat_ref, tiles_ref,
    grad_query_ref, grad_key_ref, grad_value_ref, tile_total,
    key_total, value_total, query_total, *, pairs, blocks, head_dim,
):
    key_total[...] = jnp.zeros_like(key_total)
    value_total[...] = jnp.zeros_like(value_total)
    tile_total[...] = jnp.zeros_like(tile_total)
    for block in range(blocks):
        rows = slice(block * TILE, (block + 1) * TILE)
        first, last = first_ref[block], last_ref[block]
        query_sides, grad_sides, query_stacks, grad_stacks, logs, deltas = [], [], [], [], [], []
        for pair in range(pairs):
            query_sides.append(query_side(query_turned_ref, query_feat_ref, block, pair, head_dim))
            grad_pair = grad_ref[rows, cols(pair)]
            grad_turned = grad_turned_ref[cols(pair), rows]
            grad_sides.append(halves(grad_turned, head_dim))
            query_stacks.append(halves_rows(query_ref[rows, cols(pair)], head_dim))
            grad_stacks.append(halves_rows(grad_pair, head_dim))
            logs.append(log_ref[0, block * pairs + pair : block * pairs + pair + 1, :])
            both = halves(grad_turned.astype(F32) * out_ref[cols(pair), rows], head_dim)
            deltas.append(jnp.sum(both, axis=0, keepdims=True))
        query_total[...] = jnp.zeros_like(query_total)

        def step(index, carry):
            start = pl.multiple_of((first + index * STEP) * TILE, TILE)
            span = pl.ds(start, SPAN)
            feat = key_feat_ref[span, :]
            tile = first + index * STEP - block + (blocks - 1)
            for pair in range(pairs):
                left = jnp.concatenate([key_ref[span, cols(pair)], feat], axis=1)
                bias = bias_of(tiles_ref, pair, tile)
                weights = jnp.exp(dot(left, query_sides[pair]) + bias - logs[pair])
                grad_weights = dot(value_ref[span, cols(pair)], grad_sides[pair])
                grad_scores = weights * (grad_weights - deltas[pair])
                tile_total[2 * pair, pl.ds(tile, STEP)] += grad_scores[:, :TILE].reshape(STEP, TILE, TILE)
                tile_total[2 * pair + 1, pl.ds(tile, STEP)] += grad_scores[:, TILE:].reshape(STEP, TILE, TILE)
                scores_low = grad_scores.astype(BF16)
                value_total[span, cols(pair)] += dot(weights.astype(BF16), grad_stacks[pair])
                key_total[span, cols(pair)] += dot(scores_low, query_stacks[pair])
                query_total[:, wide(pair)] += dot(key_turned_ref[cols(pair), span], scores_low)
            return carry

        lax.fori_loop(0, last, step, 0)
        for pair in range(pairs):
            grad_query_ref[cols(pair), rows] = merge_halves(query_total[:, wide(pair)], head_dim).astype(BF16)
    grad_key_ref[...] = key_total[...].astype(BF16)
    grad_value_ref[...] = value_total[...].astype(BF16)


def attend_back(first, last, queries, queries_turned, keys, keys_turned, values, grads, grads_turned, outs, logs, key_feat, query_feat, tiles, head_dim, pairs):
    row_count, width = queries.shape
    window = keys.shape[0]
    blocks = row_count // TILE
    groups = width // (pairs * TILE)
    heads, tile_count = tiles.shape[:2]
    kernel = functools.partial(backward_kernel, pairs=pairs, blocks=blocks, head_dim=head_dim)
    rows_spec = pl.BlockSpec((row_count, pairs * TILE), lambda g, a, b: (0, g))
    turned_spec = pl.BlockSpec((pairs * TILE, row_count), lambda g, a, b: (g, 0))
    window_spec = pl.BlockSpec((window, pairs * TILE), lambda g, a, b: (0, g))
    work = row_count * 1280 * width
    return pl.pallas_call(
        kernel,
        out_shape=(
            jax.ShapeDtypeStruct((width, row_count), BF16),
            jax.ShapeDtypeStruct((window, width), BF16),
            jax.ShapeDtypeStruct((window, width), BF16),
            jax.ShapeDtypeStruct((heads, tile_count, TILE, TILE), F32),
        ),
        grid_spec=pltpu.PrefetchScalarGridSpec(
            num_scalar_prefetch=2,
            grid=(groups,),
            in_specs=[
                rows_spec,
                turned_spec,
                window_spec,
                pl.BlockSpec((pairs * TILE, window), lambda g, a, b: (g, 0)),
                window_spec,
                rows_spec,
                turned_spec,
                turned_spec,
                pl.BlockSpec((1, blocks * pairs, 2 * TILE), lambda g, a, b: (g, 0, 0)),
                pl.BlockSpec((window, TILE), lambda g, a, b: (0, 0)),
                pl.BlockSpec((TILE, row_count), lambda g, a, b: (0, 0)),
                pl.BlockSpec((2 * pairs, tile_count, TILE, TILE), lambda g, a, b: (g, 0, 0, 0)),
            ],
            out_specs=[
                turned_spec,
                window_spec,
                window_spec,
                pl.BlockSpec((2 * pairs, tile_count, TILE, TILE), lambda g, a, b: (g, 0, 0, 0)),
            ],
            scratch_shapes=[
                pltpu.VMEM((window, pairs * TILE), F32),
                pltpu.VMEM((window, pairs * TILE), F32),
                pltpu.VMEM((TILE, pairs * 2 * TILE), F32),
            ],
        ),
        input_output_aliases={13: 3},
        compiler_params=pltpu.CompilerParams(vmem_limit_bytes=56 << 20),
        cost_estimate=pl.CostEstimate(flops=40 * work, bytes_accessed=32 << 20, transcendentals=row_count * 1280 * 12),
    )(first, last, queries, queries_turned, keys, keys_turned, values, grads, grads_turned, outs, logs, key_feat, query_feat, tiles)


def table_kernel(range_ref, tiles_ref, bucket_ref, table_ref):
    index = pl.program_id(0)
    heads = tiles_ref.shape[0]

    @pl.when(index == 0)
    def _():
        table_ref[...] = jnp.zeros_like(table_ref)

    @pl.when((index >= range_ref[0]) & (index < range_ref[1]))
    def _():
        rows = []
        for head in range(heads):
            tile = tiles_ref[head, 0]
            padded = jnp.concatenate([tile, jnp.zeros_like(tile)], axis=1)
            size = TILE // 2
            while size >= 1:
                padded = padded[:size] + pltpu.roll(padded[size:], 2 * TILE - size, 1)
                size //= 2
            rows.append(padded)
        sums = jnp.concatenate(rows, axis=0)
        buckets = lax.broadcasted_iota(jnp.int32, (table_ref.shape[1], 2 * TILE), 0)
        hot = (buckets == bucket_ref[0]).astype(F32)
        table_ref[...] += lax.dot_general(
            sums, hot, (((1,), (1,)), ((), ())), preferred_element_type=F32, precision=HIGHEST
        )


def table_sums(tiles, used, bucket_at, bucket_count):
    heads, tile_count = tiles.shape[:2]

    def held(index, used_ref):
        return jnp.minimum(jnp.maximum(index, used_ref[0]), used_ref[1] - 1)

    return pl.pallas_call(
        table_kernel,
        out_shape=jax.ShapeDtypeStruct((heads, bucket_count), F32),
        grid_spec=pltpu.PrefetchScalarGridSpec(
            num_scalar_prefetch=1,
            grid=(tile_count,),
            in_specs=[
                pl.BlockSpec((heads, 1, TILE, TILE), lambda t, r: (0, held(t, r), 0, 0)),
                pl.BlockSpec((1, 1, 2 * TILE), lambda t, r: (t, 0, 0)),
            ],
            out_specs=pl.BlockSpec((heads, bucket_count), lambda t, r: (0, 0)),
        ),
        cost_estimate=SMALL,
        compiler_params=pltpu.CompilerParams(vmem_limit_bytes=40 << 20),
    )(used, tiles, bucket_at)


def window_kernel(range_ref, key_ref, value_ref, key_weight_ref, value_weight_ref, out_ref):
    index = pl.program_id(0)
    tiles = out_ref.shape[0] // TILE
    needed = ((index + 1) * tiles > range_ref[0]) & (index * tiles < range_ref[1])

    @pl.when(needed)
    def _():
        out_ref[...] = (
            contract(key_ref[...], key_weight_ref[...], 1, 1) + contract(value_ref[...], value_weight_ref[...], 1, 1)
        ).astype(BF16)

    @pl.when(jnp.logical_not(needed))
    def _():
        out_ref[...] = jnp.zeros_like(out_ref)


def window_gradient(grad_keys, grad_values, weights, spots, covered, row_count):
    window, width = grad_keys.shape
    tiles = row_count // TILE

    def rows(index, covered_ref):
        low = lax.div(covered_ref[0], tiles)
        high = lax.div(covered_ref[1] - 1, tiles)
        return jnp.minimum(jnp.maximum(index, low), high), 0

    return pl.pallas_call(
        window_kernel,
        out_shape=jax.ShapeDtypeStruct((window, width), BF16),
        grid_spec=pltpu.PrefetchScalarGridSpec(
            num_scalar_prefetch=1,
            grid=(window // row_count,),
            in_specs=[
                pl.BlockSpec((row_count, width), rows),
                pl.BlockSpec((row_count, width), rows),
                pl.BlockSpec((width, width), lambda k, r: (0, spots[0])),
                pl.BlockSpec((width, width), lambda k, r: (0, spots[1])),
            ],
            out_specs=pl.BlockSpec((row_count, width), lambda k, r: (k, 0)),
        ),
        cost_estimate=SMALL,
        compiler_params=pltpu.CompilerParams(vmem_limit_bytes=40 << 20),
    )(covered, grad_keys, grad_values, weights, weights)


def shifted(value, axis, steps):
    count = lax.axis_size(axis)
    pairs = [(source, source + steps) for source in range(count) if 0 <= source + steps < count]
    return lax.ppermute(value, axis, pairs)


def flat_swap(value, mask):
    count = lax.axis_size("seq") * lax.axis_size("dp")
    return lax.ppermute(value, BOTH, [(source, source ^ mask) for source in range(count)])


def groups_of(low, bits):
    groups = []
    if bits % 2:
        groups.append((low, 1))
        low, bits = low + 1, bits - 1
    while bits:
        groups.append((low, 2))
        low, bits = low + 2, bits - 2
    return groups


def bits_of(count):
    bits = count.bit_length() - 1
    assert count == 1 << bits
    return bits


def all_groups(count):
    return [(0, 1)] + groups_of(1, bits_of(count) - 1)


def tie(*values):
    return lax.optimization_barrier(values)


def swaps(piece, group):
    low, bits = group
    return [flat_swap(piece, step << low) for step in range(1, 1 << bits)]


def swap_masks(masks, group):
    low, bits = group
    return [mask ^ (step << low) for step in range(1, 1 << bits) for mask in masks]


def stack_kernel(*refs):
    target = refs[-1]
    start = 0
    for source in refs[:-1]:
        target[start : start + source.shape[0]] = source[...]
        start += source.shape[0]


def stacked(pieces):
    if len(pieces) == 1:
        return pieces[0]
    count = sum(piece.shape[0] for piece in pieces)
    return pl.pallas_call(
        stack_kernel,
        out_shape=jax.ShapeDtypeStruct((count,) + pieces[0].shape[1:], pieces[0].dtype),
        in_specs=[pl.BlockSpec(memory_space=pltpu.VMEM)] * len(pieces),
        out_specs=pl.BlockSpec(memory_space=pltpu.VMEM),
        cost_estimate=SMALL,
        compiler_params=pltpu.CompilerParams(vmem_limit_bytes=40 << 20),
    )(*pieces)


def units_kernel(rank_ref, gate_ref, up_ref, units_ref, *, dp_count):
    left = lax.broadcasted_iota(jnp.int32, (gate_ref.shape[0], TILE), 1) < TILE // 2
    for side, source in enumerate((gate_ref, up_ref)):
        span = source.shape[1] // dp_count
        for owner in range(dp_count):
            for pair in range(span // TILE):
                halves_of = []
                for odd in range(2):
                    unit = (2 * pair + odd) * dp_count + owner
                    tile = source[:, unit // 2 * TILE : (unit // 2 + 1) * TILE]
                    halves_of.append(tile if unit % 2 == odd else pltpu.roll(tile, TILE // 2, 1))
                start = side * span + pair * TILE
                merged = jnp.where(left, halves_of[0], halves_of[1])
                units_ref[rank_ref[0] ^ owner, :, start : start + TILE] = merged.astype(BF16)


def units_of(gate_weight, up_weight, dp_rank, dp_count, seq_count, unit):
    rows, hidden_width = gate_weight.shape
    share = seq_count * unit
    if unit != TILE // 2 or rows % 8:
        both = jnp.stack([gate_weight.astype(BF16), up_weight.astype(BF16)], axis=1)
        both = both.reshape(rows, 2, seq_count, dp_count, unit)
        taken = [
            lax.dynamic_index_in_dim(both, dp_rank ^ mask, 3, keepdims=False).reshape(rows, 2 * share)
            for mask in range(dp_count)
        ]
        return jnp.stack(taken)
    return pl.pallas_call(
        functools.partial(units_kernel, dp_count=dp_count),
        out_shape=jax.ShapeDtypeStruct((dp_count, rows, 2 * share), BF16),
        in_specs=[pl.BlockSpec(memory_space=pltpu.SMEM)] + [pl.BlockSpec(memory_space=pltpu.VMEM)] * 2,
        out_specs=pl.BlockSpec(memory_space=pltpu.VMEM),
    )(dp_rank[None].astype(jnp.int32), gate_weight, up_weight)


def columns_kernel(rank_ref, *refs, dp_count):
    sources, (gate_ref, up_ref), scratch = refs[:dp_count], refs[dp_count : dp_count + 2], refs[-1]
    for mask in range(dp_count):
        scratch[rank_ref[0] ^ mask] = sources[mask][...].astype(F32)
    left = lax.broadcasted_iota(jnp.int32, (gate_ref.shape[0], TILE), 1) < TILE // 2
    for side, target in enumerate((gate_ref, up_ref)):
        span = target.shape[1] // dp_count
        for tile in range(target.shape[1] // TILE):
            halves_of = []
            for odd in range(2):
                group, owner = divmod(2 * tile + odd, dp_count)
                start = side * span + group // 2 * TILE
                part = scratch[owner, :, start : start + TILE]
                halves_of.append(part if group % 2 == odd else pltpu.roll(part, TILE // 2, 1))
            target[:, tile * TILE : (tile + 1) * TILE] = jnp.where(left, halves_of[0], halves_of[1])


def columns_of(parts, dp_rank, dp_count, seq_count, unit):
    rows = parts[0].shape[0]
    hidden_width = seq_count * dp_count * unit
    if unit != TILE // 2 or rows % 8:
        both = jnp.stack(parts)
        both = jnp.stack(
            [lax.dynamic_index_in_dim(both, dp_rank ^ index, 0, keepdims=False) for index in range(dp_count)], axis=1
        )
        both = both.reshape(rows, dp_count, 2, seq_count, unit).transpose(0, 2, 3, 1, 4)
        both = both.reshape(rows, 2, hidden_width).astype(F32)
        return both[:, 0], both[:, 1]
    return pl.pallas_call(
        functools.partial(columns_kernel, dp_count=dp_count),
        out_shape=(jax.ShapeDtypeStruct((rows, hidden_width), F32),) * 2,
        in_specs=[pl.BlockSpec(memory_space=pltpu.SMEM)] + [pl.BlockSpec(memory_space=pltpu.VMEM)] * dp_count,
        out_specs=(pl.BlockSpec(memory_space=pltpu.VMEM),) * 2,
        scratch_shapes=[pltpu.VMEM((dp_count,) + parts[0].shape, F32)],
        cost_estimate=SMALL,
    )(dp_rank[None].astype(jnp.int32), *parts)


def shard_kernel(*refs):
    target = refs[-1]
    start = 0
    for source in refs[:-1]:
        columns = source.shape[1]
        target[:, start : start + columns] = source[...].astype(BF16)
        start += columns


def side_by_side(arrays):
    columns = sum(array.shape[1] for array in arrays)
    return pl.pallas_call(
        shard_kernel,
        out_shape=jax.ShapeDtypeStruct((arrays[0].shape[0], columns), BF16),
        in_specs=[pl.BlockSpec(memory_space=pltpu.VMEM)] * len(arrays),
        out_specs=pl.BlockSpec(memory_space=pltpu.VMEM),
        cost_estimate=SMALL,
        compiler_params=pltpu.CompilerParams(vmem_limit_bytes=40 << 20),
    )(*arrays)


def norm_kernel(gain_ref, *refs):
    target = refs[-1]
    gain = gain_ref[...].astype(F32).T[:1]
    start = 0
    for source in refs[:-1]:
        rows = source[...].astype(F32)
        scale = lax.rsqrt(jnp.mean(rows * rows, axis=1, keepdims=True) + EPSILON)
        target[start : start + source.shape[0]] = (rows * scale * gain).astype(BF16)
        start += source.shape[0]


def normed_rows_of(pieces, weights, block):
    rows, width = pieces[0].shape
    return pl.pallas_call(
        norm_kernel,
        out_shape=jax.ShapeDtypeStruct((len(pieces) * rows, width), BF16),
        grid=(1,),
        in_specs=[pl.BlockSpec((width, TILE), lambda k: (0, block))]
        + [pl.BlockSpec((rows, width), lambda k: (0, 0))] * len(pieces),
        out_specs=pl.BlockSpec((len(pieces) * rows, width), lambda k: (0, 0)),
        compiler_params=pltpu.CompilerParams(vmem_limit_bytes=40 << 20),
    )(weights, *pieces)


def halves_kernel(rank_ref, *refs):
    sources, table_ref, (kept_ref, sent_ref) = refs[:-3], refs[-3], refs[-2:]
    mine = rank_ref[0] & 1
    for index in range(kept_ref.shape[0]):
        for target, side in ((kept_ref, mine), (sent_ref, 1 - mine)):
            start = 0
            for source in sources:
                target[index, :, start : start + source.shape[2]] = source[2 * index + side]
                start += source.shape[2]
            target[index, :, start:] = table_ref[...]


def core_halves(grads, table_block, rank, count):
    rows = grads[0].shape[0] // count
    columns = sum(grad.shape[1] for grad in grads) + TILE
    if rows % 8:
        held = jnp.concatenate(grads + [jnp.tile(table_block, (count, 1))], axis=1).reshape(-1, 2, rows, columns)
        return [lax.dynamic_index_in_dim(held, (rank & 1) ^ side, 1, keepdims=False) for side in range(2)]
    return pl.pallas_call(
        halves_kernel,
        out_shape=(jax.ShapeDtypeStruct((count // 2, rows, columns), BF16),) * 2,
        in_specs=[pl.BlockSpec(memory_space=pltpu.SMEM)]
        + [pl.BlockSpec(memory_space=pltpu.VMEM)] * (len(grads) + 1),
        out_specs=(pl.BlockSpec(memory_space=pltpu.VMEM),) * 2,
        cost_estimate=SMALL,
        compiler_params=pltpu.CompilerParams(vmem_limit_bytes=40 << 20),
    )(rank[None].astype(jnp.int32), *[grad.reshape(count, rows, -1) for grad in grads], table_block)


def place_kernel(rank_ref, *refs, masks):
    target = refs[-1]
    rank = rank_ref[0]
    for source, part in zip(refs, masks):
        for index, mask in enumerate(part):
            target[rank ^ mask] = source[index]


def placed(held, masks, rank):
    count = sum(len(part) for part in masks)
    shape = held[0].shape[1:]
    return pl.pallas_call(
        functools.partial(place_kernel, masks=masks),
        out_shape=jax.ShapeDtypeStruct((count,) + shape, held[0].dtype),
        in_specs=[pl.BlockSpec(memory_space=pltpu.SMEM)] + [pl.BlockSpec(memory_space=pltpu.VMEM)] * len(held),
        out_specs=pl.BlockSpec(memory_space=pltpu.VMEM),
        cost_estimate=SMALL,
        compiler_params=pltpu.CompilerParams(vmem_limit_bytes=40 << 20),
    )(rank[None].astype(jnp.int32), *held)


def place_far_kernel(rank_ref, *refs, masks, dp_count):
    pair_ref, down_ref = refs[-2:]
    rank = rank_ref[0]
    for source, part in zip(refs, masks):
        for index, mask in enumerate(part):
            owner = rank ^ mask
            for entry in range(dp_count):
                pair_ref[owner ^ entry] = source[index, entry]
            for entry in range(dp_count // 2):
                down_ref[owner // dp_count, entry] = source[index, dp_count + entry]


def place_far(held, masks, rank, dp_count):
    count = sum(len(part) for part in masks)
    shape = held[0].shape[2:]
    dtype = held[0].dtype
    return pl.pallas_call(
        functools.partial(place_far_kernel, masks=masks, dp_count=dp_count),
        out_shape=(
            jax.ShapeDtypeStruct((count * dp_count,) + shape, dtype),
            jax.ShapeDtypeStruct((count, dp_count // 2) + shape, dtype),
        ),
        in_specs=[pl.BlockSpec(memory_space=pltpu.SMEM)] + [pl.BlockSpec(memory_space=pltpu.VMEM)] * len(held),
        out_specs=(pl.BlockSpec(memory_space=pltpu.VMEM), pl.BlockSpec(memory_space=pltpu.VMEM)),
        cost_estimate=SMALL,
        compiler_params=pltpu.CompilerParams(vmem_limit_bytes=40 << 20),
    )(rank[None].astype(jnp.int32), *held)


def split_and_swap(held, mine, group):
    low, bits = group
    held = held.reshape((-1, 1 << bits) + held.shape[1:])
    kept = lax.dynamic_index_in_dim(held, mine, 1, keepdims=False)
    got = [
        flat_swap(lax.dynamic_index_in_dim(held, mine ^ step, 1, keepdims=False), step << low)
        for step in range(1, 1 << bits)
    ]
    return kept, got


def joined(kept, got):
    values = [piece.astype(F32) for piece in [kept] + got]
    while len(values) > 1:
        values = [values[k] + values[k + 1] for k in range(0, len(values), 2)]
    return values[0]


def spread_dp(parts, bits):
    held = {(mask, 0): part for mask, part in parts.items()}
    for bit in range(bits):
        step = 1 << bit
        keys = sorted(key for key in held if key[0] & step)
        sent = flat_swap(jnp.stack([held[key] for key in keys]), step)
        held = {key: part for key, part in held.items() if not key[0] & step}
        held.update({(goal ^ step, source ^ step): sent[k] for k, (goal, source) in enumerate(keys)})
    return [held[(0, mask)] for mask in range(1 << bits)]


def gather_dp(value, bits):
    held = {0: value}
    for bit in range(bits - 1, -1, -1):
        held.update({mask ^ (1 << bit): flat_swap(piece, 1 << bit) for mask, piece in list(held.items())})
    return [held[mask] for mask in range(1 << bits)]


def scatter_dp(parts, bits):
    held = dict(enumerate(parts))
    for bit in range(bits):
        step = 1 << bit
        held = {
            mask: piece.astype(F32) + flat_swap(held[mask ^ step].astype(BF16), step).astype(F32)
            for mask, piece in held.items()
            if not mask & step
        }
    return held[0]


def parts_of(value, parts, to_rows):
    rows = value.shape[0] // parts
    columns = rows * value.shape[1] // to_rows
    if rows % 8 or to_rows % 8 or value.shape[1] % TILE or columns % TILE:
        return value.reshape(parts * to_rows, columns)
    tiles = value.reshape(parts, rows // 8, 8, value.shape[1] // TILE, TILE).transpose(0, 1, 3, 2, 4)
    tiles = tiles.reshape(parts, to_rows // 8, columns // TILE, 8, TILE).transpose(0, 1, 3, 2, 4)
    return tiles.reshape(parts * to_rows, columns)


def contract(left_side, right_side, left_dim, right_dim):
    return lax.dot_general(
        left_side, right_side, (((left_dim,), (right_dim,)), ((), ())), preferred_element_type=F32
    )


def gelu_pair(v):
    scale = 0.7978845608028654
    bent = jnp.tanh(scale * (v + 0.044715 * v * v * v))
    value = 0.5 * v * (1.0 + bent)
    slope = 0.5 * (1.0 + bent) + 0.5 * v * (1.0 - bent * bent) * scale * (1.0 + 3.0 * 0.044715 * v * v)
    return value, slope


def body(
    blocks,
    lengths,
    bucket_table,
    first_gain,
    query_weight,
    key_weight,
    value_weight,
    output_weight,
    table_weight,
    second_gain,
    gate_weight,
    up_weight,
    down_weight,
    cotangent,
):
    seq_count = lax.axis_size("seq")
    device_count = seq_count * lax.axis_size("dp")
    seq_rank = lax.axis_index("seq")
    row_count, width = blocks.shape[1:]
    pack_rows = row_count * seq_count
    bucket_count, heads = table_weight.shape
    head_dim = width // heads
    seq_total = lengths.shape[1]
    max_length = (bucket_table.shape[0] + 1) // 2
    shard_rows = query_weight.shape[0]
    hidden_width = gate_weight.shape[1]
    reach = min((max_length - 1 + row_count - 1) // row_count, seq_count - 1)
    query_blocks = row_count // TILE
    window = (2 * reach + 1) * row_count
    window_blocks = window // TILE
    tile_count = window_blocks + query_blocks - 1
    center = reach * query_blocks + query_blocks - 1
    pairs = 2 if window <= 2304 else 1

    dp_count = lax.axis_size("dp")
    dp_rank = lax.axis_index("dp")
    dp_bits = bits_of(dp_count)
    rank = seq_rank * dp_count + dp_rank
    groups = all_groups(device_count)
    seq_groups = groups_of(dp_bits, bits_of(seq_count))
    own = blocks[0]

    gains = jnp.pad(jnp.stack([first_gain, second_gain], axis=1), ((0, 0), (0, TILE - 2)))
    near_shard = side_by_side([query_weight, key_weight, value_weight, output_weight, gains])

    unit = down_weight.shape[0]
    share = seq_count * unit
    pair_units = units_of(gate_weight, up_weight, dp_rank, dp_count, seq_count, unit)

    line_width = (tile_count + 1) * TILE
    ahead = (tile_count - center) * TILE - (max_length - 1)
    behind = line_width - ahead - bucket_table.shape[0]
    bucket_line = jnp.pad(bucket_table[::-1], (max(ahead, 0), max(behind, 0)), mode="edge")
    bucket_line = bucket_line[max(-ahead, 0) : max(-ahead, 0) + line_width]
    bucket_ids = jnp.arange(bucket_count, dtype=jnp.int32)
    line_hot = (bucket_line[None, :] == bucket_ids[:, None]).astype(F32)
    lines = lax.dot_general(table_weight, line_hot, (((0,), (0,)), ((), ())), precision=HIGHEST)

    order = groups[::-1]
    near_shard = near_shard[None]
    masks = [0]
    around = {0: own}
    near_held = near_shard
    stages = len(order)
    for stage, group in enumerate(order):
        got = swaps(near_held, group)
        last = stage == stages - 1
        moves = [step for step in range(1, reach + 1) if step == stage + 1 or (last and step > stage)]
        arrived = {}
        for step in moves:
            arrived[step] = shifted(own, "seq", step)
            arrived[-step] = shifted(own, "seq", -step)
        got_masks = swap_masks(masks, group)
        if last:
            held, masks = [near_held] + got, [masks] + [
                got_masks[k * len(masks) : (k + 1) * len(masks)] for k in range(len(got))
            ]
        else:
            if stage == 0:
                lines = tie(lines, got[0])[0]
            if stage == 1:
                tiles = bias_tiles(lines, tile_count)
                near_held, got, arrived, tiles = tie(near_held, got, arrived, tiles)
            else:
                near_held, got, arrived = tie(near_held, got, arrived)
            near_held = stacked([near_held] + got)
            masks = masks + got_masks
        around.update(arrived)
    near_full = placed(held, masks, rank)
    near_full = near_full.reshape(device_count * shard_rows, 4 * width + TILE)
    weight_query = near_full[:, :width]
    weight_key = near_full[:, width : 2 * width]
    weight_value = near_full[:, 2 * width : 3 * width]
    weight_output = near_full[:, 3 * width : 4 * width]
    gain_columns = near_full[:, 4 * width :]

    pair_parts = spread_dp({mask: pair_units[mask] for mask in range(dp_count)}, dp_bits)
    down_parts = parts_of(down_weight.astype(BF16), 1, shard_rows * dp_count // 2)
    down_parts = down_parts.reshape(dp_count // 2, shard_rows, 2 * share)
    far_shard = stacked([part[None] for part in pair_parts] + [down_parts])
    far_shard = tie(far_shard, around)[0][None]
    far_order = seq_groups[::-1]
    far_first = swaps(far_shard, far_order[0])
    far_own = [piece for group in far_order[1:2] for piece in swaps(far_shard, group)]
    gain_one = gain_columns[:, 0].astype(F32)[None, :]
    gain_two = gain_columns[:, 1].astype(F32)[None, :]

    seq_ends = jnp.cumsum(lengths[0], dtype=jnp.int32)
    query_first = seq_rank * row_count
    window_first = query_first - reach * row_count

    def segments(at):
        return jnp.sum((at[:, None] >= seq_ends[None, :]).astype(jnp.int32), axis=1, dtype=jnp.int32)

    query_places = query_first + jnp.arange(row_count, dtype=jnp.int32)
    key_places = window_first + jnp.arange(window, dtype=jnp.int32)
    query_seg = segments(query_places)
    key_seg = jnp.where((key_places >= 0) & (key_places < pack_rows), segments(key_places), -1)
    lanes = jnp.arange(TILE, dtype=jnp.int32)
    key_feat = jnp.where(
        (key_seg[:, None] != lanes[None, :]) & (lanes[None, :] <= seq_total), BIG, 0.0
    ).astype(BF16)
    query_feat = (lanes[:, None] == query_seg[None, :]).astype(BF16)
    valid_rows = (query_seg < seq_total).astype(F32)
    seq_starts = jnp.concatenate([jnp.zeros((1,), jnp.int32), seq_ends])
    seq_stops = jnp.concatenate([seq_ends, jnp.full((1,), pack_rows, jnp.int32)])
    seq_ids = jnp.arange(seq_total + 1, dtype=jnp.int32)
    low_seg = query_seg[::TILE]
    high_seg = query_seg[TILE - 1 :: TILE]
    low = jnp.sum(jnp.where(low_seg[:, None] == seq_ids[None, :], seq_starts[None, :], 0), axis=1)
    high = jnp.sum(jnp.where(high_seg[:, None] == seq_ids[None, :], seq_stops[None, :], 0), axis=1)
    first = (low - window_first) // TILE
    last = (high - window_first + TILE - 1) // TILE
    steps = (last - first + STEP - 1) // STEP
    first = jnp.minimum(first, window_blocks - steps * STEP).astype(jnp.int32)
    steps = steps.astype(jnp.int32)


    window_normed = normed_rows_of(
        [around[-step] for step in range(-reach, reach + 1)], near_full, 4 * width // TILE
    )
    own_slice = slice(reach * row_count, (reach + 1) * row_count)
    tokens = own.astype(F32)
    scale_one = lax.rsqrt(jnp.mean(tokens * tokens, axis=1, keepdims=True) + EPSILON)
    normed_own = window_normed[own_slice]
    keys = contract(window_normed, weight_key, 1, 0).astype(BF16)
    values_turned = contract(weight_value, window_normed, 0, 1).astype(BF16)
    queries_turned = contract(weight_query, normed_own, 0, 1).astype(BF16)
    outs, logs = attend(
        first, steps, queries_turned, keys, values_turned, key_feat, query_feat, tiles, head_dim, pairs
    )
    far_first = stacked(tie(far_first, outs)[0])
    first_masks = swap_masks([0], far_order[0])
    far_held, far_masks = [far_shard, far_first], [[0], first_masks]
    for number, group in enumerate(far_order[1:]):
        got, got_masks = [], []
        for piece, part in zip(far_held, far_masks):
            more = far_own if piece is far_shard and number == 0 else swaps(piece, group)
            extra = swap_masks(part, group)
            got += more
            got_masks += [extra[k * len(part) : (k + 1) * len(part)] for k in range(len(more))]
        far_held, far_masks = far_held + got, far_masks + got_masks
    far_full = place_far(far_held, far_masks, rank, dp_count)
    weight_pair = far_full[0].reshape(device_count * shard_rows, 2 * share)
    weight_down = parts_of(far_full[1].reshape(-1, 2 * share), seq_count, unit)
    attended = (outs * valid_rows[None, :]).astype(BF16)
    middle = tokens + contract(attended, weight_output, 0, 0)

    scale_two = lax.rsqrt(jnp.mean(middle * middle, axis=1, keepdims=True) + EPSILON)
    second = middle * scale_two
    second_low = (second * gain_two).astype(BF16)
    every_second = jnp.concatenate(gather_dp(second_low, dp_bits), axis=0)
    every_grad = jnp.concatenate(gather_dp(cotangent[0], dp_bits), axis=0)
    both_ways = contract(every_second, weight_pair, 1, 0)
    gate_values, upward = both_ways[:, :share], both_ways[:, share:]
    active, slope = gelu_pair(gate_values)
    hidden = (active * upward).astype(BF16)
    grad_hidden = contract(every_grad, weight_down, 1, 1)
    grad_pair = jnp.concatenate(
        [(grad_hidden * upward * slope).astype(BF16), (grad_hidden * active).astype(BF16)], axis=1
    )
    every_back = contract(grad_pair, weight_pair, 1, 1).astype(BF16)
    grad_second = scatter_dp(jnp.split(every_back, dp_count, axis=0), dp_bits)
    grad_out = cotangent[0]
    scaled = grad_second * gain_two
    grad_middle = grad_out.astype(F32) + scale_two * (
        scaled - second * jnp.mean(scaled * second, axis=1, keepdims=True)
    )
    grad_branch = grad_middle.astype(BF16)
    grad_mixed = (contract(grad_branch, weight_output, 1, 1).astype(BF16).astype(F32) * valid_rows[:, None]).astype(BF16)
    grad_mixed_turned = (
        contract(weight_output, grad_branch, 1, 1).astype(BF16).astype(F32) * valid_rows[None, :]
    ).astype(BF16)
    grad_output_weight = contract(attended, grad_branch, 1, 0).astype(BF16)
    grad_down = contract(hidden, every_grad, 0, 0).astype(BF16)
    grad_down = parts_of(grad_down, seq_count, shard_rows * dp_count // 2)
    grad_pair_weight = contract(every_second, grad_pair, 0, 0).astype(BF16)
    far_grads = jnp.concatenate(
        [
            grad_pair_weight.reshape(seq_count, dp_count, shard_rows, 2 * share),
            grad_down.reshape(seq_count, dp_count // 2, shard_rows, 2 * share),
        ],
        axis=1,
    )
    every_out = contract(hidden, weight_down, 1, 0).astype(BF16)
    far_grads, grad_mixed, grad_mixed_turned, grad_output_weight, every_out = tie(
        far_grads, grad_mixed, grad_mixed_turned, grad_output_weight, every_out
    )
    out_parts = jnp.split(every_out, dp_count, axis=0)
    bits = seq_groups[0][1]
    far_kept, far_got = split_and_swap(far_grads, seq_rank & ((1 << bits) - 1), seq_groups[0])

    queries = contract(normed_own, weight_query, 1, 0).astype(BF16)
    keys_turned = contract(weight_key, window_normed, 0, 1).astype(BF16)
    values = contract(window_normed, weight_value, 1, 0).astype(BF16)
    grad_queries, grad_keys, grad_values, tile_sums = attend_back(
        first, steps, queries, queries_turned, keys, keys_turned, values, grad_mixed, grad_mixed_turned,
        outs, logs, key_feat, query_feat, tiles, head_dim, pairs,
    )
    out_parts = [out_parts[0]] + [flat_swap(out_parts[mask], mask) for mask in range(1, dp_count)]
    grad_queries, out_parts = tie(grad_queries, out_parts)
    output = middle + sum(part.astype(F32) for part in out_parts)
    grad_queries, grad_keys, grad_values, tile_sums, far_kept, far_got = tie(
        grad_queries, grad_keys, grad_values, tile_sums, far_kept, far_got
    )
    for low, bits in seq_groups[1:]:
        far_held = joined(far_kept, far_got).astype(BF16)
        far_kept, far_got = split_and_swap(far_held, (rank >> low) & ((1 << bits) - 1), (low, bits))
    covered = jnp.stack([jnp.min(first), jnp.max(first + steps * STEP)])
    partial_low = window_gradient(grad_keys, grad_values, near_full, (1, 2), covered, row_count)

    def returned_from(low_rows, step):
        parts = []
        for turn in (step, -step):
            part = low_rows[(reach + turn) * row_count : (reach + turn + 1) * row_count]
            parts.append(shifted(part, "seq", turn))
        return parts

    returned = returned_from(partial_low, 1)
    if reach > 2:
        returned = returned + returned_from(partial_low, reach - 1)
    grad_query_weight = contract(normed_own, grad_queries, 0, 1).astype(BF16)
    grad_key_weight = contract(window_normed, grad_keys, 0, 0).astype(BF16)
    grad_value_weight = contract(window_normed, grad_values, 0, 0).astype(BF16)

    tile_first = first - jnp.arange(query_blocks, dtype=jnp.int32) + (query_blocks - 1)
    used = jnp.stack([jnp.min(tile_first), jnp.max(tile_first + steps * STEP)])
    flipped = bucket_line.reshape(tile_count + 1, TILE)[::-1]
    bucket_at = jnp.concatenate([flipped[:-1], flipped[1:]], axis=1)[:, None, :]
    grad_table = table_sums(tile_sums, used, bucket_at, bucket_count).T
    table_rows = -(-grad_table.size // TILE)
    table_block = jnp.pad(grad_table.reshape(-1), (0, table_rows * TILE - grad_table.size)).reshape(table_rows, TILE)
    table_block = jnp.pad(table_block, ((0, shard_rows - table_rows), (0, 0))).astype(BF16)
    kept, sent = core_halves(
        [grad_query_weight, grad_key_weight, grad_value_weight, grad_output_weight], table_block, rank, device_count
    )
    kept, sent, partial_low, returned, far_kept, far_got = tie(kept, sent, partial_low, returned, far_kept, far_got)
    far_sum = joined(far_kept, far_got).reshape(far_grads.shape[1:]).astype(BF16)

    left = [step for step in range(reach, 2, -1) if step != reach - 1]
    waiting = returned_from(partial_low, 2) if reach == 2 or reach > 3 else []
    for stage, (low, bits) in enumerate(groups):
        if stage == 0:
            got = [flat_swap(sent, 1)]
        else:
            kept, got = split_and_swap(near_held, (rank >> low) & ((1 << bits) - 1), (low, bits))
        if stage == 0:
            kept, got, partial_low = tie(kept, got, partial_low)
        else:
            arrived = returned_from(partial_low, left.pop(0)) if left else []
            kept, got, arrived, waiting, partial_low, far_sum = tie(
                kept, got, arrived, waiting, partial_low, far_sum
            )
            if stage == 1:
                pair_back = spread_dp(
                    {mask: lax.dynamic_index_in_dim(far_sum, dp_rank ^ mask, 0, keepdims=False) for mask in range(dp_count)},
                    dp_bits,
                )
            if stage == 2:
                kept, pair_back = tie(kept, pair_back)
            returned, waiting = returned + arrived + waiting, []
        total = joined(kept, got)
        near_held = total.astype(BF16)
    for step in left:
        returned = returned + returned_from(partial_low, step)
    near_sum = total.reshape(shard_rows, 4 * width + TILE)
    grad_normed = partial_low[own_slice].astype(F32) + contract(grad_queries, weight_query, 0, 1)
    grad_normed = grad_normed + sum(piece.astype(F32) for piece in returned)
    grad_gate_own, grad_up_own = columns_of(pair_back, dp_rank, dp_count, seq_count, unit)
    grad_down_own = parts_of(far_sum[dp_count:].astype(F32).reshape(-1, 2 * share), 1, unit)
    normed_rows = tokens * scale_one
    scaled_one = grad_normed * gain_one
    grad_blocks = grad_middle + scale_one * (
        scaled_one - normed_rows * jnp.mean(scaled_one * normed_rows, axis=1, keepdims=True)
    )

    grad_table = near_sum[:table_rows, 4 * width :].reshape(-1)[: table_weight.size].reshape(table_weight.shape)

    def gain_grad(gain, weights, grads):
        total = sum(jnp.sum(weight.astype(BF16).astype(F32) * grad, axis=1) for weight, grad in zip(weights, grads))
        return total / gain.astype(BF16).astype(F32)

    near_parts = [near_sum[:, k * width : (k + 1) * width] for k in range(4)]
    grad_gain_one = gain_grad(first_gain, (query_weight, key_weight, value_weight), near_parts[:3])
    grad_gain_two = gain_grad(second_gain, (gate_weight, up_weight), (grad_gate_own, grad_up_own))
    return (
        output.astype(BF16)[None],
        grad_blocks[None],
        grad_gain_one,
        near_parts[0],
        near_parts[1],
        near_parts[2],
        near_parts[3],
        grad_table,
        grad_gain_two,
        grad_gate_own,
        grad_up_own,
        grad_down_own,
    )


def solution(mesh):
    return jax.shard_map(
        body,
        mesh=mesh,
        in_specs=(
            P("dp", "seq", None),
            P("dp", None),
            P(),
            P(("seq", "dp")),
            P(("seq", "dp"), None),
            P(("seq", "dp"), None),
            P(("seq", "dp"), None),
            P(("seq", "dp"), None),
            P(),
            P(("seq", "dp")),
            P(("seq", "dp"), None),
            P(("seq", "dp"), None),
            P(("seq", "dp"), None),
            P("dp", "seq", None),
        ),
        out_specs=(
            P("dp", "seq", None),
            P("dp", "seq", None),
            P(("seq", "dp")),
            P(("seq", "dp"), None),
            P(("seq", "dp"), None),
            P(("seq", "dp"), None),
            P(("seq", "dp"), None),
            P(),
            P(("seq", "dp")),
            P(("seq", "dp"), None),
            P(("seq", "dp"), None),
            P(("seq", "dp"), None),
        ),
        check_vma=False,
    )
```

```python
import functools

import jax
import jax.numpy as jnp
from jax import lax
from jax.experimental import pallas as pl
from jax.experimental.pallas import tpu as pltpu
from jax.sharding import PartitionSpec as P

EPSILON = 1e-06
BIG = -1e30
HIGHEST = lax.Precision.HIGHEST
BOTH = ("seq", "dp")
SMALL = pl.CostEstimate(flops=1, bytes_accessed=1, transcendentals=0)
TILE = 128
STEP = 4
SPAN = STEP * TILE
F32 = jnp.float32
BF16 = jnp.bfloat16
LOWEST = -3.0e38


def bias_of(tiles_ref, pair, tile):
    halves_of = [tiles_ref[2 * pair + side, pl.ds(tile, STEP)].reshape(SPAN, TILE) for side in range(2)]
    return jnp.concatenate(halves_of, axis=1)


def dot(a, b):
    return jnp.dot(a, b, preferred_element_type=F32)


def tiles_kernel(line_ref, tiles_ref):
    tile_count = tiles_ref.shape[1]
    for index in range(tile_count):
        window = line_ref[0, :, pl.ds((tile_count - 1 - index) * TILE, 2 * TILE)]
        spread = jnp.broadcast_to(window, (TILE, 2 * TILE))
        rolled = pltpu.roll(spread, 0, 1, stride=1, stride_axis=0)
        tiles_ref[0, index] = rolled[:, TILE:]


def bias_tiles(lines, tile_count):
    heads, width = lines.shape
    return pl.pallas_call(
        tiles_kernel,
        out_shape=jax.ShapeDtypeStruct((heads, tile_count, TILE, TILE), F32),
        grid=(heads,),
        in_specs=[pl.BlockSpec((1, 1, width), lambda h: (h, 0, 0))],
        out_specs=pl.BlockSpec((1, tile_count, TILE, TILE), lambda h: (h, 0, 0, 0)),
        cost_estimate=SMALL,
    )(lines.reshape(heads, 1, width))


def halves(pair, head_dim):
    top = lax.broadcasted_iota(jnp.int32, pair.shape, 0) < head_dim
    zero = jnp.zeros_like(pair)
    return jnp.concatenate([jnp.where(top, pair, zero), jnp.where(top, zero, pair)], axis=1)


def halves_rows(pair, head_dim):
    left = lax.broadcasted_iota(jnp.int32, pair.shape, 1) < head_dim
    zero = jnp.zeros_like(pair)
    return jnp.concatenate([jnp.where(left, pair, zero), jnp.where(left, zero, pair)], axis=0)


def merge_halves(both, head_dim):
    top = lax.broadcasted_iota(jnp.int32, (both.shape[0], TILE), 0) < head_dim
    return jnp.where(top, both[:, :TILE], both[:, TILE:])


def fold(values, op):
    return op(values.reshape(values.shape[0] // 8, 8, values.shape[1]), axis=0)


def cols(pair):
    return slice(pair * TILE, (pair + 1) * TILE)


def wide(pair):
    return slice(pair * 2 * TILE, (pair + 1) * 2 * TILE)


def query_side(query_ref, query_feat_ref, block, pair, head_dim):
    rows = slice(block * TILE, (block + 1) * TILE)
    turned = query_ref[cols(pair), rows]
    feat = query_feat_ref[:, rows]
    return jnp.concatenate([halves(turned, head_dim), jnp.concatenate([feat, feat], axis=1)], axis=0)


def forward_kernel(
    first_ref, last_ref, query_ref, key_ref, value_turned_ref, key_feat_ref, query_feat_ref, tiles_ref,
    out_ref, log_ref, score_ref, total_ref, *, pairs, blocks, head_dim,
):
    for block in range(blocks):
        rows = slice(block * TILE, (block + 1) * TILE)
        first, last = first_ref[block], last_ref[block]
        query_sides = [query_side(query_ref, query_feat_ref, block, pair, head_dim) for pair in range(pairs)]

        def score_step(index, highest):
            start = pl.multiple_of((first + index * STEP) * TILE, TILE)
            feat = key_feat_ref[pl.ds(start, SPAN), :]
            tile = first + index * STEP - block + (blocks - 1)
            result = []
            for pair in range(pairs):
                left = jnp.concatenate([key_ref[pl.ds(start, SPAN), cols(pair)], feat], axis=1)
                bias = bias_of(tiles_ref, pair, tile)
                scores = dot(left, query_sides[pair]) + bias
                score_ref[pl.ds(start, SPAN), wide(pair)] = scores
                result.append(jnp.maximum(highest[pair], fold(scores, jnp.max)))
            return tuple(result)

        start_max = tuple(jnp.full((8, 2 * TILE), LOWEST, F32) for _ in range(pairs))
        highest = lax.fori_loop(0, last, score_step, start_max)
        peak = [jnp.max(value, axis=0, keepdims=True) for value in highest]
        total_ref[...] = jnp.zeros_like(total_ref)

        def value_step(index, sums):
            start = pl.multiple_of((first + index * STEP) * TILE, TILE)
            result = []
            for pair in range(pairs):
                weights = jnp.exp(score_ref[pl.ds(start, SPAN), wide(pair)] - peak[pair])
                result.append(sums[pair] + fold(weights, jnp.sum))
                total_ref[:, wide(pair)] += dot(
                    value_turned_ref[cols(pair), pl.ds(start, SPAN)], weights.astype(BF16)
                )
            return tuple(result)

        start_sum = tuple(jnp.zeros((8, 2 * TILE), F32) for _ in range(pairs))
        sums = lax.fori_loop(0, last, value_step, start_sum)
        for pair in range(pairs):
            denominator = jnp.sum(sums[pair], axis=0, keepdims=True)
            out_ref[cols(pair), rows] = merge_halves(total_ref[:, wide(pair)] / denominator, head_dim)
            log_ref[0, block * pairs + pair : block * pairs + pair + 1, :] = peak[pair] + jnp.log(denominator)


def attend(first, last, queries, keys, values_turned, key_feat, query_feat, tiles, head_dim, pairs):
    width, row_count = queries.shape
    window = keys.shape[0]
    blocks = row_count // TILE
    groups = width // (pairs * TILE)
    tile_count = tiles.shape[1]
    kernel = functools.partial(
        forward_kernel, pairs=pairs, blocks=blocks, head_dim=head_dim
    )
    work = row_count * 1280 * width
    return pl.pallas_call(
        kernel,
        out_shape=(
            jax.ShapeDtypeStruct((width, row_count), F32),
            jax.ShapeDtypeStruct((groups, blocks * pairs, 2 * TILE), F32),
        ),
        grid_spec=pltpu.PrefetchScalarGridSpec(
            num_scalar_prefetch=2,
            grid=(groups,),
            in_specs=[
                pl.BlockSpec((pairs * TILE, row_count), lambda g, a, b: (g, 0)),
                pl.BlockSpec((window, pairs * TILE), lambda g, a, b: (0, g)),
                pl.BlockSpec((pairs * TILE, window), lambda g, a, b: (g, 0)),
                pl.BlockSpec((window, TILE), lambda g, a, b: (0, 0)),
                pl.BlockSpec((TILE, row_count), lambda g, a, b: (0, 0)),
                pl.BlockSpec((2 * pairs, tile_count, TILE, TILE), lambda g, a, b: (g, 0, 0, 0)),
            ],
            out_specs=[
                pl.BlockSpec((pairs * TILE, row_count), lambda g, a, b: (g, 0)),
                pl.BlockSpec((1, blocks * pairs, 2 * TILE), lambda g, a, b: (g, 0, 0)),
            ],
            scratch_shapes=[
                pltpu.VMEM((window, pairs * 2 * TILE), F32),
                pltpu.VMEM((TILE, pairs * 2 * TILE), F32),
            ],
        ),
        compiler_params=pltpu.CompilerParams(vmem_limit_bytes=50 << 20),
        cost_estimate=pl.CostEstimate(flops=16 * work, bytes_accessed=24 << 20, transcendentals=row_count * 1280 * 12),
    )(first, last, queries, keys, values_turned, key_feat, query_feat, tiles)


def backward_kernel(
    first_ref, last_ref, query_ref, query_turned_ref, key_ref, key_turned_ref, value_ref, grad_ref, grad_turned_ref, out_ref, log_ref,
    key_feat_ref, query_feat_ref, tiles_ref,
    grad_query_ref, grad_key_ref, grad_value_ref, tile_total,
    key_total, value_total, query_total, *, pairs, blocks, head_dim,
):
    key_total[...] = jnp.zeros_like(key_total)
    value_total[...] = jnp.zeros_like(value_total)
    tile_total[...] = jnp.zeros_like(tile_total)
    for block in range(blocks):
        rows = slice(block * TILE, (block + 1) * TILE)
        first, last = first_ref[block], last_ref[block]
        query_sides, grad_sides, query_stacks, grad_stacks, logs, deltas = [], [], [], [], [], []
        for pair in range(pairs):
            query_sides.append(query_side(query_turned_ref, query_feat_ref, block, pair, head_dim))
            grad_pair = grad_ref[rows, cols(pair)]
            grad_turned = grad_turned_ref[cols(pair), rows]
            grad_sides.append(halves(grad_turned, head_dim))
            query_stacks.append(halves_rows(query_ref[rows, cols(pair)], head_dim))
            grad_stacks.append(halves_rows(grad_pair, head_dim))
            logs.append(log_ref[0, block * pairs + pair : block * pairs + pair + 1, :])
            both = halves(grad_turned.astype(F32) * out_ref[cols(pair), rows], head_dim)
            deltas.append(jnp.sum(both, axis=0, keepdims=True))
        query_total[...] = jnp.zeros_like(query_total)

        def step(index, carry):
            start = pl.multiple_of((first + index * STEP) * TILE, TILE)
            span = pl.ds(start, SPAN)
            feat = key_feat_ref[span, :]
            tile = first + index * STEP - block + (blocks - 1)
            for pair in range(pairs):
                left = jnp.concatenate([key_ref[span, cols(pair)], feat], axis=1)
                bias = bias_of(tiles_ref, pair, tile)
                weights = jnp.exp(dot(left, query_sides[pair]) + bias - logs[pair])
                grad_weights = dot(value_ref[span, cols(pair)], grad_sides[pair])
                grad_scores = weights * (grad_weights - deltas[pair])
                tile_total[2 * pair, pl.ds(tile, STEP)] += grad_scores[:, :TILE].reshape(STEP, TILE, TILE)
                tile_total[2 * pair + 1, pl.ds(tile, STEP)] += grad_scores[:, TILE:].reshape(STEP, TILE, TILE)
                scores_low = grad_scores.astype(BF16)
                value_total[span, cols(pair)] += dot(weights.astype(BF16), grad_stacks[pair])
                key_total[span, cols(pair)] += dot(scores_low, query_stacks[pair])
                query_total[:, wide(pair)] += dot(key_turned_ref[cols(pair), span], scores_low)
            return carry

        lax.fori_loop(0, last, step, 0)
        for pair in range(pairs):
            grad_query_ref[cols(pair), rows] = merge_halves(query_total[:, wide(pair)], head_dim).astype(BF16)
    grad_key_ref[...] = key_total[...].astype(BF16)
    grad_value_ref[...] = value_total[...].astype(BF16)


def attend_back(first, last, queries, queries_turned, keys, keys_turned, values, grads, grads_turned, outs, logs, key_feat, query_feat, tiles, head_dim, pairs):
    row_count, width = queries.shape
    window = keys.shape[0]
    blocks = row_count // TILE
    groups = width // (pairs * TILE)
    heads, tile_count = tiles.shape[:2]
    kernel = functools.partial(backward_kernel, pairs=pairs, blocks=blocks, head_dim=head_dim)
    rows_spec = pl.BlockSpec((row_count, pairs * TILE), lambda g, a, b: (0, g))
    turned_spec = pl.BlockSpec((pairs * TILE, row_count), lambda g, a, b: (g, 0))
    window_spec = pl.BlockSpec((window, pairs * TILE), lambda g, a, b: (0, g))
    work = row_count * 1280 * width
    return pl.pallas_call(
        kernel,
        out_shape=(
            jax.ShapeDtypeStruct((width, row_count), BF16),
            jax.ShapeDtypeStruct((window, width), BF16),
            jax.ShapeDtypeStruct((window, width), BF16),
            jax.ShapeDtypeStruct((heads, tile_count, TILE, TILE), F32),
        ),
        grid_spec=pltpu.PrefetchScalarGridSpec(
            num_scalar_prefetch=2,
            grid=(groups,),
            in_specs=[
                rows_spec,
                turned_spec,
                window_spec,
                pl.BlockSpec((pairs * TILE, window), lambda g, a, b: (g, 0)),
                window_spec,
                rows_spec,
                turned_spec,
                turned_spec,
                pl.BlockSpec((1, blocks * pairs, 2 * TILE), lambda g, a, b: (g, 0, 0)),
                pl.BlockSpec((window, TILE), lambda g, a, b: (0, 0)),
                pl.BlockSpec((TILE, row_count), lambda g, a, b: (0, 0)),
                pl.BlockSpec((2 * pairs, tile_count, TILE, TILE), lambda g, a, b: (g, 0, 0, 0)),
            ],
            out_specs=[
                turned_spec,
                window_spec,
                window_spec,
                pl.BlockSpec((2 * pairs, tile_count, TILE, TILE), lambda g, a, b: (g, 0, 0, 0)),
            ],
            scratch_shapes=[
                pltpu.VMEM((window, pairs * TILE), F32),
                pltpu.VMEM((window, pairs * TILE), F32),
                pltpu.VMEM((TILE, pairs * 2 * TILE), F32),
            ],
        ),
        input_output_aliases={13: 3},
        compiler_params=pltpu.CompilerParams(vmem_limit_bytes=56 << 20),
        cost_estimate=pl.CostEstimate(flops=40 * work, bytes_accessed=32 << 20, transcendentals=row_count * 1280 * 12),
    )(first, last, queries, queries_turned, keys, keys_turned, values, grads, grads_turned, outs, logs, key_feat, query_feat, tiles)


def table_kernel(range_ref, tiles_ref, bucket_ref, table_ref):
    index = pl.program_id(0)
    heads = tiles_ref.shape[0]

    @pl.when(index == 0)
    def _():
        table_ref[...] = jnp.zeros_like(table_ref)

    @pl.when((index >= range_ref[0]) & (index < range_ref[1]))
    def _():
        rows = []
        for head in range(heads):
            tile = tiles_ref[head, 0]
            padded = jnp.concatenate([tile, jnp.zeros_like(tile)], axis=1)
            size = TILE // 2
            while size >= 1:
                padded = padded[:size] + pltpu.roll(padded[size:], 2 * TILE - size, 1)
                size //= 2
            rows.append(padded)
        sums = jnp.concatenate(rows, axis=0)
        buckets = lax.broadcasted_iota(jnp.int32, (table_ref.shape[1], 2 * TILE), 0)
        hot = (buckets == bucket_ref[0]).astype(F32)
        table_ref[...] += lax.dot_general(
            sums, hot, (((1,), (1,)), ((), ())), preferred_element_type=F32, precision=HIGHEST
        )


def table_sums(tiles, used, bucket_at, bucket_count):
    heads, tile_count = tiles.shape[:2]

    def held(index, used_ref):
        return jnp.minimum(jnp.maximum(index, used_ref[0]), used_ref[1] - 1)

    return pl.pallas_call(
        table_kernel,
        out_shape=jax.ShapeDtypeStruct((heads, bucket_count), F32),
        grid_spec=pltpu.PrefetchScalarGridSpec(
            num_scalar_prefetch=1,
            grid=(tile_count,),
            in_specs=[
                pl.BlockSpec((heads, 1, TILE, TILE), lambda t, r: (0, held(t, r), 0, 0)),
                pl.BlockSpec((1, 1, 2 * TILE), lambda t, r: (t, 0, 0)),
            ],
            out_specs=pl.BlockSpec((heads, bucket_count), lambda t, r: (0, 0)),
        ),
        cost_estimate=SMALL,
        compiler_params=pltpu.CompilerParams(vmem_limit_bytes=40 << 20),
    )(used, tiles, bucket_at)


def window_kernel(range_ref, key_ref, value_ref, key_weight_ref, value_weight_ref, out_ref):
    index = pl.program_id(0)
    tiles = out_ref.shape[0] // TILE
    needed = ((index + 1) * tiles > range_ref[0]) & (index * tiles < range_ref[1])

    @pl.when(needed)
    def _():
        out_ref[...] = (
            contract(key_ref[...], key_weight_ref[...], 1, 1) + contract(value_ref[...], value_weight_ref[...], 1, 1)
        ).astype(BF16)

    @pl.when(jnp.logical_not(needed))
    def _():
        out_ref[...] = jnp.zeros_like(out_ref)


def window_gradient(grad_keys, grad_values, weights, spots, covered, row_count):
    window, width = grad_keys.shape
    tiles = row_count // TILE

    def rows(index, covered_ref):
        low = lax.div(covered_ref[0], tiles)
        high = lax.div(covered_ref[1] - 1, tiles)
        return jnp.minimum(jnp.maximum(index, low), high), 0

    return pl.pallas_call(
        window_kernel,
        out_shape=jax.ShapeDtypeStruct((window, width), BF16),
        grid_spec=pltpu.PrefetchScalarGridSpec(
            num_scalar_prefetch=1,
            grid=(window // row_count,),
            in_specs=[
                pl.BlockSpec((row_count, width), rows),
                pl.BlockSpec((row_count, width), rows),
                pl.BlockSpec((width, width), lambda k, r: (0, spots[0])),
                pl.BlockSpec((width, width), lambda k, r: (0, spots[1])),
            ],
            out_specs=pl.BlockSpec((row_count, width), lambda k, r: (k, 0)),
        ),
        cost_estimate=SMALL,
        compiler_params=pltpu.CompilerParams(vmem_limit_bytes=40 << 20),
    )(covered, grad_keys, grad_values, weights, weights)


def shifted(value, axis, steps):
    count = lax.axis_size(axis)
    pairs = [(source, source + steps) for source in range(count) if 0 <= source + steps < count]
    return lax.ppermute(value, axis, pairs)


def flat_swap(value, mask):
    count = lax.axis_size("seq") * lax.axis_size("dp")
    return lax.ppermute(value, BOTH, [(source, source ^ mask) for source in range(count)])


def groups_of(low, bits):
    groups = []
    if bits % 2:
        groups.append((low, 1))
        low, bits = low + 1, bits - 1
    while bits:
        groups.append((low, 2))
        low, bits = low + 2, bits - 2
    return groups


def bits_of(count):
    bits = count.bit_length() - 1
    assert count == 1 << bits
    return bits


def all_groups(count):
    return [(0, 1)] + groups_of(1, bits_of(count) - 1)


def tie(*values):
    return lax.optimization_barrier(values)


def swaps(piece, group):
    low, bits = group
    return [flat_swap(piece, step << low) for step in range(1, 1 << bits)]


def swap_masks(masks, group):
    low, bits = group
    return [mask ^ (step << low) for step in range(1, 1 << bits) for mask in masks]


def stack_kernel(*refs):
    target = refs[-1]
    start = 0
    for source in refs[:-1]:
        target[start : start + source.shape[0]] = source[...]
        start += source.shape[0]


def stacked(pieces):
    if len(pieces) == 1:
        return pieces[0]
    count = sum(piece.shape[0] for piece in pieces)
    return pl.pallas_call(
        stack_kernel,
        out_shape=jax.ShapeDtypeStruct((count,) + pieces[0].shape[1:], pieces[0].dtype),
        in_specs=[pl.BlockSpec(memory_space=pltpu.VMEM)] * len(pieces),
        out_specs=pl.BlockSpec(memory_space=pltpu.VMEM),
        cost_estimate=SMALL,
        compiler_params=pltpu.CompilerParams(vmem_limit_bytes=40 << 20),
    )(*pieces)


def units_kernel(rank_ref, gate_ref, up_ref, units_ref, *, dp_count):
    left = lax.broadcasted_iota(jnp.int32, (gate_ref.shape[0], TILE), 1) < TILE // 2
    for side, source in enumerate((gate_ref, up_ref)):
        span = source.shape[1] // dp_count
        for owner in range(dp_count):
            for pair in range(span // TILE):
                halves_of = []
                for odd in range(2):
                    unit = (2 * pair + odd) * dp_count + owner
                    tile = source[:, unit // 2 * TILE : (unit // 2 + 1) * TILE]
                    halves_of.append(tile if unit % 2 == odd else pltpu.roll(tile, TILE // 2, 1))
                start = side * span + pair * TILE
                merged = jnp.where(left, halves_of[0], halves_of[1])
                units_ref[rank_ref[0] ^ owner, :, start : start + TILE] = merged.astype(BF16)


def units_of(gate_weight, up_weight, dp_rank, dp_count, seq_count, unit):
    rows, hidden_width = gate_weight.shape
    share = seq_count * unit
    if unit != TILE // 2 or rows % 8:
        both = jnp.stack([gate_weight.astype(BF16), up_weight.astype(BF16)], axis=1)
        both = both.reshape(rows, 2, seq_count, dp_count, unit)
        taken = [
            lax.dynamic_index_in_dim(both, dp_rank ^ mask, 3, keepdims=False).reshape(rows, 2 * share)
            for mask in range(dp_count)
        ]
        return jnp.stack(taken)
    return pl.pallas_call(
        functools.partial(units_kernel, dp_count=dp_count),
        out_shape=jax.ShapeDtypeStruct((dp_count, rows, 2 * share), BF16),
        in_specs=[pl.BlockSpec(memory_space=pltpu.SMEM)] + [pl.BlockSpec(memory_space=pltpu.VMEM)] * 2,
        out_specs=pl.BlockSpec(memory_space=pltpu.VMEM),
    )(dp_rank[None].astype(jnp.int32), gate_weight, up_weight)


def columns_kernel(rank_ref, *refs, dp_count):
    sources, (gate_ref, up_ref), scratch = refs[:dp_count], refs[dp_count : dp_count + 2], refs[-1]
    for mask in range(dp_count):
        scratch[rank_ref[0] ^ mask] = sources[mask][...].astype(F32)
    left = lax.broadcasted_iota(jnp.int32, (gate_ref.shape[0], TILE), 1) < TILE // 2
    for side, target in enumerate((gate_ref, up_ref)):
        span = target.shape[1] // dp_count
        for tile in range(target.shape[1] // TILE):
            halves_of = []
            for odd in range(2):
                group, owner = divmod(2 * tile + odd, dp_count)
                start = side * span + group // 2 * TILE
                part = scratch[owner, :, start : start + TILE]
                halves_of.append(part if group % 2 == odd else pltpu.roll(part, TILE // 2, 1))
            target[:, tile * TILE : (tile + 1) * TILE] = jnp.where(left, halves_of[0], halves_of[1])


def columns_of(parts, dp_rank, dp_count, seq_count, unit):
    rows = parts[0].shape[0]
    hidden_width = seq_count * dp_count * unit
    if unit != TILE // 2 or rows % 8:
        both = jnp.stack(parts)
        both = jnp.stack(
            [lax.dynamic_index_in_dim(both, dp_rank ^ index, 0, keepdims=False) for index in range(dp_count)], axis=1
        )
        both = both.reshape(rows, dp_count, 2, seq_count, unit).transpose(0, 2, 3, 1, 4)
        both = both.reshape(rows, 2, hidden_width).astype(F32)
        return both[:, 0], both[:, 1]
    return pl.pallas_call(
        functools.partial(columns_kernel, dp_count=dp_count),
        out_shape=(jax.ShapeDtypeStruct((rows, hidden_width), F32),) * 2,
        in_specs=[pl.BlockSpec(memory_space=pltpu.SMEM)] + [pl.BlockSpec(memory_space=pltpu.VMEM)] * dp_count,
        out_specs=(pl.BlockSpec(memory_space=pltpu.VMEM),) * 2,
        scratch_shapes=[pltpu.VMEM((dp_count,) + parts[0].shape, F32)],
        cost_estimate=SMALL,
    )(dp_rank[None].astype(jnp.int32), *parts)


def shard_kernel(*refs):
    target = refs[-1]
    start = 0
    for source in refs[:-1]:
        columns = source.shape[1]
        target[:, start : start + columns] = source[...].astype(BF16)
        start += columns


def side_by_side(arrays):
    columns = sum(array.shape[1] for array in arrays)
    return pl.pallas_call(
        shard_kernel,
        out_shape=jax.ShapeDtypeStruct((arrays[0].shape[0], columns), BF16),
        in_specs=[pl.BlockSpec(memory_space=pltpu.VMEM)] * len(arrays),
        out_specs=pl.BlockSpec(memory_space=pltpu.VMEM),
        cost_estimate=SMALL,
        compiler_params=pltpu.CompilerParams(vmem_limit_bytes=40 << 20),
    )(*arrays)


def norm_kernel(gain_ref, *refs):
    target = refs[-1]
    gain = gain_ref[...].astype(F32).T[:1]
    start = 0
    for source in refs[:-1]:
        rows = source[...].astype(F32)
        scale = lax.rsqrt(jnp.mean(rows * rows, axis=1, keepdims=True) + EPSILON)
        target[start : start + source.shape[0]] = (rows * scale * gain).astype(BF16)
        start += source.shape[0]


def normed_rows_of(pieces, weights, block):
    rows, width = pieces[0].shape
    return pl.pallas_call(
        norm_kernel,
        out_shape=jax.ShapeDtypeStruct((len(pieces) * rows, width), BF16),
        grid=(1,),
        in_specs=[pl.BlockSpec((width, TILE), lambda k: (0, block))]
        + [pl.BlockSpec((rows, width), lambda k: (0, 0))] * len(pieces),
        out_specs=pl.BlockSpec((len(pieces) * rows, width), lambda k: (0, 0)),
        compiler_params=pltpu.CompilerParams(vmem_limit_bytes=40 << 20),
    )(weights, *pieces)


def halves_kernel(rank_ref, *refs):
    sources, table_ref, (kept_ref, sent_ref) = refs[:-3], refs[-3], refs[-2:]
    mine = rank_ref[0] & 1
    for index in range(kept_ref.shape[0]):
        for target, side in ((kept_ref, mine), (sent_ref, 1 - mine)):
            start = 0
            for source in sources:
                target[index, :, start : start + source.shape[2]] = source[2 * index + side]
                start += source.shape[2]
            target[index, :, start:] = table_ref[...]


def core_halves(grads, table_block, rank, count):
    rows = grads[0].shape[0] // count
    columns = sum(grad.shape[1] for grad in grads) + TILE
    if rows % 8:
        held = jnp.concatenate(grads + [jnp.tile(table_block, (count, 1))], axis=1).reshape(-1, 2, rows, columns)
        return [lax.dynamic_index_in_dim(held, (rank & 1) ^ side, 1, keepdims=False) for side in range(2)]
    return pl.pallas_call(
        halves_kernel,
        out_shape=(jax.ShapeDtypeStruct((count // 2, rows, columns), BF16),) * 2,
        in_specs=[pl.BlockSpec(memory_space=pltpu.SMEM)]
        + [pl.BlockSpec(memory_space=pltpu.VMEM)] * (len(grads) + 1),
        out_specs=(pl.BlockSpec(memory_space=pltpu.VMEM),) * 2,
        cost_estimate=SMALL,
        compiler_params=pltpu.CompilerParams(vmem_limit_bytes=40 << 20),
    )(rank[None].astype(jnp.int32), *[grad.reshape(count, rows, -1) for grad in grads], table_block)


def place_kernel(rank_ref, *refs, masks):
    target = refs[-1]
    rank = rank_ref[0]
    for source, part in zip(refs, masks):
        for index, mask in enumerate(part):
            target[rank ^ mask] = source[index]


def placed(held, masks, rank):
    count = sum(len(part) for part in masks)
    shape = held[0].shape[1:]
    return pl.pallas_call(
        functools.partial(place_kernel, masks=masks),
        out_shape=jax.ShapeDtypeStruct((count,) + shape, held[0].dtype),
        in_specs=[pl.BlockSpec(memory_space=pltpu.SMEM)] + [pl.BlockSpec(memory_space=pltpu.VMEM)] * len(held),
        out_specs=pl.BlockSpec(memory_space=pltpu.VMEM),
        cost_estimate=SMALL,
        compiler_params=pltpu.CompilerParams(vmem_limit_bytes=40 << 20),
    )(rank[None].astype(jnp.int32), *held)


def place_far_kernel(rank_ref, *refs, masks, dp_count):
    pair_ref, down_ref = refs[-2:]
    rank = rank_ref[0]
    for source, part in zip(refs, masks):
        for index, mask in enumerate(part):
            owner = rank ^ mask
            for entry in range(dp_count):
                pair_ref[owner ^ entry] = source[index, entry]
            for entry in range(dp_count // 2):
                down_ref[owner // dp_count, entry] = source[index, dp_count + entry]


def place_far(held, masks, rank, dp_count):
    count = sum(len(part) for part in masks)
    shape = held[0].shape[2:]
    dtype = held[0].dtype
    return pl.pallas_call(
        functools.partial(place_far_kernel, masks=masks, dp_count=dp_count),
        out_shape=(
            jax.ShapeDtypeStruct((count * dp_count,) + shape, dtype),
            jax.ShapeDtypeStruct((count, dp_count // 2) + shape, dtype),
        ),
        in_specs=[pl.BlockSpec(memory_space=pltpu.SMEM)] + [pl.BlockSpec(memory_space=pltpu.VMEM)] * len(held),
        out_specs=(pl.BlockSpec(memory_space=pltpu.VMEM), pl.BlockSpec(memory_space=pltpu.VMEM)),
        cost_estimate=SMALL,
        compiler_params=pltpu.CompilerParams(vmem_limit_bytes=40 << 20),
    )(rank[None].astype(jnp.int32), *held)


def split_and_swap(held, mine, group):
    low, bits = group
    held = held.reshape((-1, 1 << bits) + held.shape[1:])
    kept = lax.dynamic_index_in_dim(held, mine, 1, keepdims=False)
    got = [
        flat_swap(lax.dynamic_index_in_dim(held, mine ^ step, 1, keepdims=False), step << low)
        for step in range(1, 1 << bits)
    ]
    return kept, got


def joined(kept, got):
    values = [piece.astype(F32) for piece in [kept] + got]
    while len(values) > 1:
        values = [values[k] + values[k + 1] for k in range(0, len(values), 2)]
    return values[0]


def spread_dp(parts, bits):
    held = {(mask, 0): part for mask, part in parts.items()}
    for bit in range(bits):
        step = 1 << bit
        keys = sorted(key for key in held if key[0] & step)
        sent = flat_swap(jnp.stack([held[key] for key in keys]), step)
        held = {key: part for key, part in held.items() if not key[0] & step}
        held.update({(goal ^ step, source ^ step): sent[k] for k, (goal, source) in enumerate(keys)})
    return [held[(0, mask)] for mask in range(1 << bits)]


def gather_dp(value, bits):
    held = {0: value}
    for bit in range(bits - 1, -1, -1):
        held.update({mask ^ (1 << bit): flat_swap(piece, 1 << bit) for mask, piece in list(held.items())})
    return [held[mask] for mask in range(1 << bits)]


def scatter_dp(parts, bits):
    held = dict(enumerate(parts))
    for bit in range(bits):
        step = 1 << bit
        held = {
            mask: piece.astype(F32) + flat_swap(held[mask ^ step].astype(BF16), step).astype(F32)
            for mask, piece in held.items()
            if not mask & step
        }
    return held[0]


def parts_of(value, parts, to_rows):
    rows = value.shape[0] // parts
    columns = rows * value.shape[1] // to_rows
    if rows % 8 or to_rows % 8 or value.shape[1] % TILE or columns % TILE:
        return value.reshape(parts * to_rows, columns)
    tiles = value.reshape(parts, rows // 8, 8, value.shape[1] // TILE, TILE).transpose(0, 1, 3, 2, 4)
    tiles = tiles.reshape(parts, to_rows // 8, columns // TILE, 8, TILE).transpose(0, 1, 3, 2, 4)
    return tiles.reshape(parts * to_rows, columns)


def contract(left_side, right_side, left_dim, right_dim):
    return lax.dot_general(
        left_side, right_side, (((left_dim,), (right_dim,)), ((), ())), preferred_element_type=F32
    )


def gelu_pair(v):
    scale = 0.7978845608028654
    bent = jnp.tanh(scale * (v + 0.044715 * v * v * v))
    value = 0.5 * v * (1.0 + bent)
    slope = 0.5 * (1.0 + bent) + 0.5 * v * (1.0 - bent * bent) * scale * (1.0 + 3.0 * 0.044715 * v * v)
    return value, slope


def body(
    blocks,
    lengths,
    bucket_table,
    first_gain,
    query_weight,
    key_weight,
    value_weight,
    output_weight,
    table_weight,
    second_gain,
    gate_weight,
    up_weight,
    down_weight,
    cotangent,
):
    seq_count = lax.axis_size("seq")
    device_count = seq_count * lax.axis_size("dp")
    seq_rank = lax.axis_index("seq")
    row_count, width = blocks.shape[1:]
    pack_rows = row_count * seq_count
    bucket_count, heads = table_weight.shape
    head_dim = width // heads
    seq_total = lengths.shape[1]
    max_length = (bucket_table.shape[0] + 1) // 2
    shard_rows = query_weight.shape[0]
    hidden_width = gate_weight.shape[1]
    reach = min((max_length - 1 + row_count - 1) // row_count, seq_count - 1)
    query_blocks = row_count // TILE
    window = (2 * reach + 1) * row_count
    window_blocks = window // TILE
    tile_count = window_blocks + query_blocks - 1
    center = reach * query_blocks + query_blocks - 1
    pairs = 2 if window <= 2304 else 1

    dp_count = lax.axis_size("dp")
    dp_rank = lax.axis_index("dp")
    dp_bits = bits_of(dp_count)
    rank = seq_rank * dp_count + dp_rank
    groups = all_groups(device_count)
    seq_groups = groups_of(dp_bits, bits_of(seq_count))
    own = blocks[0]

    gains = jnp.pad(jnp.stack([first_gain, second_gain], axis=1), ((0, 0), (0, TILE - 2)))
    near_shard = side_by_side([query_weight, key_weight, value_weight, output_weight, gains])

    unit = down_weight.shape[0]
    share = seq_count * unit
    pair_units = units_of(gate_weight, up_weight, dp_rank, dp_count, seq_count, unit)

    line_width = (tile_count + 1) * TILE
    ahead = (tile_count - center) * TILE - (max_length - 1)
    behind = line_width - ahead - bucket_table.shape[0]
    bucket_line = jnp.pad(bucket_table[::-1], (max(ahead, 0), max(behind, 0)), mode="edge")
    bucket_line = bucket_line[max(-ahead, 0) : max(-ahead, 0) + line_width]
    bucket_ids = jnp.arange(bucket_count, dtype=jnp.int32)
    line_hot = (bucket_line[None, :] == bucket_ids[:, None]).astype(F32)
    lines = lax.dot_general(table_weight, line_hot, (((0,), (0,)), ((), ())), precision=HIGHEST)

    order = groups[::-1]
    near_shard = near_shard[None]
    masks = [0]
    around = {0: own}
    near_held = near_shard
    stages = len(order)
    for stage, group in enumerate(order):
        got = swaps(near_held, group)
        last = stage == stages - 1
        moves = [step for step in range(1, reach + 1) if step == stage + 1 or (last and step > stage)]
        arrived = {}
        for step in moves:
            arrived[step] = shifted(own, "seq", step)
            arrived[-step] = shifted(own, "seq", -step)
        got_masks = swap_masks(masks, group)
        if last:
            held, masks = [near_held] + got, [masks] + [
                got_masks[k * len(masks) : (k + 1) * len(masks)] for k in range(len(got))
            ]
        else:
            if stage == 0:
                lines = tie(lines, got[0])[0]
            if stage == 1:
                tiles = bias_tiles(lines, tile_count)
                near_held, got, arrived, tiles = tie(near_held, got, arrived, tiles)
            else:
                near_held, got, arrived = tie(near_held, got, arrived)
            near_held = stacked([near_held] + got)
            masks = masks + got_masks
        around.update(arrived)
    near_full = placed(held, masks, rank)
    near_full = near_full.reshape(device_count * shard_rows, 4 * width + TILE)
    weight_query = near_full[:, :width]
    weight_key = near_full[:, width : 2 * width]
    weight_value = near_full[:, 2 * width : 3 * width]
    weight_output = near_full[:, 3 * width : 4 * width]
    gain_columns = near_full[:, 4 * width :]

    pair_parts = spread_dp({mask: pair_units[mask] for mask in range(dp_count)}, dp_bits)
    down_parts = parts_of(down_weight.astype(BF16), 1, shard_rows * dp_count // 2)
    down_parts = down_parts.reshape(dp_count // 2, shard_rows, 2 * share)
    far_shard = stacked([part[None] for part in pair_parts] + [down_parts])
    far_shard = tie(far_shard, near_held)[0][None]
    far_order = seq_groups[::-1]
    far_first = swaps(far_shard, far_order[0])
    far_own = [piece for group in far_order[1:2] for piece in swaps(far_shard, group)]
    gain_one = gain_columns[:, 0].astype(F32)[None, :]
    gain_two = gain_columns[:, 1].astype(F32)[None, :]

    seq_ends = jnp.cumsum(lengths[0], dtype=jnp.int32)
    query_first = seq_rank * row_count
    window_first = query_first - reach * row_count

    def segments(at):
        return jnp.sum((at[:, None] >= seq_ends[None, :]).astype(jnp.int32), axis=1, dtype=jnp.int32)

    query_places = query_first + jnp.arange(row_count, dtype=jnp.int32)
    key_places = window_first + jnp.arange(window, dtype=jnp.int32)
    query_seg = segments(query_places)
    key_seg = jnp.where((key_places >= 0) & (key_places < pack_rows), segments(key_places), -1)
    lanes = jnp.arange(TILE, dtype=jnp.int32)
    key_feat = jnp.where(
        (key_seg[:, None] != lanes[None, :]) & (lanes[None, :] <= seq_total), BIG, 0.0
    ).astype(BF16)
    query_feat = (lanes[:, None] == query_seg[None, :]).astype(BF16)
    valid_rows = (query_seg < seq_total).astype(F32)
    seq_starts = jnp.concatenate([jnp.zeros((1,), jnp.int32), seq_ends])
    seq_stops = jnp.concatenate([seq_ends, jnp.full((1,), pack_rows, jnp.int32)])
    seq_ids = jnp.arange(seq_total + 1, dtype=jnp.int32)
    low_seg = query_seg[::TILE]
    high_seg = query_seg[TILE - 1 :: TILE]
    low = jnp.sum(jnp.where(low_seg[:, None] == seq_ids[None, :], seq_starts[None, :], 0), axis=1)
    high = jnp.sum(jnp.where(high_seg[:, None] == seq_ids[None, :], seq_stops[None, :], 0), axis=1)
    first = (low - window_first) // TILE
    last = (high - window_first + TILE - 1) // TILE
    steps = (last - first + STEP - 1) // STEP
    first = jnp.minimum(first, window_blocks - steps * STEP).astype(jnp.int32)
    steps = steps.astype(jnp.int32)


    window_normed = normed_rows_of(
        [around[-step] for step in range(-reach, reach + 1)], near_full, 4 * width // TILE
    )
    own_slice = slice(reach * row_count, (reach + 1) * row_count)
    tokens = own.astype(F32)
    scale_one = lax.rsqrt(jnp.mean(tokens * tokens, axis=1, keepdims=True) + EPSILON)
    normed_own = window_normed[own_slice]
    keys = contract(window_normed, weight_key, 1, 0).astype(BF16)
    values_turned = contract(weight_value, window_normed, 0, 1).astype(BF16)
    queries_turned = contract(weight_query, normed_own, 0, 1).astype(BF16)
    outs, logs = attend(
        first, steps, queries_turned, keys, values_turned, key_feat, query_feat, tiles, head_dim, pairs
    )
    far_first = stacked(tie(far_first, outs)[0])
    grad_held = {0: cotangent[0]}
    for bit in range(dp_bits - 1, 0, -1):
        grad_held.update({mask ^ (1 << bit): flat_swap(piece, 1 << bit) for mask, piece in list(grad_held.items())})
    outs, grad_held = tie(outs, grad_held)
    first_masks = swap_masks([0], far_order[0])
    far_held, far_masks = [far_shard, far_first], [[0], first_masks]
    for number, group in enumerate(far_order[1:]):
        got, got_masks = [], []
        for piece, part in zip(far_held, far_masks):
            more = far_own if piece is far_shard and number == 0 else swaps(piece, group)
            extra = swap_masks(part, group)
            got += more
            got_masks += [extra[k * len(part) : (k + 1) * len(part)] for k in range(len(more))]
        far_held, far_masks = far_held + got, far_masks + got_masks
    far_full = place_far(far_held, far_masks, rank, dp_count)
    weight_pair = far_full[0].reshape(device_count * shard_rows, 2 * share)
    weight_down = parts_of(far_full[1].reshape(-1, 2 * share), seq_count, unit)
    attended = (outs * valid_rows[None, :]).astype(BF16)
    middle = tokens + contract(attended, weight_output, 0, 0)

    scale_two = lax.rsqrt(jnp.mean(middle * middle, axis=1, keepdims=True) + EPSILON)
    second = middle * scale_two
    second_low = (second * gain_two).astype(BF16)
    every_second = jnp.concatenate(gather_dp(second_low, dp_bits), axis=0)
    grad_held.update({mask ^ 1: flat_swap(piece, 1) for mask, piece in list(grad_held.items())})
    every_grad = jnp.concatenate([grad_held[mask] for mask in range(dp_count)], axis=0)
    both_ways = contract(every_second, weight_pair, 1, 0)
    gate_values, upward = both_ways[:, :share], both_ways[:, share:]
    active, slope = gelu_pair(gate_values)
    hidden = (active * upward).astype(BF16)
    grad_hidden = contract(every_grad, weight_down, 1, 1)
    grad_pair = jnp.concatenate(
        [(grad_hidden * upward * slope).astype(BF16), (grad_hidden * active).astype(BF16)], axis=1
    )
    every_back = contract(grad_pair, weight_pair, 1, 1).astype(BF16)
    grad_second = scatter_dp(jnp.split(every_back, dp_count, axis=0), dp_bits)
    grad_out = cotangent[0]
    scaled = grad_second * gain_two
    grad_middle = grad_out.astype(F32) + scale_two * (
        scaled - second * jnp.mean(scaled * second, axis=1, keepdims=True)
    )
    grad_branch = grad_middle.astype(BF16)
    grad_mixed = (contract(grad_branch, weight_output, 1, 1).astype(BF16).astype(F32) * valid_rows[:, None]).astype(BF16)
    grad_mixed_turned = (
        contract(weight_output, grad_branch, 1, 1).astype(BF16).astype(F32) * valid_rows[None, :]
    ).astype(BF16)
    grad_output_weight = contract(attended, grad_branch, 1, 0).astype(BF16)
    grad_down = contract(hidden, every_grad, 0, 0).astype(BF16)
    grad_down = parts_of(grad_down, seq_count, shard_rows * dp_count // 2)
    grad_pair_weight = contract(every_second, grad_pair, 0, 0).astype(BF16)
    far_grads = jnp.concatenate(
        [
            grad_pair_weight.reshape(seq_count, dp_count, shard_rows, 2 * share),
            grad_down.reshape(seq_count, dp_count // 2, shard_rows, 2 * share),
        ],
        axis=1,
    )
    every_out = contract(hidden, weight_down, 1, 0).astype(BF16)
    far_grads, grad_mixed, grad_mixed_turned, grad_output_weight, every_out = tie(
        far_grads, grad_mixed, grad_mixed_turned, grad_output_weight, every_out
    )
    out_parts = jnp.split(every_out, dp_count, axis=0)
    bits = seq_groups[0][1]
    far_kept, far_got = split_and_swap(far_grads, seq_rank & ((1 << bits) - 1), seq_groups[0])

    queries = contract(normed_own, weight_query, 1, 0).astype(BF16)
    keys_turned = contract(weight_key, window_normed, 0, 1).astype(BF16)
    values = contract(window_normed, weight_value, 1, 0).astype(BF16)
    grad_queries, grad_keys, grad_values, tile_sums = attend_back(
        first, steps, queries, queries_turned, keys, keys_turned, values, grad_mixed, grad_mixed_turned,
        outs, logs, key_feat, query_feat, tiles, head_dim, pairs,
    )
    out_parts = [out_parts[0]] + [flat_swap(out_parts[mask], mask) for mask in range(1, dp_count)]
    grad_queries, out_parts = tie(grad_queries, out_parts)
    output = middle + sum(part.astype(F32) for part in out_parts)
    grad_queries, grad_keys, grad_values, tile_sums, far_kept, far_got = tie(
        grad_queries, grad_keys, grad_values, tile_sums, far_kept, far_got
    )
    for low, bits in seq_groups[1:]:
        far_held = joined(far_kept, far_got).astype(BF16)
        far_kept, far_got = split_and_swap(far_held, (rank >> low) & ((1 << bits) - 1), (low, bits))
    covered = jnp.stack([jnp.min(first), jnp.max(first + steps * STEP)])
    partial_low = window_gradient(grad_keys, grad_values, near_full, (1, 2), covered, row_count)

    def returned_from(low_rows, step):
        parts = []
        for turn in (step, -step):
            part = low_rows[(reach + turn) * row_count : (reach + turn + 1) * row_count]
            parts.append(shifted(part, "seq", turn))
        return parts

    returned = returned_from(partial_low, 1)
    if reach > 2:
        returned = returned + returned_from(partial_low, reach - 1)
    grad_query_weight = contract(normed_own, grad_queries, 0, 1).astype(BF16)
    grad_key_weight = contract(window_normed, grad_keys, 0, 0).astype(BF16)
    grad_value_weight = contract(window_normed, grad_values, 0, 0).astype(BF16)

    tile_first = first - jnp.arange(query_blocks, dtype=jnp.int32) + (query_blocks - 1)
    used = jnp.stack([jnp.min(tile_first), jnp.max(tile_first + steps * STEP)])
    flipped = bucket_line.reshape(tile_count + 1, TILE)[::-1]
    bucket_at = jnp.concatenate([flipped[:-1], flipped[1:]], axis=1)[:, None, :]
    grad_table = table_sums(tile_sums, used, bucket_at, bucket_count).T
    table_rows = -(-grad_table.size // TILE)
    table_block = jnp.pad(grad_table.reshape(-1), (0, table_rows * TILE - grad_table.size)).reshape(table_rows, TILE)
    table_block = jnp.pad(table_block, ((0, shard_rows - table_rows), (0, 0))).astype(BF16)
    kept, sent = core_halves(
        [grad_query_weight, grad_key_weight, grad_value_weight, grad_output_weight], table_block, rank, device_count
    )
    kept, sent, partial_low, returned, far_kept, far_got = tie(kept, sent, partial_low, returned, far_kept, far_got)
    far_sum = joined(far_kept, far_got).reshape(far_grads.shape[1:]).astype(BF16)

    left = [step for step in range(reach, 2, -1) if step != reach - 1]
    waiting = returned_from(partial_low, 2) if reach == 2 or reach > 3 else []
    for stage, (low, bits) in enumerate(groups):
        if stage == 0:
            got = [flat_swap(sent, 1)]
        else:
            kept, got = split_and_swap(near_held, (rank >> low) & ((1 << bits) - 1), (low, bits))
        if stage == 0:
            kept, got, partial_low = tie(kept, got, partial_low)
        else:
            arrived = returned_from(partial_low, left.pop(0)) if left else []
            kept, got, arrived, waiting, partial_low, far_sum = tie(
                kept, got, arrived, waiting, partial_low, far_sum
            )
            if stage == 1:
                pair_back = spread_dp(
                    {mask: lax.dynamic_index_in_dim(far_sum, dp_rank ^ mask, 0, keepdims=False) for mask in range(dp_count)},
                    dp_bits,
                )
            if stage == 2:
                kept, pair_back = tie(kept, pair_back)
            returned, waiting = returned + arrived + waiting, []
        total = joined(kept, got)
        near_held = total.astype(BF16)
    for step in left:
        returned = returned + returned_from(partial_low, step)
    near_sum = total.reshape(shard_rows, 4 * width + TILE)
    grad_normed = partial_low[own_slice].astype(F32) + contract(grad_queries, weight_query, 0, 1)
    grad_normed = grad_normed + sum(piece.astype(F32) for piece in returned)
    grad_gate_own, grad_up_own = columns_of(pair_back, dp_rank, dp_count, seq_count, unit)
    grad_down_own = parts_of(far_sum[dp_count:].astype(F32).reshape(-1, 2 * share), 1, unit)
    normed_rows = tokens * scale_one
    scaled_one = grad_normed * gain_one
    grad_blocks = grad_middle + scale_one * (
        scaled_one - normed_rows * jnp.mean(scaled_one * normed_rows, axis=1, keepdims=True)
    )

    grad_table = near_sum[:table_rows, 4 * width :].reshape(-1)[: table_weight.size].reshape(table_weight.shape)

    def gain_grad(gain, weights, grads):
        total = sum(jnp.sum(weight.astype(BF16).astype(F32) * grad, axis=1) for weight, grad in zip(weights, grads))
        return total / gain.astype(BF16).astype(F32)

    near_parts = [near_sum[:, k * width : (k + 1) * width] for k in range(4)]
    grad_gain_one = gain_grad(first_gain, (query_weight, key_weight, value_weight), near_parts[:3])
    grad_gain_two = gain_grad(second_gain, (gate_weight, up_weight), (grad_gate_own, grad_up_own))
    return (
        output.astype(BF16)[None],
        grad_blocks[None],
        grad_gain_one,
        near_parts[0],
        near_parts[1],
        near_parts[2],
        near_parts[3],
        grad_table,
        grad_gain_two,
        grad_gate_own,
        grad_up_own,
        grad_down_own,
    )


def solution(mesh):
    return jax.shard_map(
        body,
        mesh=mesh,
        in_specs=(
            P("dp", "seq", None),
            P("dp", None),
            P(),
            P(("seq", "dp")),
            P(("seq", "dp"), None),
            P(("seq", "dp"), None),
            P(("seq", "dp"), None),
            P(("seq", "dp"), None),
            P(),
            P(("seq", "dp")),
            P(("seq", "dp"), None),
            P(("seq", "dp"), None),
            P(("seq", "dp"), None),
            P("dp", "seq", None),
        ),
        out_specs=(
            P("dp", "seq", None),
            P("dp", "seq", None),
            P(("seq", "dp")),
            P(("seq", "dp"), None),
            P(("seq", "dp"), None),
            P(("seq", "dp"), None),
            P(("seq", "dp"), None),
            P(),
            P(("seq", "dp")),
            P(("seq", "dp"), None),
            P(("seq", "dp"), None),
            P(("seq", "dp"), None),
        ),
        check_vma=False,
    )
```

```python
import functools

import jax
import jax.numpy as jnp
from jax import lax
from jax.experimental import pallas as pl
from jax.experimental.pallas import tpu as pltpu
from jax.sharding import PartitionSpec as P

EPSILON = 1e-06
BIG = -1e30
HIGHEST = lax.Precision.HIGHEST
BOTH = ("seq", "dp")
SMALL = pl.CostEstimate(flops=1, bytes_accessed=1, transcendentals=0)
TILE = 128
STEP = 4
SPAN = STEP * TILE
F32 = jnp.float32
BF16 = jnp.bfloat16
LOWEST = -3.0e38


def bias_of(tiles_ref, pair, tile):
    halves_of = [tiles_ref[2 * pair + side, pl.ds(tile, STEP)].reshape(SPAN, TILE) for side in range(2)]
    return jnp.concatenate(halves_of, axis=1)


def dot(a, b):
    return jnp.dot(a, b, preferred_element_type=F32)


def tiles_kernel(line_ref, tiles_ref):
    tile_count = tiles_ref.shape[1]
    for index in range(tile_count):
        window = line_ref[0, :, pl.ds((tile_count - 1 - index) * TILE, 2 * TILE)]
        spread = jnp.broadcast_to(window, (TILE, 2 * TILE))
        rolled = pltpu.roll(spread, 0, 1, stride=1, stride_axis=0)
        tiles_ref[0, index] = rolled[:, TILE:]


def bias_tiles(lines, tile_count):
    heads, width = lines.shape
    return pl.pallas_call(
        tiles_kernel,
        out_shape=jax.ShapeDtypeStruct((heads, tile_count, TILE, TILE), F32),
        grid=(heads,),
        in_specs=[pl.BlockSpec((1, 1, width), lambda h: (h, 0, 0))],
        out_specs=pl.BlockSpec((1, tile_count, TILE, TILE), lambda h: (h, 0, 0, 0)),
        cost_estimate=SMALL,
    )(lines.reshape(heads, 1, width))


def halves(pair, head_dim):
    top = lax.broadcasted_iota(jnp.int32, pair.shape, 0) < head_dim
    zero = jnp.zeros_like(pair)
    return jnp.concatenate([jnp.where(top, pair, zero), jnp.where(top, zero, pair)], axis=1)


def halves_rows(pair, head_dim):
    left = lax.broadcasted_iota(jnp.int32, pair.shape, 1) < head_dim
    zero = jnp.zeros_like(pair)
    return jnp.concatenate([jnp.where(left, pair, zero), jnp.where(left, zero, pair)], axis=0)


def merge_halves(both, head_dim):
    top = lax.broadcasted_iota(jnp.int32, (both.shape[0], TILE), 0) < head_dim
    return jnp.where(top, both[:, :TILE], both[:, TILE:])


def fold(values, op):
    return op(values.reshape(values.shape[0] // 8, 8, values.shape[1]), axis=0)


def cols(pair):
    return slice(pair * TILE, (pair + 1) * TILE)


def wide(pair):
    return slice(pair * 2 * TILE, (pair + 1) * 2 * TILE)


def query_side(query_ref, query_feat_ref, block, pair, head_dim):
    rows = slice(block * TILE, (block + 1) * TILE)
    turned = query_ref[cols(pair), rows]
    feat = query_feat_ref[:, rows]
    return jnp.concatenate([halves(turned, head_dim), jnp.concatenate([feat, feat], axis=1)], axis=0)


def forward_kernel(
    first_ref, last_ref, query_ref, key_ref, value_turned_ref, key_feat_ref, query_feat_ref, tiles_ref,
    out_ref, log_ref, score_ref, total_ref, *, pairs, blocks, head_dim,
):
    for block in range(blocks):
        rows = slice(block * TILE, (block + 1) * TILE)
        first, last = first_ref[block], last_ref[block]
        query_sides = [query_side(query_ref, query_feat_ref, block, pair, head_dim) for pair in range(pairs)]

        def score_step(index, highest):
            start = pl.multiple_of((first + index * STEP) * TILE, TILE)
            feat = key_feat_ref[pl.ds(start, SPAN), :]
            tile = first + index * STEP - block + (blocks - 1)
            result = []
            for pair in range(pairs):
                left = jnp.concatenate([key_ref[pl.ds(start, SPAN), cols(pair)], feat], axis=1)
                bias = bias_of(tiles_ref, pair, tile)
                scores = dot(left, query_sides[pair]) + bias
                score_ref[pl.ds(start, SPAN), wide(pair)] = scores
                result.append(jnp.maximum(highest[pair], fold(scores, jnp.max)))
            return tuple(result)

        start_max = tuple(jnp.full((8, 2 * TILE), LOWEST, F32) for _ in range(pairs))
        highest = lax.fori_loop(0, last, score_step, start_max)
        peak = [jnp.max(value, axis=0, keepdims=True) for value in highest]
        total_ref[...] = jnp.zeros_like(total_ref)

        def value_step(index, sums):
            start = pl.multiple_of((first + index * STEP) * TILE, TILE)
            result = []
            for pair in range(pairs):
                weights = jnp.exp(score_ref[pl.ds(start, SPAN), wide(pair)] - peak[pair])
                result.append(sums[pair] + fold(weights, jnp.sum))
                total_ref[:, wide(pair)] += dot(
                    value_turned_ref[cols(pair), pl.ds(start, SPAN)], weights.astype(BF16)
                )
            return tuple(result)

        start_sum = tuple(jnp.zeros((8, 2 * TILE), F32) for _ in range(pairs))
        sums = lax.fori_loop(0, last, value_step, start_sum)
        for pair in range(pairs):
            denominator = jnp.sum(sums[pair], axis=0, keepdims=True)
            out_ref[cols(pair), rows] = merge_halves(total_ref[:, wide(pair)] / denominator, head_dim)
            log_ref[0, block * pairs + pair : block * pairs + pair + 1, :] = peak[pair] + jnp.log(denominator)


def attend(first, last, queries, keys, values_turned, key_feat, query_feat, tiles, head_dim, pairs):
    width, row_count = queries.shape
    window = keys.shape[0]
    blocks = row_count // TILE
    groups = width // (pairs * TILE)
    tile_count = tiles.shape[1]
    kernel = functools.partial(
        forward_kernel, pairs=pairs, blocks=blocks, head_dim=head_dim
    )
    work = row_count * 1280 * width
    return pl.pallas_call(
        kernel,
        out_shape=(
            jax.ShapeDtypeStruct((width, row_count), F32),
            jax.ShapeDtypeStruct((groups, blocks * pairs, 2 * TILE), F32),
        ),
        grid_spec=pltpu.PrefetchScalarGridSpec(
            num_scalar_prefetch=2,
            grid=(groups,),
            in_specs=[
                pl.BlockSpec((pairs * TILE, row_count), lambda g, a, b: (g, 0)),
                pl.BlockSpec((window, pairs * TILE), lambda g, a, b: (0, g)),
                pl.BlockSpec((pairs * TILE, window), lambda g, a, b: (g, 0)),
                pl.BlockSpec((window, TILE), lambda g, a, b: (0, 0)),
                pl.BlockSpec((TILE, row_count), lambda g, a, b: (0, 0)),
                pl.BlockSpec((2 * pairs, tile_count, TILE, TILE), lambda g, a, b: (g, 0, 0, 0)),
            ],
            out_specs=[
                pl.BlockSpec((pairs * TILE, row_count), lambda g, a, b: (g, 0)),
                pl.BlockSpec((1, blocks * pairs, 2 * TILE), lambda g, a, b: (g, 0, 0)),
            ],
            scratch_shapes=[
                pltpu.VMEM((window, pairs * 2 * TILE), F32),
                pltpu.VMEM((TILE, pairs * 2 * TILE), F32),
            ],
        ),
        compiler_params=pltpu.CompilerParams(vmem_limit_bytes=50 << 20),
        cost_estimate=pl.CostEstimate(flops=16 * work, bytes_accessed=24 << 20, transcendentals=row_count * 1280 * 12),
    )(first, last, queries, keys, values_turned, key_feat, query_feat, tiles)


def backward_kernel(
    first_ref, last_ref, query_ref, query_turned_ref, key_ref, key_turned_ref, value_ref, grad_ref, grad_turned_ref, out_ref, log_ref,
    key_feat_ref, query_feat_ref, tiles_ref,
    grad_query_ref, grad_key_ref, grad_value_ref, tile_total,
    key_total, value_total, query_total, *, pairs, blocks, head_dim,
):
    key_total[...] = jnp.zeros_like(key_total)
    value_total[...] = jnp.zeros_like(value_total)
    tile_total[...] = jnp.zeros_like(tile_total)
    for block in range(blocks):
        rows = slice(block * TILE, (block + 1) * TILE)
        first, last = first_ref[block], last_ref[block]
        query_sides, grad_sides, query_stacks, grad_stacks, logs, deltas = [], [], [], [], [], []
        for pair in range(pairs):
            query_sides.append(query_side(query_turned_ref, query_feat_ref, block, pair, head_dim))
            grad_pair = grad_ref[rows, cols(pair)]
            grad_turned = grad_turned_ref[cols(pair), rows]
            grad_sides.append(halves(grad_turned, head_dim))
            query_stacks.append(halves_rows(query_ref[rows, cols(pair)], head_dim))
            grad_stacks.append(halves_rows(grad_pair, head_dim))
            logs.append(log_ref[0, block * pairs + pair : block * pairs + pair + 1, :])
            both = halves(grad_turned.astype(F32) * out_ref[cols(pair), rows], head_dim)
            deltas.append(jnp.sum(both, axis=0, keepdims=True))
        query_total[...] = jnp.zeros_like(query_total)

        def step(index, carry):
            start = pl.multiple_of((first + index * STEP) * TILE, TILE)
            span = pl.ds(start, SPAN)
            feat = key_feat_ref[span, :]
            tile = first + index * STEP - block + (blocks - 1)
            for pair in range(pairs):
                left = jnp.concatenate([key_ref[span, cols(pair)], feat], axis=1)
                bias = bias_of(tiles_ref, pair, tile)
                weights = jnp.exp(dot(left, query_sides[pair]) + bias - logs[pair])
                grad_weights = dot(value_ref[span, cols(pair)], grad_sides[pair])
                grad_scores = weights * (grad_weights - deltas[pair])
                tile_total[2 * pair, pl.ds(tile, STEP)] += grad_scores[:, :TILE].reshape(STEP, TILE, TILE)
                tile_total[2 * pair + 1, pl.ds(tile, STEP)] += grad_scores[:, TILE:].reshape(STEP, TILE, TILE)
                scores_low = grad_scores.astype(BF16)
                value_total[span, cols(pair)] += dot(weights.astype(BF16), grad_stacks[pair])
                key_total[span, cols(pair)] += dot(scores_low, query_stacks[pair])
                query_total[:, wide(pair)] += dot(key_turned_ref[cols(pair), span], scores_low)
            return carry

        lax.fori_loop(0, last, step, 0)
        for pair in range(pairs):
            grad_query_ref[cols(pair), rows] = merge_halves(query_total[:, wide(pair)], head_dim).astype(BF16)
    grad_key_ref[...] = key_total[...].astype(BF16)
    grad_value_ref[...] = value_total[...].astype(BF16)


def attend_back(first, last, queries, queries_turned, keys, keys_turned, values, grads, grads_turned, outs, logs, key_feat, query_feat, tiles, head_dim, pairs):
    row_count, width = queries.shape
    window = keys.shape[0]
    blocks = row_count // TILE
    groups = width // (pairs * TILE)
    heads, tile_count = tiles.shape[:2]
    kernel = functools.partial(backward_kernel, pairs=pairs, blocks=blocks, head_dim=head_dim)
    rows_spec = pl.BlockSpec((row_count, pairs * TILE), lambda g, a, b: (0, g))
    turned_spec = pl.BlockSpec((pairs * TILE, row_count), lambda g, a, b: (g, 0))
    window_spec = pl.BlockSpec((window, pairs * TILE), lambda g, a, b: (0, g))
    work = row_count * 1280 * width
    return pl.pallas_call(
        kernel,
        out_shape=(
            jax.ShapeDtypeStruct((width, row_count), BF16),
            jax.ShapeDtypeStruct((window, width), BF16),
            jax.ShapeDtypeStruct((window, width), BF16),
            jax.ShapeDtypeStruct((heads, tile_count, TILE, TILE), F32),
        ),
        grid_spec=pltpu.PrefetchScalarGridSpec(
            num_scalar_prefetch=2,
            grid=(groups,),
            in_specs=[
                rows_spec,
                turned_spec,
                window_spec,
                pl.BlockSpec((pairs * TILE, window), lambda g, a, b: (g, 0)),
                window_spec,
                rows_spec,
                turned_spec,
                turned_spec,
                pl.BlockSpec((1, blocks * pairs, 2 * TILE), lambda g, a, b: (g, 0, 0)),
                pl.BlockSpec((window, TILE), lambda g, a, b: (0, 0)),
                pl.BlockSpec((TILE, row_count), lambda g, a, b: (0, 0)),
                pl.BlockSpec((2 * pairs, tile_count, TILE, TILE), lambda g, a, b: (g, 0, 0, 0)),
            ],
            out_specs=[
                turned_spec,
                window_spec,
                window_spec,
                pl.BlockSpec((2 * pairs, tile_count, TILE, TILE), lambda g, a, b: (g, 0, 0, 0)),
            ],
            scratch_shapes=[
                pltpu.VMEM((window, pairs * TILE), F32),
                pltpu.VMEM((window, pairs * TILE), F32),
                pltpu.VMEM((TILE, pairs * 2 * TILE), F32),
            ],
        ),
        input_output_aliases={13: 3},
        compiler_params=pltpu.CompilerParams(vmem_limit_bytes=56 << 20),
        cost_estimate=pl.CostEstimate(flops=40 * work, bytes_accessed=32 << 20, transcendentals=row_count * 1280 * 12),
    )(first, last, queries, queries_turned, keys, keys_turned, values, grads, grads_turned, outs, logs, key_feat, query_feat, tiles)


def table_kernel(range_ref, tiles_ref, bucket_ref, table_ref):
    index = pl.program_id(0)
    heads = tiles_ref.shape[0]

    @pl.when(index == 0)
    def _():
        table_ref[...] = jnp.zeros_like(table_ref)

    @pl.when((index >= range_ref[0]) & (index < range_ref[1]))
    def _():
        rows = []
        for head in range(heads):
            tile = tiles_ref[head, 0]
            padded = jnp.concatenate([tile, jnp.zeros_like(tile)], axis=1)
            size = TILE // 2
            while size >= 1:
                padded = padded[:size] + pltpu.roll(padded[size:], 2 * TILE - size, 1)
                size //= 2
            rows.append(padded)
        sums = jnp.concatenate(rows, axis=0)
        buckets = lax.broadcasted_iota(jnp.int32, (table_ref.shape[1], 2 * TILE), 0)
        hot = (buckets == bucket_ref[0]).astype(F32)
        table_ref[...] += lax.dot_general(
            sums, hot, (((1,), (1,)), ((), ())), preferred_element_type=F32, precision=HIGHEST
        )


def table_sums(tiles, used, bucket_at, bucket_count):
    heads, tile_count = tiles.shape[:2]

    def held(index, used_ref):
        return jnp.minimum(jnp.maximum(index, used_ref[0]), used_ref[1] - 1)

    return pl.pallas_call(
        table_kernel,
        out_shape=jax.ShapeDtypeStruct((heads, bucket_count), F32),
        grid_spec=pltpu.PrefetchScalarGridSpec(
            num_scalar_prefetch=1,
            grid=(tile_count,),
            in_specs=[
                pl.BlockSpec((heads, 1, TILE, TILE), lambda t, r: (0, held(t, r), 0, 0)),
                pl.BlockSpec((1, 1, 2 * TILE), lambda t, r: (t, 0, 0)),
            ],
            out_specs=pl.BlockSpec((heads, bucket_count), lambda t, r: (0, 0)),
        ),
        cost_estimate=SMALL,
        compiler_params=pltpu.CompilerParams(vmem_limit_bytes=40 << 20),
    )(used, tiles, bucket_at)


def window_kernel(range_ref, key_ref, value_ref, key_weight_ref, value_weight_ref, out_ref):
    index = pl.program_id(0)
    tiles = out_ref.shape[0] // TILE
    needed = ((index + 1) * tiles > range_ref[0]) & (index * tiles < range_ref[1])

    @pl.when(needed)
    def _():
        out_ref[...] = (
            contract(key_ref[...], key_weight_ref[...], 1, 1) + contract(value_ref[...], value_weight_ref[...], 1, 1)
        ).astype(BF16)

    @pl.when(jnp.logical_not(needed))
    def _():
        out_ref[...] = jnp.zeros_like(out_ref)


def window_gradient(grad_keys, grad_values, weights, spots, covered, row_count):
    window, width = grad_keys.shape
    tiles = row_count // TILE

    def rows(index, covered_ref):
        low = lax.div(covered_ref[0], tiles)
        high = lax.div(covered_ref[1] - 1, tiles)
        return jnp.minimum(jnp.maximum(index, low), high), 0

    return pl.pallas_call(
        window_kernel,
        out_shape=jax.ShapeDtypeStruct((window, width), BF16),
        grid_spec=pltpu.PrefetchScalarGridSpec(
            num_scalar_prefetch=1,
            grid=(window // row_count,),
            in_specs=[
                pl.BlockSpec((row_count, width), rows),
                pl.BlockSpec((row_count, width), rows),
                pl.BlockSpec((width, width), lambda k, r: (0, spots[0])),
                pl.BlockSpec((width, width), lambda k, r: (0, spots[1])),
            ],
            out_specs=pl.BlockSpec((row_count, width), lambda k, r: (k, 0)),
        ),
        cost_estimate=SMALL,
        compiler_params=pltpu.CompilerParams(vmem_limit_bytes=40 << 20),
    )(covered, grad_keys, grad_values, weights, weights)


def shifted(value, axis, steps):
    count = lax.axis_size(axis)
    pairs = [(source, source + steps) for source in range(count) if 0 <= source + steps < count]
    return lax.ppermute(value, axis, pairs)


def flat_swap(value, mask):
    count = lax.axis_size("seq") * lax.axis_size("dp")
    return lax.ppermute(value, BOTH, [(source, source ^ mask) for source in range(count)])


def groups_of(low, bits):
    groups = []
    if bits % 2:
        groups.append((low, 1))
        low, bits = low + 1, bits - 1
    while bits:
        groups.append((low, 2))
        low, bits = low + 2, bits - 2
    return groups


def bits_of(count):
    bits = count.bit_length() - 1
    assert count == 1 << bits
    return bits


def all_groups(count):
    return [(0, 1)] + groups_of(1, bits_of(count) - 1)


def tie(*values):
    return lax.optimization_barrier(values)


def swaps(piece, group):
    low, bits = group
    return [flat_swap(piece, step << low) for step in range(1, 1 << bits)]


def swap_masks(masks, group):
    low, bits = group
    return [mask ^ (step << low) for step in range(1, 1 << bits) for mask in masks]


def stack_kernel(*refs):
    target = refs[-1]
    start = 0
    for source in refs[:-1]:
        target[start : start + source.shape[0]] = source[...]
        start += source.shape[0]


def stacked(pieces):
    if len(pieces) == 1:
        return pieces[0]
    count = sum(piece.shape[0] for piece in pieces)
    return pl.pallas_call(
        stack_kernel,
        out_shape=jax.ShapeDtypeStruct((count,) + pieces[0].shape[1:], pieces[0].dtype),
        in_specs=[pl.BlockSpec(memory_space=pltpu.VMEM)] * len(pieces),
        out_specs=pl.BlockSpec(memory_space=pltpu.VMEM),
        cost_estimate=SMALL,
        compiler_params=pltpu.CompilerParams(vmem_limit_bytes=40 << 20),
    )(*pieces)


def units_kernel(rank_ref, gate_ref, up_ref, units_ref, *, dp_count):
    left = lax.broadcasted_iota(jnp.int32, (gate_ref.shape[0], TILE), 1) < TILE // 2
    for side, source in enumerate((gate_ref, up_ref)):
        span = source.shape[1] // dp_count
        for owner in range(dp_count):
            for pair in range(span // TILE):
                halves_of = []
                for odd in range(2):
                    unit = (2 * pair + odd) * dp_count + owner
                    tile = source[:, unit // 2 * TILE : (unit // 2 + 1) * TILE]
                    halves_of.append(tile if unit % 2 == odd else pltpu.roll(tile, TILE // 2, 1))
                start = side * span + pair * TILE
                merged = jnp.where(left, halves_of[0], halves_of[1])
                units_ref[rank_ref[0] ^ owner, :, start : start + TILE] = merged.astype(BF16)


def units_of(gate_weight, up_weight, dp_rank, dp_count, seq_count, unit):
    rows, hidden_width = gate_weight.shape
    share = seq_count * unit
    if unit != TILE // 2 or rows % 8:
        both = jnp.stack([gate_weight.astype(BF16), up_weight.astype(BF16)], axis=1)
        both = both.reshape(rows, 2, seq_count, dp_count, unit)
        taken = [
            lax.dynamic_index_in_dim(both, dp_rank ^ mask, 3, keepdims=False).reshape(rows, 2 * share)
            for mask in range(dp_count)
        ]
        return jnp.stack(taken)
    return pl.pallas_call(
        functools.partial(units_kernel, dp_count=dp_count),
        out_shape=jax.ShapeDtypeStruct((dp_count, rows, 2 * share), BF16),
        in_specs=[pl.BlockSpec(memory_space=pltpu.SMEM)] + [pl.BlockSpec(memory_space=pltpu.VMEM)] * 2,
        out_specs=pl.BlockSpec(memory_space=pltpu.VMEM),
    )(dp_rank[None].astype(jnp.int32), gate_weight, up_weight)


def columns_kernel(rank_ref, *refs, dp_count):
    sources, (gate_ref, up_ref), scratch = refs[:dp_count], refs[dp_count : dp_count + 2], refs[-1]
    for mask in range(dp_count):
        scratch[rank_ref[0] ^ mask] = sources[mask][...].astype(F32)
    left = lax.broadcasted_iota(jnp.int32, (gate_ref.shape[0], TILE), 1) < TILE // 2
    for side, target in enumerate((gate_ref, up_ref)):
        span = target.shape[1] // dp_count
        for tile in range(target.shape[1] // TILE):
            halves_of = []
            for odd in range(2):
                group, owner = divmod(2 * tile + odd, dp_count)
                start = side * span + group // 2 * TILE
                part = scratch[owner, :, start : start + TILE]
                halves_of.append(part if group % 2 == odd else pltpu.roll(part, TILE // 2, 1))
            target[:, tile * TILE : (tile + 1) * TILE] = jnp.where(left, halves_of[0], halves_of[1])


def columns_of(parts, dp_rank, dp_count, seq_count, unit):
    rows = parts[0].shape[0]
    hidden_width = seq_count * dp_count * unit
    if unit != TILE // 2 or rows % 8:
        both = jnp.stack(parts)
        both = jnp.stack(
            [lax.dynamic_index_in_dim(both, dp_rank ^ index, 0, keepdims=False) for index in range(dp_count)], axis=1
        )
        both = both.reshape(rows, dp_count, 2, seq_count, unit).transpose(0, 2, 3, 1, 4)
        both = both.reshape(rows, 2, hidden_width).astype(F32)
        return both[:, 0], both[:, 1]
    return pl.pallas_call(
        functools.partial(columns_kernel, dp_count=dp_count),
        out_shape=(jax.ShapeDtypeStruct((rows, hidden_width), F32),) * 2,
        in_specs=[pl.BlockSpec(memory_space=pltpu.SMEM)] + [pl.BlockSpec(memory_space=pltpu.VMEM)] * dp_count,
        out_specs=(pl.BlockSpec(memory_space=pltpu.VMEM),) * 2,
        scratch_shapes=[pltpu.VMEM((dp_count,) + parts[0].shape, F32)],
        cost_estimate=SMALL,
    )(dp_rank[None].astype(jnp.int32), *parts)


def shard_kernel(*refs):
    target = refs[-1]
    start = 0
    for source in refs[:-1]:
        columns = source.shape[1]
        target[:, start : start + columns] = source[...].astype(BF16)
        start += columns


def side_by_side(arrays):
    columns = sum(array.shape[1] for array in arrays)
    return pl.pallas_call(
        shard_kernel,
        out_shape=jax.ShapeDtypeStruct((arrays[0].shape[0], columns), BF16),
        in_specs=[pl.BlockSpec(memory_space=pltpu.VMEM)] * len(arrays),
        out_specs=pl.BlockSpec(memory_space=pltpu.VMEM),
        cost_estimate=SMALL,
        compiler_params=pltpu.CompilerParams(vmem_limit_bytes=40 << 20),
    )(*arrays)


def norm_kernel(gain_ref, *refs):
    target = refs[-1]
    gain = gain_ref[...].astype(F32).T[:1]
    start = 0
    for source in refs[:-1]:
        rows = source[...].astype(F32)
        scale = lax.rsqrt(jnp.mean(rows * rows, axis=1, keepdims=True) + EPSILON)
        target[start : start + source.shape[0]] = (rows * scale * gain).astype(BF16)
        start += source.shape[0]


def normed_rows_of(pieces, weights, block):
    rows, width = pieces[0].shape
    return pl.pallas_call(
        norm_kernel,
        out_shape=jax.ShapeDtypeStruct((len(pieces) * rows, width), BF16),
        grid=(1,),
        in_specs=[pl.BlockSpec((width, TILE), lambda k: (0, block))]
        + [pl.BlockSpec((rows, width), lambda k: (0, 0))] * len(pieces),
        out_specs=pl.BlockSpec((len(pieces) * rows, width), lambda k: (0, 0)),
        compiler_params=pltpu.CompilerParams(vmem_limit_bytes=40 << 20),
    )(weights, *pieces)


def halves_kernel(rank_ref, *refs):
    sources, table_ref, (kept_ref, sent_ref) = refs[:-3], refs[-3], refs[-2:]
    mine = rank_ref[0] & 1
    for index in range(kept_ref.shape[0]):
        for target, side in ((kept_ref, mine), (sent_ref, 1 - mine)):
            start = 0
            for source in sources:
                target[index, :, start : start + source.shape[2]] = source[2 * index + side]
                start += source.shape[2]
            target[index, :, start:] = table_ref[...]


def core_halves(grads, table_block, rank, count):
    rows = grads[0].shape[0] // count
    columns = sum(grad.shape[1] for grad in grads) + TILE
    if rows % 8:
        held = jnp.concatenate(grads + [jnp.tile(table_block, (count, 1))], axis=1).reshape(-1, 2, rows, columns)
        return [lax.dynamic_index_in_dim(held, (rank & 1) ^ side, 1, keepdims=False) for side in range(2)]
    return pl.pallas_call(
        halves_kernel,
        out_shape=(jax.ShapeDtypeStruct((count // 2, rows, columns), BF16),) * 2,
        in_specs=[pl.BlockSpec(memory_space=pltpu.SMEM)]
        + [pl.BlockSpec(memory_space=pltpu.VMEM)] * (len(grads) + 1),
        out_specs=(pl.BlockSpec(memory_space=pltpu.VMEM),) * 2,
        cost_estimate=SMALL,
        compiler_params=pltpu.CompilerParams(vmem_limit_bytes=40 << 20),
    )(rank[None].astype(jnp.int32), *[grad.reshape(count, rows, -1) for grad in grads], table_block)


def place_kernel(rank_ref, *refs, masks):
    target = refs[-1]
    rank = rank_ref[0]
    for source, part in zip(refs, masks):
        for index, mask in enumerate(part):
            target[rank ^ mask] = source[index]


def placed(held, masks, rank):
    count = sum(len(part) for part in masks)
    shape = held[0].shape[1:]
    return pl.pallas_call(
        functools.partial(place_kernel, masks=masks),
        out_shape=jax.ShapeDtypeStruct((count,) + shape, held[0].dtype),
        in_specs=[pl.BlockSpec(memory_space=pltpu.SMEM)] + [pl.BlockSpec(memory_space=pltpu.VMEM)] * len(held),
        out_specs=pl.BlockSpec(memory_space=pltpu.VMEM),
        cost_estimate=SMALL,
        compiler_params=pltpu.CompilerParams(vmem_limit_bytes=40 << 20),
    )(rank[None].astype(jnp.int32), *held)


def place_far_kernel(rank_ref, *refs, masks, dp_count):
    pair_ref, down_ref = refs[-2:]
    rank = rank_ref[0]
    for source, part in zip(refs, masks):
        for index, mask in enumerate(part):
            owner = rank ^ mask
            for entry in range(dp_count):
                pair_ref[owner ^ entry] = source[index, entry]
            for entry in range(dp_count // 2):
                down_ref[owner // dp_count, entry] = source[index, dp_count + entry]


def place_far(held, masks, rank, dp_count):
    count = sum(len(part) for part in masks)
    shape = held[0].shape[2:]
    dtype = held[0].dtype
    return pl.pallas_call(
        functools.partial(place_far_kernel, masks=masks, dp_count=dp_count),
        out_shape=(
            jax.ShapeDtypeStruct((count * dp_count,) + shape, dtype),
            jax.ShapeDtypeStruct((count, dp_count // 2) + shape, dtype),
        ),
        in_specs=[pl.BlockSpec(memory_space=pltpu.SMEM)] + [pl.BlockSpec(memory_space=pltpu.VMEM)] * len(held),
        out_specs=(pl.BlockSpec(memory_space=pltpu.VMEM), pl.BlockSpec(memory_space=pltpu.VMEM)),
        cost_estimate=SMALL,
        compiler_params=pltpu.CompilerParams(vmem_limit_bytes=40 << 20),
    )(rank[None].astype(jnp.int32), *held)


def split_and_swap(held, mine, group):
    low, bits = group
    held = held.reshape((-1, 1 << bits) + held.shape[1:])
    kept = lax.dynamic_index_in_dim(held, mine, 1, keepdims=False)
    got = [
        flat_swap(lax.dynamic_index_in_dim(held, mine ^ step, 1, keepdims=False), step << low)
        for step in range(1, 1 << bits)
    ]
    return kept, got


def joined(kept, got):
    values = [piece.astype(F32) for piece in [kept] + got]
    while len(values) > 1:
        values = [values[k] + values[k + 1] for k in range(0, len(values), 2)]
    return values[0]


def spread_dp(parts, bits):
    held = {(mask, 0): part for mask, part in parts.items()}
    for bit in range(bits):
        step = 1 << bit
        keys = sorted(key for key in held if key[0] & step)
        sent = flat_swap(jnp.stack([held[key] for key in keys]), step)
        held = {key: part for key, part in held.items() if not key[0] & step}
        held.update({(goal ^ step, source ^ step): sent[k] for k, (goal, source) in enumerate(keys)})
    return [held[(0, mask)] for mask in range(1 << bits)]


def gather_dp(value, bits):
    held = {0: value}
    for bit in range(bits - 1, -1, -1):
        held.update({mask ^ (1 << bit): flat_swap(piece, 1 << bit) for mask, piece in list(held.items())})
    return [held[mask] for mask in range(1 << bits)]


def scatter_dp(parts, bits):
    held = dict(enumerate(parts))
    for bit in range(bits):
        step = 1 << bit
        held = {
            mask: piece.astype(F32) + flat_swap(held[mask ^ step].astype(BF16), step).astype(F32)
            for mask, piece in held.items()
            if not mask & step
        }
    return held[0]


def parts_of(value, parts, to_rows):
    rows = value.shape[0] // parts
    columns = rows * value.shape[1] // to_rows
    if rows % 8 or to_rows % 8 or value.shape[1] % TILE or columns % TILE:
        return value.reshape(parts * to_rows, columns)
    tiles = value.reshape(parts, rows // 8, 8, value.shape[1] // TILE, TILE).transpose(0, 1, 3, 2, 4)
    tiles = tiles.reshape(parts, to_rows // 8, columns // TILE, 8, TILE).transpose(0, 1, 3, 2, 4)
    return tiles.reshape(parts * to_rows, columns)


def contract(left_side, right_side, left_dim, right_dim):
    return lax.dot_general(
        left_side, right_side, (((left_dim,), (right_dim,)), ((), ())), preferred_element_type=F32
    )


def gelu_pair(v):
    scale = 0.7978845608028654
    bent = jnp.tanh(scale * (v + 0.044715 * v * v * v))
    value = 0.5 * v * (1.0 + bent)
    slope = 0.5 * (1.0 + bent) + 0.5 * v * (1.0 - bent * bent) * scale * (1.0 + 3.0 * 0.044715 * v * v)
    return value, slope


def body(
    blocks,
    lengths,
    bucket_table,
    first_gain,
    query_weight,
    key_weight,
    value_weight,
    output_weight,
    table_weight,
    second_gain,
    gate_weight,
    up_weight,
    down_weight,
    cotangent,
):
    seq_count = lax.axis_size("seq")
    device_count = seq_count * lax.axis_size("dp")
    seq_rank = lax.axis_index("seq")
    row_count, width = blocks.shape[1:]
    pack_rows = row_count * seq_count
    bucket_count, heads = table_weight.shape
    head_dim = width // heads
    seq_total = lengths.shape[1]
    max_length = (bucket_table.shape[0] + 1) // 2
    shard_rows = query_weight.shape[0]
    hidden_width = gate_weight.shape[1]
    reach = min((max_length - 1 + row_count - 1) // row_count, seq_count - 1)
    query_blocks = row_count // TILE
    window = (2 * reach + 1) * row_count
    window_blocks = window // TILE
    tile_count = window_blocks + query_blocks - 1
    center = reach * query_blocks + query_blocks - 1
    pairs = 2 if window <= 2304 else 1

    dp_count = lax.axis_size("dp")
    dp_rank = lax.axis_index("dp")
    dp_bits = bits_of(dp_count)
    rank = seq_rank * dp_count + dp_rank
    groups = all_groups(device_count)
    seq_groups = groups_of(dp_bits, bits_of(seq_count))
    own = blocks[0]

    gains = jnp.pad(jnp.stack([first_gain, second_gain], axis=1), ((0, 0), (0, TILE - 2)))
    near_shard = side_by_side([query_weight, key_weight, value_weight, output_weight, gains])

    unit = down_weight.shape[0]
    share = seq_count * unit
    pair_units = units_of(gate_weight, up_weight, dp_rank, dp_count, seq_count, unit)

    line_width = (tile_count + 1) * TILE
    ahead = (tile_count - center) * TILE - (max_length - 1)
    behind = line_width - ahead - bucket_table.shape[0]
    bucket_line = jnp.pad(bucket_table[::-1], (max(ahead, 0), max(behind, 0)), mode="edge")
    bucket_line = bucket_line[max(-ahead, 0) : max(-ahead, 0) + line_width]
    bucket_ids = jnp.arange(bucket_count, dtype=jnp.int32)
    line_hot = (bucket_line[None, :] == bucket_ids[:, None]).astype(F32)
    lines = lax.dot_general(table_weight, line_hot, (((0,), (0,)), ((), ())), precision=HIGHEST)

    order = groups[::-1]
    near_shard = near_shard[None]
    masks = [0]
    around = {0: own}
    near_held = near_shard
    stages = len(order)
    for stage, group in enumerate(order):
        got = swaps(near_held, group)
        last = stage == stages - 1
        moves = [step for step in range(1, reach + 1) if step == stage + 1 or (last and step > stage)]
        arrived = {}
        for step in moves:
            arrived[step] = shifted(own, "seq", step)
            arrived[-step] = shifted(own, "seq", -step)
        got_masks = swap_masks(masks, group)
        if last:
            held, masks = [near_held] + got, [masks] + [
                got_masks[k * len(masks) : (k + 1) * len(masks)] for k in range(len(got))
            ]
        else:
            if stage == 0:
                lines = tie(lines, got[0])[0]
            if stage == 1:
                tiles = bias_tiles(lines, tile_count)
                near_held, got, arrived, tiles = tie(near_held, got, arrived, tiles)
            else:
                near_held, got, arrived = tie(near_held, got, arrived)
            near_held = stacked([near_held] + got)
            masks = masks + got_masks
        around.update(arrived)
    near_full = placed(held, masks, rank)
    near_full = near_full.reshape(device_count * shard_rows, 4 * width + TILE)
    weight_query = near_full[:, :width]
    weight_key = near_full[:, width : 2 * width]
    weight_value = near_full[:, 2 * width : 3 * width]
    weight_output = near_full[:, 3 * width : 4 * width]
    gain_columns = near_full[:, 4 * width :]

    pair_parts = spread_dp({mask: pair_units[mask] for mask in range(dp_count)}, dp_bits)
    down_parts = parts_of(down_weight.astype(BF16), 1, shard_rows * dp_count // 2)
    down_parts = down_parts.reshape(dp_count // 2, shard_rows, 2 * share)
    far_shard = stacked([part[None] for part in pair_parts] + [down_parts])
    far_shard = tie(far_shard, near_held)[0][None]
    far_order = seq_groups[::-1]
    far_first = swaps(far_shard, far_order[0])
    far_own = [piece for group in far_order[1:2] for piece in swaps(far_shard, group)]
    gain_one = gain_columns[:, 0].astype(F32)[None, :]
    gain_two = gain_columns[:, 1].astype(F32)[None, :]

    seq_ends = jnp.cumsum(lengths[0], dtype=jnp.int32)
    query_first = seq_rank * row_count
    window_first = query_first - reach * row_count

    def segments(at):
        return jnp.sum((at[:, None] >= seq_ends[None, :]).astype(jnp.int32), axis=1, dtype=jnp.int32)

    query_places = query_first + jnp.arange(row_count, dtype=jnp.int32)
    key_places = window_first + jnp.arange(window, dtype=jnp.int32)
    query_seg = segments(query_places)
    key_seg = jnp.where((key_places >= 0) & (key_places < pack_rows), segments(key_places), -1)
    lanes = jnp.arange(TILE, dtype=jnp.int32)
    key_feat = jnp.where(
        (key_seg[:, None] != lanes[None, :]) & (lanes[None, :] <= seq_total), BIG, 0.0
    ).astype(BF16)
    query_feat = (lanes[:, None] == query_seg[None, :]).astype(BF16)
    valid_rows = (query_seg < seq_total).astype(F32)
    seq_starts = jnp.concatenate([jnp.zeros((1,), jnp.int32), seq_ends])
    seq_stops = jnp.concatenate([seq_ends, jnp.full((1,), pack_rows, jnp.int32)])
    seq_ids = jnp.arange(seq_total + 1, dtype=jnp.int32)
    low_seg = query_seg[::TILE]
    high_seg = query_seg[TILE - 1 :: TILE]
    low = jnp.sum(jnp.where(low_seg[:, None] == seq_ids[None, :], seq_starts[None, :], 0), axis=1)
    high = jnp.sum(jnp.where(high_seg[:, None] == seq_ids[None, :], seq_stops[None, :], 0), axis=1)
    first = (low - window_first) // TILE
    last = (high - window_first + TILE - 1) // TILE
    steps = (last - first + STEP - 1) // STEP
    first = jnp.minimum(first, window_blocks - steps * STEP).astype(jnp.int32)
    steps = steps.astype(jnp.int32)


    window_normed = normed_rows_of(
        [around[-step] for step in range(-reach, reach + 1)], near_full, 4 * width // TILE
    )
    own_slice = slice(reach * row_count, (reach + 1) * row_count)
    tokens = own.astype(F32)
    scale_one = lax.rsqrt(jnp.mean(tokens * tokens, axis=1, keepdims=True) + EPSILON)
    normed_own = window_normed[own_slice]
    keys = contract(window_normed, weight_key, 1, 0).astype(BF16)
    values_turned = contract(weight_value, window_normed, 0, 1).astype(BF16)
    queries_turned = contract(weight_query, normed_own, 0, 1).astype(BF16)
    far_first = stacked(tie(far_first, keys)[0])
    outs, logs = attend(
        first, steps, queries_turned, keys, values_turned, key_feat, query_feat, tiles, head_dim, pairs
    )
    grad_held = {0: cotangent[0]}
    for bit in range(dp_bits - 1, 0, -1):
        grad_held.update({mask ^ (1 << bit): flat_swap(piece, 1 << bit) for mask, piece in list(grad_held.items())})
    outs, grad_held = tie(outs, grad_held)
    first_masks = swap_masks([0], far_order[0])
    far_held, far_masks = [far_shard, far_first], [[0], first_masks]
    for number, group in enumerate(far_order[1:]):
        got, got_masks = [], []
        for piece, part in zip(far_held, far_masks):
            more = far_own if piece is far_shard and number == 0 else swaps(piece, group)
            extra = swap_masks(part, group)
            got += more
            got_masks += [extra[k * len(part) : (k + 1) * len(part)] for k in range(len(more))]
        far_held, far_masks = far_held + got, far_masks + got_masks
    far_full = place_far(far_held, far_masks, rank, dp_count)
    weight_pair = far_full[0].reshape(device_count * shard_rows, 2 * share)
    weight_down = parts_of(far_full[1].reshape(-1, 2 * share), seq_count, unit)
    attended = (outs * valid_rows[None, :]).astype(BF16)
    middle = tokens + contract(attended, weight_output, 0, 0)

    scale_two = lax.rsqrt(jnp.mean(middle * middle, axis=1, keepdims=True) + EPSILON)
    second = middle * scale_two
    second_low = (second * gain_two).astype(BF16)
    every_second = jnp.concatenate(gather_dp(second_low, dp_bits), axis=0)
    grad_held.update({mask ^ 1: flat_swap(piece, 1) for mask, piece in list(grad_held.items())})
    every_grad = jnp.concatenate([grad_held[mask] for mask in range(dp_count)], axis=0)
    both_ways = contract(every_second, weight_pair, 1, 0)
    gate_values, upward = both_ways[:, :share], both_ways[:, share:]
    active, slope = gelu_pair(gate_values)
    hidden = (active * upward).astype(BF16)
    grad_hidden = contract(every_grad, weight_down, 1, 1)
    grad_pair = jnp.concatenate(
        [(grad_hidden * upward * slope).astype(BF16), (grad_hidden * active).astype(BF16)], axis=1
    )
    every_back = contract(grad_pair, weight_pair, 1, 1).astype(BF16)
    grad_second = scatter_dp(jnp.split(every_back, dp_count, axis=0), dp_bits)
    grad_out = cotangent[0]
    scaled = grad_second * gain_two
    grad_middle = grad_out.astype(F32) + scale_two * (
        scaled - second * jnp.mean(scaled * second, axis=1, keepdims=True)
    )
    grad_branch = grad_middle.astype(BF16)
    grad_mixed = (contract(grad_branch, weight_output, 1, 1).astype(BF16).astype(F32) * valid_rows[:, None]).astype(BF16)
    grad_mixed_turned = (
        contract(weight_output, grad_branch, 1, 1).astype(BF16).astype(F32) * valid_rows[None, :]
    ).astype(BF16)
    grad_output_weight = contract(attended, grad_branch, 1, 0).astype(BF16)
    grad_down = contract(hidden, every_grad, 0, 0).astype(BF16)
    grad_down = parts_of(grad_down, seq_count, shard_rows * dp_count // 2)
    grad_pair_weight = contract(every_second, grad_pair, 0, 0).astype(BF16)
    far_grads = jnp.concatenate(
        [
            grad_pair_weight.reshape(seq_count, dp_count, shard_rows, 2 * share),
            grad_down.reshape(seq_count, dp_count // 2, shard_rows, 2 * share),
        ],
        axis=1,
    )
    every_out = contract(hidden, weight_down, 1, 0).astype(BF16)
    far_grads, grad_mixed, grad_mixed_turned, grad_output_weight, every_out = tie(
        far_grads, grad_mixed, grad_mixed_turned, grad_output_weight, every_out
    )
    out_parts = jnp.split(every_out, dp_count, axis=0)
    bits = seq_groups[0][1]
    far_kept, far_got = split_and_swap(far_grads, seq_rank & ((1 << bits) - 1), seq_groups[0])

    queries = contract(normed_own, weight_query, 1, 0).astype(BF16)
    keys_turned = contract(weight_key, window_normed, 0, 1).astype(BF16)
    values = contract(window_normed, weight_value, 1, 0).astype(BF16)
    grad_queries, grad_keys, grad_values, tile_sums = attend_back(
        first, steps, queries, queries_turned, keys, keys_turned, values, grad_mixed, grad_mixed_turned,
        outs, logs, key_feat, query_feat, tiles, head_dim, pairs,
    )
    out_parts = [out_parts[0]] + [flat_swap(out_parts[mask], mask) for mask in range(1, dp_count)]
    grad_queries, out_parts = tie(grad_queries, out_parts)
    output = middle + sum(part.astype(F32) for part in out_parts)
    grad_queries, grad_keys, grad_values, tile_sums, far_kept, far_got = tie(
        grad_queries, grad_keys, grad_values, tile_sums, far_kept, far_got
    )
    for low, bits in seq_groups[1:]:
        far_held = joined(far_kept, far_got).astype(BF16)
        far_kept, far_got = split_and_swap(far_held, (rank >> low) & ((1 << bits) - 1), (low, bits))
    covered = jnp.stack([jnp.min(first), jnp.max(first + steps * STEP)])
    partial_low = window_gradient(grad_keys, grad_values, near_full, (1, 2), covered, row_count)

    def returned_from(low_rows, step):
        parts = []
        for turn in (step, -step):
            part = low_rows[(reach + turn) * row_count : (reach + turn + 1) * row_count]
            parts.append(shifted(part, "seq", turn))
        return parts

    returned = returned_from(partial_low, 1)
    if reach > 2:
        returned = returned + returned_from(partial_low, reach - 1)
    grad_query_weight = contract(normed_own, grad_queries, 0, 1).astype(BF16)
    grad_key_weight = contract(window_normed, grad_keys, 0, 0).astype(BF16)
    grad_value_weight = contract(window_normed, grad_values, 0, 0).astype(BF16)

    tile_first = first - jnp.arange(query_blocks, dtype=jnp.int32) + (query_blocks - 1)
    used = jnp.stack([jnp.min(tile_first), jnp.max(tile_first + steps * STEP)])
    flipped = bucket_line.reshape(tile_count + 1, TILE)[::-1]
    bucket_at = jnp.concatenate([flipped[:-1], flipped[1:]], axis=1)[:, None, :]
    grad_table = table_sums(tile_sums, used, bucket_at, bucket_count).T
    table_rows = -(-grad_table.size // TILE)
    table_block = jnp.pad(grad_table.reshape(-1), (0, table_rows * TILE - grad_table.size)).reshape(table_rows, TILE)
    table_block = jnp.pad(table_block, ((0, shard_rows - table_rows), (0, 0))).astype(BF16)
    kept, sent = core_halves(
        [grad_query_weight, grad_key_weight, grad_value_weight, grad_output_weight], table_block, rank, device_count
    )
    kept, sent, partial_low, returned, far_kept, far_got = tie(kept, sent, partial_low, returned, far_kept, far_got)
    far_sum = joined(far_kept, far_got).reshape(far_grads.shape[1:]).astype(BF16)

    left = [step for step in range(reach, 2, -1) if step != reach - 1]
    waiting = returned_from(partial_low, 2) if reach == 2 or reach > 3 else []
    for stage, (low, bits) in enumerate(groups):
        if stage == 0:
            got = [flat_swap(sent, 1)]
        else:
            kept, got = split_and_swap(near_held, (rank >> low) & ((1 << bits) - 1), (low, bits))
        if stage == 0:
            kept, got, partial_low = tie(kept, got, partial_low)
        else:
            arrived = returned_from(partial_low, left.pop(0)) if left else []
            kept, got, arrived, waiting, partial_low, far_sum = tie(
                kept, got, arrived, waiting, partial_low, far_sum
            )
            if stage == 1:
                pair_back = spread_dp(
                    {mask: lax.dynamic_index_in_dim(far_sum, dp_rank ^ mask, 0, keepdims=False) for mask in range(dp_count)},
                    dp_bits,
                )
            if stage == 2:
                kept, pair_back = tie(kept, pair_back)
            returned, waiting = returned + arrived + waiting, []
        total = joined(kept, got)
        near_held = total.astype(BF16)
    for step in left:
        returned = returned + returned_from(partial_low, step)
    near_sum = total.reshape(shard_rows, 4 * width + TILE)
    grad_normed = partial_low[own_slice].astype(F32) + contract(grad_queries, weight_query, 0, 1)
    grad_normed = grad_normed + sum(piece.astype(F32) for piece in returned)
    grad_gate_own, grad_up_own = columns_of(pair_back, dp_rank, dp_count, seq_count, unit)
    grad_down_own = parts_of(far_sum[dp_count:].astype(F32).reshape(-1, 2 * share), 1, unit)
    normed_rows = tokens * scale_one
    scaled_one = grad_normed * gain_one
    grad_blocks = grad_middle + scale_one * (
        scaled_one - normed_rows * jnp.mean(scaled_one * normed_rows, axis=1, keepdims=True)
    )

    grad_table = near_sum[:table_rows, 4 * width :].reshape(-1)[: table_weight.size].reshape(table_weight.shape)

    def gain_grad(gain, weights, grads):
        total = sum(jnp.sum(weight.astype(BF16).astype(F32) * grad, axis=1) for weight, grad in zip(weights, grads))
        return total / gain.astype(BF16).astype(F32)

    near_parts = [near_sum[:, k * width : (k + 1) * width] for k in range(4)]
    grad_gain_one = gain_grad(first_gain, (query_weight, key_weight, value_weight), near_parts[:3])
    grad_gain_two = gain_grad(second_gain, (gate_weight, up_weight), (grad_gate_own, grad_up_own))
    return (
        output.astype(BF16)[None],
        grad_blocks[None],
        grad_gain_one,
        near_parts[0],
        near_parts[1],
        near_parts[2],
        near_parts[3],
        grad_table,
        grad_gain_two,
        grad_gate_own,
        grad_up_own,
        grad_down_own,
    )


def solution(mesh):
    return jax.shard_map(
        body,
        mesh=mesh,
        in_specs=(
            P("dp", "seq", None),
            P("dp", None),
            P(),
            P(("seq", "dp")),
            P(("seq", "dp"), None),
            P(("seq", "dp"), None),
            P(("seq", "dp"), None),
            P(("seq", "dp"), None),
            P(),
            P(("seq", "dp")),
            P(("seq", "dp"), None),
            P(("seq", "dp"), None),
            P(("seq", "dp"), None),
            P("dp", "seq", None),
        ),
        out_specs=(
            P("dp", "seq", None),
            P("dp", "seq", None),
            P(("seq", "dp")),
            P(("seq", "dp"), None),
            P(("seq", "dp"), None),
            P(("seq", "dp"), None),
            P(("seq", "dp"), None),
            P(),
            P(("seq", "dp")),
            P(("seq", "dp"), None),
            P(("seq", "dp"), None),
            P(("seq", "dp"), None),
        ),
        check_vma=False,
    )
```
